32 devices in a mesh: dp: 8 (over y, x, core), frame: 4 (over z).
Axes of the slice: x: 2, y: 2, z: 4, core: 2. Of those that a mesh axis runs over, the one named last changes fastest.
Arguments:
- frames_in: bfloat16 [128, 256, 768], P(('dp', 'frame')), may hold values from -6 to 6
- condition: bfloat16 [128, 768], P(('dp', 'frame')), may hold values from -6 to 6
- segments: int32 [8, 16], P('dp'), may hold values from 0 to 1, as said below
- spatial_in: bfloat16 [768, 2304], P('frame'), may hold values from -0.21875 to 0.21875
- spatial_in_bias: bfloat16 [2304], P('frame'), may hold values from -3 to 3
- spatial_out: bfloat16 [768, 768], P('frame'), may hold values from -0.875 to 0.875
- spatial_out_bias: bfloat16 [768], P('frame'), may hold values from -3 to 3
- temporal_in: bfloat16 [768, 2304], P('frame'), may hold values from -0.21875 to 0.21875
- temporal_in_bias: bfloat16 [2304], P('frame'), may hold values from -3 to 3
- temporal_out: bfloat16 [768, 768], P('frame'), may hold values from -0.3125 to 0.3125
- temporal_out_bias: bfloat16 [768], P('frame'), may hold values from -3 to 3
- expand_weight: bfloat16 [768, 3072], P('frame'), may hold values from -0.21875 to 0.21875
- expand_bias: bfloat16 [3072], P('frame'), may hold values from -3 to 3
- shrink_weight: bfloat16 [3072, 768], P('frame'), may hold values from -0.109375 to 0.109375
- shrink_bias: bfloat16 [768], P('frame'), may hold values from -3 to 3
- modulate_weight: bfloat16 [768, 6912], P('frame'), may hold values from -0.21875 to 0.21875
- modulate_bias: bfloat16 [6912], P('frame'), may hold values from -3 to 3
- cotangent: bfloat16 [128, 256, 768], P(('dp', 'frame')), may hold values from -6 to 6
Outputs:
- frames_out: bfloat16 [128, 256, 768], P(('dp', 'frame'))
- grad_frames: float32 [128, 256, 768], P(('dp', 'frame'))
- grad_condition: float32 [128, 768], P(('dp', 'frame'))
- grad_spatial_in: float32 [768, 2304], P('frame')
- grad_spatial_in_bias: float32 [2304], P('frame')
- grad_spatial_out: float32 [768, 768], P('frame')
- grad_spatial_out_bias: float32 [768], P('frame')
- grad_temporal_in: float32 [768, 2304], P('frame')
- grad_temporal_in_bias: float32 [2304], P('frame')
- grad_temporal_out: float32 [768, 768], P('frame')
- grad_temporal_out_bias: float32 [768], P('frame')
- grad_expand_weight: float32 [768, 3072], P('frame')
- grad_expand_bias: float32 [3072], P('frame')
- grad_shrink_weight: float32 [3072, 768], P('frame')
- grad_shrink_bias: float32 [768], P('frame')
- grad_modulate_weight: float32 [768, 6912], P('frame')
- grad_modulate_bias: float32 [6912], P('frame')
The draws below stay inside these ranges and needn't reach their ends.
Inputs may be any that keep to these rules, and one draw needn't show every extreme that they name: `segments`: each row holds two clips numbered 0 and 1 in order, never falling: one of exactly 12 frames and one of 4 frames, in either order.
All inputs are finite; a program needn't handle non-finite values.
Results may differ from the reference program's by a relative error of at most 0.03.
Values may be sent and summed in bfloat16 or wider, within the bound.
No kernel may reach another device: no remote copies, remote signals or barrier semaphores. Data moves between devices by JAX's collectives and lax.ppermute only.
A program may use at most 320 MiB of HBM per device.

```python
import jax
import jax.numpy as jnp
from jax import lax

D = 768
HEADS = 12
HEAD_DIM = 64
FF = 3072
PATCHES = 256
WINDOW = 2
FRAMES_GRP = 16
FRAMES = 128
MOST = 12
N_DP = 8


def draw_segments(key, part):
    flips = jax.random.randint(jax.random.fold_in(key, 17), (N_DP,), 0, 2)
    first_len = jnp.where(flips == 1, MOST, FRAMES_GRP - MOST).astype(jnp.int32)
    positions = jnp.arange(FRAMES_GRP, dtype=jnp.int32)
    return (positions[None, :] >= first_len[:, None]).astype(jnp.int32)


def shard_levels(rng, dims, cuts, smallest, largest):
    level, own = 1.0, jax.random.fold_in(rng, 6)
    for position, blocks in cuts:
        steps = jnp.exp(jax.random.uniform(jax.random.fold_in(own, position), (blocks,), jnp.float32, smallest / len(cuts), largest / len(cuts)))
        level = level * jnp.repeat(steps, dims[position] // blocks).reshape([-1 if axis == position else 1 for axis in range(len(dims))])
    return level


def noise(rng, extent, width, most, cuts=(), held_as=jnp.bfloat16):
    values = jax.random.normal(rng, extent, jnp.float32) * width
    if len(cuts) > 0:
        values = shard_levels(rng, extent, cuts, -0.22, 0.18) * values
    return jnp.clip(values, min=-most, max=most).astype(held_as)


def setup_inputs(seed: int = 0) -> dict:
    arg_keys = jax.random.split(jax.random.key(seed), 19)
    return {
        "frames_in": noise(arg_keys[0], (FRAMES, PATCHES, D), 1.0, 6.0, ((0, 32),)),
        "condition": noise(arg_keys[1], (FRAMES, D), 1.0, 6.0, ((0, 32),)),
        "segments": draw_segments(jax.random.fold_in(arg_keys[18], 71), 0),
        "spatial_in": noise(arg_keys[3], (D, 3 * D), D ** -0.5, 0.21875, ((0, 4),)),
        "spatial_in_bias": noise(arg_keys[4], (3 * D,), 0.5, 3.0, ((0, 4),)),
        "spatial_out": noise(arg_keys[5], (D, D), (D // 16) ** -0.5, 0.875, ((0, 4),)),
        "spatial_out_bias": noise(arg_keys[6], (D,), 0.5, 3.0, ((0, 4),)),
        "temporal_in": noise(arg_keys[7], (D, 3 * D), D ** -0.5, 0.21875, ((0, 4),)),
        "temporal_in_bias": noise(arg_keys[8], (3 * D,), 0.5, 3.0, ((0, 4),)),
        "temporal_out": noise(arg_keys[9], (D, D), (D // 2) ** -0.5, 0.3125, ((0, 4),)),
        "temporal_out_bias": noise(arg_keys[10], (D,), 0.5, 3.0, ((0, 4),)),
        "expand_weight": noise(arg_keys[11], (D, FF), D ** -0.5, 0.21875, ((0, 4),)),
        "expand_bias": noise(arg_keys[12], (FF,), 0.5, 3.0, ((0, 4),)),
        "shrink_weight": noise(arg_keys[13], (FF, D), FF ** -0.5, 0.109375, ((0, 4),)),
        "shrink_bias": noise(arg_keys[14], (D,), 0.5, 3.0, ((0, 4),)),
        "modulate_weight": noise(arg_keys[15], (D, 9 * D), D ** -0.5, 0.21875, ((0, 4),)),
        "modulate_bias": noise(arg_keys[16], (9 * D,), 0.5, 3.0, ((0, 4),)),
        "cotangent": noise(arg_keys[17], (FRAMES, PATCHES, D), 1.0, 6.0, ((0, 32),)),
    }


HIGH = lax.Precision.HIGHEST

@jax.custom_vjp
def low(v):
    return lax.optimization_barrier(v.astype(jnp.bfloat16)).astype(jnp.float32)

@jax.custom_vjp
def low_back(v):
    return v

def low_keep(v):
    return (low(v), None)

def low_pass(kept, grad):
    return (grad,)

def back_keep(v):
    return (v, None)

def back_low(kept, grad):
    return (low(grad),)
low.defvjp(low_keep, low_pass)
low_back.defvjp(back_keep, back_low)

def norm_mod(values, shifts, scaling):
    average = lax.optimization_barrier(jnp.mean(values, axis=-1, keepdims=True))
    centred = values - average
    spread = lax.optimization_barrier(jnp.mean(centred * centred, axis=-1, keepdims=True))
    return centred * lax.rsqrt(spread + 1e-06) * (1.0 + scaling[:, None, :]) + shifts[:, None, :]

def project(values, matrix, vector):
    return jnp.einsum('fpd,de->fpe', values, matrix, precision=HIGH) + vector

def forward(params, hidden, condition, seg_row):
    spatial_in, spatial_in_bias, spatial_out, spatial_out_bias, temporal_in, temporal_in_bias, temporal_out, temporal_out_bias, expand_weight, expand_bias, shrink_weight, shrink_bias, modulate_weight, modulate_bias = params
    frames = hidden.shape[0]
    patches = hidden.shape[1]
    heads_shape = (frames, patches, HEADS, HEAD_DIM)
    scaling = HEAD_DIM ** (-0.5)
    cond_act = low(jax.nn.silu(condition))
    modvec = low_back(jnp.dot(cond_act, modulate_weight, precision=HIGH) + modulate_bias)
    pieces = jnp.split(modvec, 9, axis=1)
    normed_one = low(norm_mod(hidden, pieces[0], pieces[1]))
    qkv_one = low(low_back(project(normed_one, spatial_in, spatial_in_bias)))
    queries = qkv_one[..., :D].reshape(heads_shape)
    keyset = qkv_one[..., D:2 * D].reshape(heads_shape)
    valset = qkv_one[..., 2 * D:].reshape(heads_shape)
    scores = low_back(jnp.einsum('fphd,fqhd->fhpq', queries, keyset, precision=HIGH) * scaling)
    probs_one = low(jax.nn.softmax(scores, axis=-1))
    attn_one = low(low_back(jnp.einsum('fhpq,fqhd->fphd', probs_one, valset, precision=HIGH)))
    attn_one = attn_one.reshape(frames, patches, D)
    branch_one = low_back(project(attn_one, spatial_out, spatial_out_bias))
    after_one = hidden + pieces[2][:, None, :] * branch_one
    normed_two = low(norm_mod(after_one, pieces[3], pieces[4]))
    qkv_two = low(low_back(project(normed_two, temporal_in, temporal_in_bias)))
    query_two = qkv_two[..., :D].reshape(heads_shape)
    kv_pad = jnp.pad(qkv_two[..., D:], ((WINDOW, WINDOW), (0, 0), (0, 0)))
    seg_pad = jnp.pad(seg_row, (WINDOW, WINDOW), constant_values=-1)
    span_count = 2 * WINDOW + 1
    allowed = jnp.stack([seg_pad[offset:offset + frames] == seg_row for offset in range(span_count)])
    key_stack = jnp.stack([kv_pad[offset:offset + frames, :, :D] for offset in range(span_count)])
    key_stack = key_stack.reshape((span_count,) + heads_shape)
    val_stack = jnp.stack([kv_pad[offset:offset + frames, :, D:] for offset in range(span_count)])
    val_stack = val_stack.reshape((span_count,) + heads_shape)
    raw_two = low_back(jnp.einsum('fphd,jfphd->jfhp', query_two, key_stack, precision=HIGH) * scaling)
    masked = jnp.where(allowed[:, :, None, None], raw_two, -1e+30)
    probs_two = low(jax.nn.softmax(masked, axis=0))
    attn_two = low(low_back(jnp.einsum('jfhp,jfphd->fphd', probs_two, val_stack, precision=HIGH)))
    attn_two = attn_two.reshape(frames, patches, D)
    branch_two = low_back(project(attn_two, temporal_out, temporal_out_bias))
    after_two = after_one + pieces[5][:, None, :] * branch_two
    normed_three = low(norm_mod(after_two, pieces[6], pieces[7]))
    pre_act = low_back(project(normed_three, expand_weight, expand_bias))
    activ = low(jax.nn.gelu(pre_act, approximate=False))
    branch_three = low_back(project(activ, shrink_weight, shrink_bias))
    return after_two + pieces[8][:, None, :] * branch_three

def reference(frames_in, condition, segments, spatial_in, spatial_in_bias, spatial_out, spatial_out_bias, temporal_in, temporal_in_bias, temporal_out, temporal_out_bias, expand_weight, expand_bias, shrink_weight, shrink_bias, modulate_weight, modulate_bias, cotangent):
    weight_set = (spatial_in, spatial_in_bias, spatial_out, spatial_out_bias, temporal_in, temporal_in_bias, temporal_out, temporal_out_bias, expand_weight, expand_bias, shrink_weight, shrink_bias, modulate_weight, modulate_bias)
    params = tuple((weight_arr.astype(jnp.float32) for weight_arr in weight_set))
    hidden_all = frames_in.astype(jnp.float32).reshape(N_DP, FRAMES_GRP, PATCHES, D)
    cond_all = condition.astype(jnp.float32).reshape(N_DP, FRAMES_GRP, D)
    cot_all = cotangent.astype(jnp.float32).reshape(N_DP, FRAMES_GRP, PATCHES, D)

    def one_group(totals, member):
        hidden, cond_rows, seg_row, cot_rows = member

        def apply_block(param_set, hidden_in, cond_in):
            return forward(param_set, hidden_in, cond_in, seg_row)
        result, pullback = jax.vjp(apply_block, params, hidden, cond_rows)
        dparams, dhidden, dcond = pullback(cot_rows)
        totals = tuple((running + fresh for running, fresh in zip(totals, dparams)))
        return (totals, (result.astype(jnp.bfloat16), dhidden, dcond))
    zero_set = tuple((jnp.zeros(weight_arr.shape, jnp.float32) for weight_arr in params))
    grad_set, outputs = lax.scan(one_group, zero_set, (hidden_all, cond_all, segments, cot_all))
    frames_out = outputs[0].reshape(FRAMES, PATCHES, D)
    grad_frames = outputs[1].reshape(FRAMES, PATCHES, D)
    grad_condition = outputs[2].reshape(FRAMES, D)
    return (frames_out, grad_frames, grad_condition, grad_set[0], grad_set[1], grad_set[2], grad_set[3], grad_set[4], grad_set[5], grad_set[6], grad_set[7], grad_set[8], grad_set[9], grad_set[10], grad_set[11], grad_set[12], grad_set[13])
```

```python
import jax
import jax.numpy as jnp
from jax import lax
from jax.sharding import PartitionSpec as P

HEADS = 12
HEAD_DIM = 64
WINDOW = 2


def extended(block, sides, width):
    for axis, dim in sides:
        count = lax.axis_size(axis)
        forward = [(i, i + 1) for i in range(count - 1)]
        backward = [(target, source) for source, target in forward]
        low = lax.ppermute(
            lax.slice_in_dim(block, block.shape[dim] - width, None, axis=dim), axis, forward
        )
        high = lax.ppermute(lax.slice_in_dim(block, 0, width, axis=dim), axis, backward)
        block = jnp.concatenate([low, block, high], axis=dim)
    return block


def passed_along(x, axis, by):
    peers = lax.axis_size(axis)
    pairs = [(i, i + by) for i in range(peers) if 0 <= i + by < peers]
    return lax.ppermute(x, axis, pairs)


def norm_mod(values, shifts, scaling):
    average = jnp.mean(values, axis=-1, keepdims=True)
    centred = values - average
    spread = jnp.mean(centred * centred, axis=-1, keepdims=True)
    return centred * lax.rsqrt(spread + 1e-06) * (1.0 + scaling[:, None, :]) + shifts[:, None, :]


def gelu_exact(values):
    return jax.nn.gelu(values, approximate=False)


def mat_dot(values, matrix):
    return lax.dot_general(
        values, matrix, (((values.ndim - 1,), (0,)), ((), ())), preferred_element_type=jnp.float32
    )


def back_dot(values, matrix):
    return lax.dot_general(
        values, matrix, (((values.ndim - 1,), (1,)), ((), ())), preferred_element_type=jnp.float32
    )


def outer_sum(left_rows, right_rows):
    left_flat = left_rows.reshape(-1, left_rows.shape[-1])
    right_flat = right_rows.reshape(-1, right_rows.shape[-1])
    return lax.dot_general(
        left_flat, right_flat, (((0,), (0,)), ((), ())), preferred_element_type=jnp.float32
    )


def column_sum(values):
    return jnp.sum(values.astype(jnp.float32).reshape(-1, values.shape[-1]), axis=0)


def own_part(vector):
    size = vector.shape[0] // lax.axis_size("frame")
    return lax.dynamic_slice_in_dim(vector, lax.axis_index("frame") * size, size)


def stacked(block, width):
    count = block.shape[-1] // width
    return jnp.concatenate(
        [block[..., k * width : (k + 1) * width] for k in range(count)], axis=-2
    )


def unstacked(block, count):
    rows = block.shape[-2] // count
    return jnp.concatenate(
        [block[..., k * rows : (k + 1) * rows, :] for k in range(count)], axis=-1
    )


def gathered(shards):
    groups, parts = lax.axis_size("dp"), lax.axis_size("frame")
    width = min(shard.shape[1] for shard in shards)
    pieces = []
    for shard in shards:
        rows = shard.shape[0] // groups
        piece = lax.dynamic_slice_in_dim(shard, lax.axis_index("dp") * rows, rows)
        pieces.append(stacked(piece, width))
    mine = jnp.concatenate(pieces, axis=0)
    column = lax.all_gather(mine, "frame", axis=0)
    whole = lax.all_gather(column, "dp", axis=0)
    results, at = [], 0
    for shard, piece in zip(shards, pieces):
        part = unstacked(whole[:, :, at : at + piece.shape[0]], shard.shape[1] // width)
        results.append(jnp.swapaxes(part, 0, 1).reshape(parts * shard.shape[0], shard.shape[1]))
        at += piece.shape[0]
    return results


def gathered_small(biases, condition):
    parts = lax.axis_size("frame")
    flat = jnp.concatenate(biases + [condition.reshape(-1)])
    rows = lax.all_gather(flat, "frame", axis=0)
    results, at = [], 0
    for bias in biases:
        results.append(rows[:, at : at + bias.shape[0]].reshape(-1))
        at += bias.shape[0]
    results.append(rows[:, at:].reshape(parts * condition.shape[0], condition.shape[1]))
    return results


def modulated(act_group, matrix, frames):
    parts = lax.axis_size("frame")
    rows, width = matrix.shape
    columns = lax.dynamic_slice_in_dim(act_group, lax.axis_index("frame") * rows, rows, axis=1)
    partial = mat_dot(columns, matrix).reshape(parts, frames, width)
    return jnp.sum(lax.all_to_all(partial, "frame", split_axis=0, concat_axis=0), axis=0)


def reduced(grads):
    groups, parts = lax.axis_size("dp"), lax.axis_size("frame")
    width = min(grad.shape[1] for grad in grads)
    blocks = []
    for grad in grads:
        rows = grad.shape[0] // (groups * parts)
        part = grad.astype(jnp.bfloat16).reshape(parts, groups, rows, grad.shape[1])
        blocks.append(stacked(jnp.swapaxes(part, 0, 1), width))
    stack = jnp.concatenate(blocks, axis=2)
    size = stack.shape[2]
    column = lax.psum_scatter(stack.reshape(-1, width), "dp", scatter_dimension=0, tiled=True)
    mine = lax.psum_scatter(column, "frame", scatter_dimension=0, tiled=True)
    whole = lax.all_gather(mine, "dp", axis=0, tiled=True).reshape(groups, size, width)
    results, at = [], 0
    for grad, block in zip(grads, blocks):
        part = unstacked(whole[:, at : at + block.shape[2]], grad.shape[1] // width)
        results.append(part.reshape(-1, grad.shape[1]).astype(jnp.float32))
        at += block.shape[2]
    return results


def per_device(
    frames_in,
    condition,
    segments,
    spatial_in,
    spatial_in_bias,
    spatial_out,
    spatial_out_bias,
    temporal_in,
    temporal_in_bias,
    temporal_out,
    temporal_out_bias,
    expand_weight,
    expand_bias,
    shrink_weight,
    shrink_bias,
    modulate_weight,
    modulate_bias,
    cotangent,
):
    bfloat = jnp.bfloat16
    full_spatial_in = gathered([spatial_in])[0]
    full_spatial_out, full_temporal_in, full_temporal_out = gathered(
        [spatial_out, temporal_in, temporal_out]
    )
    full_expand, full_shrink = gathered([expand_weight, shrink_weight])
    biases = [
        spatial_in_bias,
        spatial_out_bias,
        temporal_in_bias,
        temporal_out_bias,
        expand_bias,
        shrink_bias,
        modulate_bias,
    ]
    (
        full_spatial_inb,
        full_spatial_outb,
        full_temporal_inb,
        full_temporal_outb,
        full_expand_bias,
        full_shrink_bias,
        full_modulate_bias,
        cond_group,
    ) = gathered_small(biases, condition)
    frames, patches, model_width = frames_in.shape
    heads_shape = (frames, patches, HEADS, HEAD_DIM)
    scaling = HEAD_DIM ** (-0.5)
    span_count = 2 * WINDOW + 1
    cond_float = condition.astype(jnp.float32)
    act_group = jax.nn.silu(cond_group.astype(jnp.float32)).astype(bfloat)
    modvec = modulated(act_group, modulate_weight, frames) + full_modulate_bias
    pieces = jnp.split(modvec, 9, axis=1)
    hidden_in = frames_in.astype(jnp.float32)
    normed_one = norm_mod(hidden_in, pieces[0], pieces[1]).astype(bfloat)
    qkv_one = (mat_dot(normed_one, full_spatial_in) + full_spatial_inb).astype(bfloat)
    queries = qkv_one[..., :model_width].reshape(heads_shape)
    keyset = qkv_one[..., model_width : 2 * model_width].reshape(heads_shape)
    valset = qkv_one[..., 2 * model_width :].reshape(heads_shape)
    raw_one = (
        jnp.einsum("fphd,fqhd->fhpq", queries, keyset, preferred_element_type=jnp.float32) * scaling
    )
    top_one = jnp.max(raw_one, axis=-1, keepdims=True)
    expo_one = jnp.exp(raw_one - top_one)
    total_one = jnp.sum(expo_one, axis=-1, keepdims=True)
    probs_one = (expo_one / total_one).astype(bfloat)
    lse_one = top_one + jnp.log(total_one)
    attn_one = jnp.einsum("fhpq,fqhd->fphd", probs_one, valset, preferred_element_type=jnp.float32)
    attn_one = attn_one.astype(bfloat).reshape(frames, patches, model_width)
    branch_one = mat_dot(attn_one, full_spatial_out) + full_spatial_outb
    after_one = hidden_in + pieces[2][:, None, :] * branch_one
    normed_two = norm_mod(after_one, pieces[3], pieces[4]).astype(bfloat)
    qkv_two = (mat_dot(normed_two, full_temporal_in) + full_temporal_inb).astype(bfloat)
    query_two = qkv_two[..., :model_width].reshape(heads_shape)
    kv_ext = extended(qkv_two[..., model_width:], (("frame", 0),), WINDOW)
    seg_row = segments[0]
    seg_pad = jnp.pad(seg_row, (WINDOW, WINDOW), constant_values=-1)
    begin = lax.axis_index("frame") * frames
    nearby = lax.dynamic_slice_in_dim(seg_pad, begin, frames + 2 * WINDOW)
    own_seg = nearby[WINDOW : WINDOW + frames]
    allowed = jnp.stack(
        [nearby[offset : offset + frames] == own_seg for offset in range(span_count)]
    )
    key_stack = jnp.stack(
        [kv_ext[offset : offset + frames, :, :model_width] for offset in range(span_count)]
    )
    key_stack = key_stack.reshape((span_count,) + heads_shape)
    val_stack = jnp.stack(
        [kv_ext[offset : offset + frames, :, model_width:] for offset in range(span_count)]
    )
    val_stack = val_stack.reshape((span_count,) + heads_shape)
    raw_two = (
        jnp.einsum("fphd,jfphd->jfhp", query_two, key_stack, preferred_element_type=jnp.float32)
        * scaling
    )
    masked = jnp.where(allowed[:, :, None, None], raw_two, -1e30)
    top_two = jnp.max(masked, axis=0, keepdims=True)
    expo_two = jnp.exp(masked - top_two)
    probs_two = expo_two / jnp.sum(expo_two, axis=0, keepdims=True)
    probs_low = probs_two.astype(bfloat)
    attn_two = jnp.einsum(
        "jfhp,jfphd->fphd", probs_low, val_stack, preferred_element_type=jnp.float32
    )
    attn_two = attn_two.astype(bfloat).reshape(frames, patches, model_width)
    branch_two = mat_dot(attn_two, full_temporal_out) + full_temporal_outb
    after_two = after_one + pieces[5][:, None, :] * branch_two
    normed_three = norm_mod(after_two, pieces[6], pieces[7]).astype(bfloat)
    pre_act = mat_dot(normed_three, full_expand) + full_expand_bias
    activ, gelu_pull = jax.vjp(gelu_exact, pre_act)
    activ_low = activ.astype(bfloat)
    branch_three = mat_dot(activ_low, full_shrink) + full_shrink_bias
    result = after_two + pieces[8][:, None, :] * branch_three
    frames_out = result.astype(bfloat)
    grad_three = cotangent.astype(jnp.float32)
    dgate_three = jnp.sum(grad_three * branch_three, axis=1)
    dbranch_three = (pieces[8][:, None, :] * grad_three).astype(bfloat)
    grad_shrink_weight = outer_sum(activ_low, dbranch_three)
    grad_shrink_bias = column_sum(dbranch_three)
    dactiv = back_dot(dbranch_three, full_shrink)
    dpre = gelu_pull(dactiv)[0].astype(bfloat)
    grad_expand_weight = outer_sum(normed_three, dpre)
    grad_expand_bias = column_sum(dpre)
    dnormed_three = back_dot(dpre, full_expand)
    dafter_two, dshift_three, dscale_three = jax.vjp(norm_mod, after_two, pieces[6], pieces[7])[1](
        dnormed_three
    )
    grad_two = grad_three + dafter_two
    dgate_two = jnp.sum(grad_two * branch_two, axis=1)
    dbranch_two = (pieces[5][:, None, :] * grad_two).astype(bfloat)
    grad_temporal_out = outer_sum(attn_two, dbranch_two)
    grad_temporal_out_bias = column_sum(dbranch_two)
    dattn_two = back_dot(dbranch_two, full_temporal_out).astype(bfloat).reshape(heads_shape)
    dprob_two = jnp.einsum(
        "fphd,jfphd->jfhp", dattn_two, val_stack, preferred_element_type=jnp.float32
    )
    rowdot_two = jnp.sum(probs_two * dprob_two, axis=0, keepdims=True)
    dscore_two = (probs_two * (dprob_two - rowdot_two)).astype(bfloat)
    dquery_two = (
        jnp.einsum("jfhp,jfphd->fphd", dscore_two, key_stack, preferred_element_type=jnp.float32)
        * scaling
    )
    dkey_stack = (
        jnp.einsum("jfhp,fphd->jfphd", dscore_two, query_two, preferred_element_type=jnp.float32)
        * scaling
    )
    dval_stack = jnp.einsum(
        "jfhp,fphd->jfphd", probs_low, dattn_two, preferred_element_type=jnp.float32
    )
    stack_shape = (span_count, frames, patches, model_width)
    dkv_stack = jnp.concatenate(
        [dkey_stack.reshape(stack_shape), dval_stack.reshape(stack_shape)], axis=-1
    )
    ext_grad = jnp.zeros((frames + 2 * WINDOW, patches, 2 * model_width), jnp.float32)
    for offset in range(span_count):
        ext_grad = ext_grad.at[offset : offset + frames].add(dkv_stack[offset])
    from_right = passed_along(ext_grad[:WINDOW].astype(jnp.bfloat16), "frame", -1).astype(
        jnp.float32
    )
    from_left = passed_along(ext_grad[frames + WINDOW :].astype(jnp.bfloat16), "frame", 1).astype(
        jnp.float32
    )
    inner_grad = ext_grad[WINDOW : WINDOW + frames]
    inner_grad = inner_grad.at[:WINDOW].add(from_left).at[frames - WINDOW :].add(from_right)
    dqkv_two = jnp.concatenate(
        [dquery_two.reshape(frames, patches, model_width), inner_grad], axis=-1
    ).astype(bfloat)
    grad_temporal_in = outer_sum(normed_two, dqkv_two)
    grad_temporal_in_bias = column_sum(dqkv_two)
    dnormed_two = back_dot(dqkv_two, full_temporal_in)
    dafter_one, dshift_two, dscale_two = jax.vjp(norm_mod, after_one, pieces[3], pieces[4])[1](
        dnormed_two
    )
    grad_one = grad_two + dafter_one
    dgate_one = jnp.sum(grad_one * branch_one, axis=1)
    dbranch_one = (pieces[2][:, None, :] * grad_one).astype(bfloat)
    grad_spatial_out = outer_sum(attn_one, dbranch_one)
    grad_spatial_out_bias = column_sum(dbranch_one)
    dattn_one = back_dot(dbranch_one, full_spatial_out).astype(bfloat).reshape(heads_shape)
    raw_again = (
        jnp.einsum("fphd,fqhd->fhpq", queries, keyset, preferred_element_type=jnp.float32) * scaling
    )
    probs_again = jnp.exp(raw_again - lse_one)
    dprob_one = jnp.einsum("fphd,fqhd->fhpq", dattn_one, valset, preferred_element_type=jnp.float32)
    rowdot_one = jnp.sum(probs_again * dprob_one, axis=-1, keepdims=True)
    dscore_one = (probs_again * (dprob_one - rowdot_one)).astype(bfloat)
    dquery_one = (
        jnp.einsum("fhpq,fqhd->fphd", dscore_one, keyset, preferred_element_type=jnp.float32)
        * scaling
    )
    dkeys_one = (
        jnp.einsum("fhpq,fphd->fqhd", dscore_one, queries, preferred_element_type=jnp.float32)
        * scaling
    )
    dvals_one = jnp.einsum(
        "fhpq,fphd->fqhd", probs_again.astype(bfloat), dattn_one, preferred_element_type=jnp.float32
    )
    row_shape = (frames, patches, model_width)
    dqkv_one = jnp.concatenate(
        [dquery_one.reshape(row_shape), dkeys_one.reshape(row_shape), dvals_one.reshape(row_shape)],
        axis=-1,
    ).astype(bfloat)
    grad_spatial_in = outer_sum(normed_one, dqkv_one)
    grad_spatial_in_bias = column_sum(dqkv_one)
    dnormed_one = back_dot(dqkv_one, full_spatial_in)
    dinput, dshift_one, dscale_one = jax.vjp(norm_mod, hidden_in, pieces[0], pieces[1])[1](
        dnormed_one
    )
    grad_frames = grad_one + dinput
    dmod = jnp.concatenate(
        [
            dshift_one,
            dscale_one,
            dgate_one,
            dshift_two,
            dscale_two,
            dgate_two,
            dshift_three,
            dscale_three,
            dgate_three,
        ],
        axis=1,
    ).astype(bfloat)
    own_act = jax.nn.silu(cond_float).astype(bfloat)
    every = lax.all_gather(jnp.concatenate([own_act, dmod], axis=1), "frame", axis=0, tiled=True)
    dmod_group = every[:, model_width:]
    every = lax.all_gather(every, "dp", axis=0, tiled=True)
    rows = modulate_weight.shape[0]
    place = lax.axis_index("frame")
    parts = lax.axis_size("frame")
    own_columns = lax.dynamic_slice_in_dim(every[:, :model_width], place * rows, rows, axis=1)
    grad_modulate_weight = outer_sum(own_columns, every[:, model_width:])
    grad_modulate_bias = own_part(column_sum(every[:, model_width:]))
    dact_group = back_dot(dmod_group, modulate_weight)
    pieces_act = lax.all_to_all(
        dact_group.reshape(parts, frames, rows), "frame", split_axis=0, concat_axis=0
    )
    dcond_act = jnp.swapaxes(pieces_act, 0, 1).reshape(frames, parts * rows)
    grad_condition = jax.vjp(jax.nn.silu, cond_float)[1](dcond_act)[0]
    grad_expand_sum, grad_shrink_sum = reduced([grad_expand_weight, grad_shrink_weight])
    (
        grad_spatial_in_sum,
        grad_spatial_out_sum,
        grad_temporal_in_sum,
        grad_temporal_out_sum,
    ) = reduced([grad_spatial_in, grad_spatial_out, grad_temporal_in, grad_temporal_out])
    bias_grads = [
        grad_spatial_in_bias,
        grad_spatial_out_bias,
        grad_temporal_in_bias,
        grad_temporal_out_bias,
        grad_expand_bias,
        grad_shrink_bias,
    ]
    together = lax.psum(jnp.concatenate(bias_grads), ("dp", "frame"))
    bias_sums, at = [], 0
    for grad in bias_grads:
        bias_sums.append(own_part(together[at : at + grad.shape[0]]))
        at += grad.shape[0]
    return (
        frames_out,
        grad_frames,
        grad_condition,
        grad_spatial_in_sum,
        bias_sums[0],
        grad_spatial_out_sum,
        bias_sums[1],
        grad_temporal_in_sum,
        bias_sums[2],
        grad_temporal_out_sum,
        bias_sums[3],
        grad_expand_sum,
        bias_sums[4],
        grad_shrink_sum,
        bias_sums[5],
        grad_modulate_weight,
        grad_modulate_bias,
    )


def solution(mesh):
    in_specs = (
        P(("dp", "frame"), None, None),
        P(("dp", "frame"), None),
        P("dp", None),
        P("frame", None),
        P("frame"),
        P("frame", None),
        P("frame"),
        P("frame", None),
        P("frame"),
        P("frame", None),
        P("frame"),
        P("frame", None),
        P("frame"),
        P("frame", None),
        P("frame"),
        P("frame", None),
        P("frame"),
        P(("dp", "frame"), None, None),
    )
    out_specs = (
        P(("dp", "frame"), None, None),
        P(("dp", "frame"), None, None),
        P(("dp", "frame"), None),
        P("frame", None),
        P("frame"),
        P("frame", None),
        P("frame"),
        P("frame", None),
        P("frame"),
        P("frame", None),
        P("frame"),
        P("frame", None),
        P("frame"),
        P("frame", None),
        P("frame"),
        P("frame", None),
        P("frame"),
    )
    return jax.shard_map(
        per_device, mesh=mesh, in_specs=in_specs, out_specs=out_specs, check_vma=False
    )
```

```python
import functools

import jax
import jax.numpy as jnp
from jax import lax
from jax.experimental import pallas as pl
from jax.experimental.pallas import tpu as pltpu
from jax.sharding import PartitionSpec as P

HEADS = 12
HEAD_DIM = 64
WINDOW = 2

F32 = jnp.float32
BF16 = jnp.bfloat16
SCALE = HEAD_DIM ** (-0.5)
SPAN = 2 * WINDOW + 1


def mm(a, b):
    return lax.dot_general(a, b, (((1,), (0,)), ((), ())), preferred_element_type=F32)


def mm_nt(a, b):
    return lax.dot_general(a, b, (((1,), (1,)), ((), ())), preferred_element_type=F32)


def mm_tn(a, b):
    return lax.dot_general(a, b, (((0,), (0,)), ((), ())), preferred_element_type=F32)


def unit(x):
    centred = x - jnp.mean(x, axis=-1, keepdims=True)
    inv = lax.rsqrt(jnp.mean(centred * centred, axis=-1, keepdims=True) + 1e-06)
    return centred * inv, inv


def unit_back(dn, xhat, inv, scale):
    e = dn * (1.0 + scale)
    first = jnp.mean(e, axis=-1, keepdims=True)
    second = jnp.mean(e * xhat, axis=-1, keepdims=True)
    return inv * (e - first - xhat * second)


def down(x):
    return jnp.sum(x, axis=0, keepdims=True)


def low_half(rows):
    return lax.broadcasted_iota(jnp.int32, (rows, 2 * HEAD_DIM), 1) < HEAD_DIM


def soft(scores):
    e = jnp.exp(scores - jnp.max(scores, axis=-1, keepdims=True))
    return e / jnp.sum(e, axis=-1, keepdims=True)


def params(flops, nbytes, trans=0):
    return dict(
        compiler_params=pltpu.CompilerParams(vmem_limit_bytes=60 * 2**20),
        cost_estimate=pl.CostEstimate(
            flops=int(flops), bytes_accessed=int(nbytes), transcendentals=int(trans)
        ),
    )


def fixed(shape):
    return pl.BlockSpec(shape, lambda *_: (0,) * len(shape), pipeline_mode=pl.Buffered(1))


def per_first(shape):
    return pl.BlockSpec((1,) + shape, lambda i: (i,) + (0,) * len(shape))


def per_second(lead, tile, width):
    return pl.BlockSpec((lead, tile, width), lambda i: (0, i, 0))


def spatial_kernel(
    x_ref, mod_ref, wsi, bsi, wso, bso, wti, bti,
    n1_ref, qkv1_ref, attn_ref, branch_ref, after_ref, n2_ref, qkv2_ref,
):
    x = x_ref[0].astype(F32)
    width = x.shape[1]
    xhat, _ = unit(x)
    n1 = (xhat * (1.0 + mod_ref[0, 1:2]) + mod_ref[0, 0:1]).astype(BF16)
    n1_ref[0] = n1
    qkv1_ref[0] = (mm(n1, wsi[...]) + bsi[...]).astype(BF16)
    half = low_half(x.shape[0])
    for pair in range(width // (2 * HEAD_DIM)):
        at = pair * 2 * HEAD_DIM
        q = qkv1_ref[0, :, at : at + 2 * HEAD_DIM]
        k = qkv1_ref[0, :, width + at : width + at + 2 * HEAD_DIM]
        v = qkv1_ref[0, :, 2 * width + at : 2 * width + at + 2 * HEAD_DIM]
        zero = jnp.zeros_like(q)
        first = soft(mm_nt(jnp.where(half, q, zero), k) * SCALE).astype(BF16)
        second = soft(mm_nt(jnp.where(half, zero, q), k) * SCALE).astype(BF16)
        out = jnp.where(half, mm(first, v), mm(second, v))
        attn_ref[0, :, at : at + 2 * HEAD_DIM] = out.astype(BF16)
    branch = mm(attn_ref[0], wso[...]) + bso[...]
    branch_ref[0] = branch
    after = x + mod_ref[0, 2:3] * branch
    after_ref[0] = after
    xhat2, _ = unit(after)
    n2 = (xhat2 * (1.0 + mod_ref[0, 4:5]) + mod_ref[0, 3:4]).astype(BF16)
    n2_ref[0] = n2
    qkv2_ref[0] = (mm(n2, wti[...]) + bti[...]).astype(BF16)


def spatial_forward(x, mod, wsi, bsi, wso, bso, wti, bti):
    frames, patches, width = x.shape
    shape = lambda n, t: jax.ShapeDtypeStruct((frames, patches, n), t)
    block = lambda n: per_first((patches, n))
    outs = [(width, BF16), (3 * width, BF16), (width, BF16), (width, F32), (width, F32),
            (width, BF16), (3 * width, BF16)]
    tokens = frames * patches
    return pl.pallas_call(
        spatial_kernel,
        grid=(frames,),
        in_specs=[block(width), per_first(mod.shape[1:])]
        + [fixed(w.shape) for w in (wsi, bsi, wso, bso, wti, bti)],
        out_specs=[block(n) for n, _ in outs],
        out_shape=[shape(n, t) for n, t in outs],
        name="spatial_forward",
        **params(2 * tokens * width * (7 * width + 2 * patches), 24e6, tokens * patches * HEADS),
    )(x, mod, wsi, bsi, wso, bso, wti, bti)


def split_store(hi_ref, lo_ref, row, prod):
    hi = prod.astype(BF16)
    hi_ref[row] = hi
    lo_ref[row] = (prod - hi.astype(F32)).astype(BF16)


def ext_rows(e, frames, left, own, right, base, width):
    if e < WINDOW:
        return left[e, :, base - width : base]
    if e < WINDOW + frames:
        return own[e - WINDOW, :, base : base + width]
    return right[e - WINDOW - frames, :, base - width : base]


def head_sums(hi_ref, lo_ref, first, count, ones):
    tile, width = hi_ref.shape[1:]
    hi = hi_ref[first : first + count].reshape(count * tile, width)
    lo = lo_ref[first : first + count].reshape(count * tile, width)
    return mm(hi, ones) + mm(lo, ones)


def temporal_kernel(
    allowed, qkv_ref, left_ref, right_ref, after_ref, mod_ref, wto, bto, ones, ones_t,
    probs_ref, attn_ref, branch_ref, out_ref, hi_ref, lo_ref,
):
    frames, tile, width = after_ref.shape
    for t in range(frames):
        q = qkv_ref[t, :, :width].astype(F32)
        for o in range(SPAN):
            k = ext_rows(t + o, frames, left_ref, qkv_ref, right_ref, width, width)
            split_store(hi_ref, lo_ref, t * SPAN + o, q * k.astype(F32))
    for t in range(frames):
        raw = head_sums(hi_ref, lo_ref, t * SPAN, SPAN, ones[...]) * SCALE
        raw = [
            jnp.where(allowed[o, t] > 0, raw[o * tile : (o + 1) * tile], -1e30)
            for o in range(SPAN)
        ]
        top = raw[0]
        for o in range(1, SPAN):
            top = jnp.maximum(top, raw[o])
        expo = [jnp.exp(r - top) for r in raw]
        total = expo[0]
        for o in range(1, SPAN):
            total = total + expo[o]
        inv = 1.0 / total
        probs = [e * inv for e in expo]
        for o in range(SPAN):
            probs_ref[t, o] = probs[o]
        wide = mm(jnp.concatenate(probs, axis=0).astype(BF16), ones_t[...])
        total = None
        for o in range(SPAN):
            v = ext_rows(t + o, frames, left_ref, qkv_ref, right_ref, 2 * width, width)
            term = wide[o * tile : (o + 1) * tile] * v.astype(F32)
            total = term if total is None else total + term
        attn_ref[t] = total.astype(BF16)
    branch = mm(attn_ref[...].reshape(frames * tile, width), wto[...]) + bto[...]
    for t in range(frames):
        part = branch[t * tile : (t + 1) * tile]
        branch_ref[t] = part
        out_ref[t] = after_ref[t] + mod_ref[t, 5:6] * part


def head_ones(width):
    head = jnp.arange(width, dtype=jnp.int32)[:, None] // HEAD_DIM
    return (head == jnp.arange(128, dtype=jnp.int32)[None, :]).astype(BF16)


def temporal_forward(allowed, qkv, left, right, after, mod, wto, bto):
    frames, patches, width = after.shape
    tile = 64
    ones = head_ones(width)
    spec = lambda n: per_second(frames, tile, n)
    halo = per_second(WINDOW, tile, 2 * width)
    shape = lambda t: jax.ShapeDtypeStruct((frames, patches, width), t)
    tokens = frames * patches
    return pl.pallas_call(
        temporal_kernel,
        grid=(patches // tile,),
        in_specs=[
            pl.BlockSpec(memory_space=pltpu.SMEM),
            spec(3 * width), halo, halo, spec(width),
            fixed(mod.shape), fixed(wto.shape), fixed(bto.shape),
            fixed(ones.shape), fixed(ones.shape[::-1]),
        ],
        out_specs=[
            pl.BlockSpec((frames, SPAN, tile, 128), lambda i: (0, 0, i, 0)),
            spec(width), spec(width), spec(width),
        ],
        out_shape=[
            jax.ShapeDtypeStruct((frames, SPAN, patches, 128), F32),
            shape(BF16), shape(F32), shape(F32),
        ],
        scratch_shapes=[pltpu.VMEM((frames * SPAN, tile, width), BF16)] * 2,
        name="temporal_forward",
        **params(2 * tokens * width * (width + SPAN * 400), 22e6, tokens * SPAN * 128),
    )(allowed, qkv, left, right, after, mod, wto, bto, ones, ones.T)


def feed_kernel(
    after_ref, cot_ref, mod_ref, w1, b1, w2, b2,
    out_ref, g_ref, n_ref, act_ref, dpre_ref, db_ref, dmod_ref, sum1_ref, sum2_ref,
):
    after = after_ref[0]
    width = after.shape[1]
    hidden = w1.shape[1]
    xhat, inv = unit(after)
    scale = mod_ref[0, 7:8]
    gate = mod_ref[0, 8:9]
    n = (xhat * (1.0 + scale) + mod_ref[0, 6:7]).astype(BF16)
    n_ref[0] = n
    g3 = cot_ref[0].astype(F32)
    db = (gate * g3).astype(BF16)
    db_ref[0] = db

    @pl.when(pl.program_id(0) == 0)
    def _():
        sum1_ref[...] = jnp.zeros_like(sum1_ref)
        sum2_ref[...] = jnp.zeros_like(sum2_ref)

    sum2_ref[...] += down(db.astype(F32))
    branch = jnp.zeros_like(after)
    dn = jnp.zeros_like(after)
    chunk = width
    for c in range(hidden // chunk):
        cols = slice(c * chunk, (c + 1) * chunk)
        pre = mm(n, w1[:, cols]) + b1[:, cols]
        dact = mm_nt(db, w2[cols, :])
        phi = 0.5 * (1.0 + lax.erf(pre * 0.7071067811865476))
        act = (pre * phi).astype(BF16)
        slope = phi + pre * (jnp.exp(-0.5 * pre * pre) * 0.3989422804014327)
        dpre = (dact * slope).astype(BF16)
        act_ref[0, :, cols] = act
        dpre_ref[0, :, cols] = dpre
        sum1_ref[:, cols] += down(dpre.astype(F32))
        branch += mm(act, w2[cols, :])
        dn += mm_nt(dpre, w1[:, cols])
    branch = branch + b2[...]
    out_ref[0] = (after + gate * branch).astype(BF16)
    dmod_ref[0, 0:1] = down(dn)
    dmod_ref[0, 1:2] = down(dn * xhat)
    dmod_ref[0, 2:3] = down(g3 * branch)
    g_ref[0] = g3 + unit_back(dn, xhat, inv, scale)


def feed_forward(after, cot, mod, w1, b1, w2, b2):
    frames, patches, width = after.shape
    hidden = w1.shape[1]
    shape = lambda n, t: jax.ShapeDtypeStruct((frames, patches, n), t)
    block = lambda n: per_first((patches, n))
    outs = [(width, BF16), (width, F32), (width, BF16), (hidden, BF16), (hidden, BF16), (width, BF16)]
    tokens = frames * patches
    return pl.pallas_call(
        feed_kernel,
        grid=(frames,),
        in_specs=[block(width), block(width), per_first(mod.shape[1:])]
        + [fixed(w.shape) for w in (w1, b1, w2, b2)],
        out_specs=[block(n) for n, _ in outs]
        + [per_first((3, width)), pl.BlockSpec((1, hidden), lambda i: (0, 0)),
           pl.BlockSpec((1, width), lambda i: (0, 0))],
        out_shape=[shape(n, t) for n, t in outs]
        + [jax.ShapeDtypeStruct((frames, 3, width), F32),
           jax.ShapeDtypeStruct((1, hidden), F32), jax.ShapeDtypeStruct((1, width), F32)],
        name="feed_forward",
        **params(8 * tokens * width * hidden, 32e6, 2 * tokens * hidden),
    )(after, cot, mod, w1, b1, w2, b2)


def temporal_back_kernel(
    g_ref, branch_ref, mod_ref, wto, qkv_ref, left_ref, right_ref, probs_ref, ones, ones_t,
    db_ref, dq_ref, dkv_ref, dleft_ref, dright_ref, dgate_ref, sum_ref,
    hi_ref, lo_ref, da_ref, ds_ref, pw_ref,
):
    frames, tile, width = g_ref.shape

    @pl.when(pl.program_id(0) == 0)
    def _():
        dgate_ref[...] = jnp.zeros_like(dgate_ref)
        sum_ref[...] = jnp.zeros_like(sum_ref)

    for t in range(frames):
        g = g_ref[t]
        dgate_ref[t : t + 1] += down(g * branch_ref[t])
        db = (mod_ref[t, 5:6] * g).astype(BF16)
        db_ref[t] = db
        sum_ref[...] += down(db.astype(F32))
    da_all = mm_nt(db_ref[...].reshape(frames * tile, width), wto[...]).astype(BF16)
    da_ref[...] = da_all.reshape(frames, tile, width)
    for t in range(frames):
        da = da_ref[t].astype(F32)
        for o in range(SPAN):
            v = ext_rows(t + o, frames, left_ref, qkv_ref, right_ref, 2 * width, width)
            split_store(hi_ref, lo_ref, t * SPAN + o, da * v.astype(F32))
    for t in range(frames):
        dp = head_sums(hi_ref, lo_ref, t * SPAN, SPAN, ones[...])
        probs = probs_ref[t].reshape(SPAN * tile, 128)
        both = probs * dp
        dot = both[:tile]
        for o in range(1, SPAN):
            dot = dot + both[o * tile : (o + 1) * tile]
        ds = both - probs * jnp.concatenate([dot] * SPAN, axis=0)
        wide = mm(ds.astype(BF16), ones_t[...]).astype(BF16)
        ds_ref[t * SPAN : (t + 1) * SPAN] = wide.reshape(SPAN, tile, width)
        wide = mm(probs.astype(BF16), ones_t[...]).astype(BF16)
        pw_ref[t * SPAN : (t + 1) * SPAN] = wide.reshape(SPAN, tile, width)
    for t in range(frames):
        total = None
        for o in range(SPAN):
            k = ext_rows(t + o, frames, left_ref, qkv_ref, right_ref, width, width)
            term = ds_ref[t * SPAN + o].astype(F32) * k.astype(F32)
            total = term if total is None else total + term
        dq_ref[t] = (total * SCALE).astype(BF16)
    for e in range(frames + 2 * WINDOW):
        dk = dv = None
        for t in range(max(0, e - SPAN + 1), min(frames, e + 1)):
            row = t * SPAN + e - t
            q = qkv_ref[t, :, :width].astype(F32)
            term = ds_ref[row].astype(F32) * q
            dk = term if dk is None else dk + term
            term = pw_ref[row].astype(F32) * da_ref[t].astype(F32)
            dv = term if dv is None else dv + term
        dk = dk * SCALE
        if e < WINDOW:
            dleft_ref[e, :, :width] = dk.astype(BF16)
            dleft_ref[e, :, width:] = dv.astype(BF16)
        elif e < WINDOW + frames:
            dkv_ref[e - WINDOW, :, :width] = dk
            dkv_ref[e - WINDOW, :, width:] = dv
        else:
            dright_ref[e - WINDOW - frames, :, :width] = dk.astype(BF16)
            dright_ref[e - WINDOW - frames, :, width:] = dv.astype(BF16)


def temporal_backward(g, branch, mod, wto, qkv, left, right, probs):
    frames, patches, width = g.shape
    tile = 64
    ones = head_ones(width)
    spec = lambda n: per_second(frames, tile, n)
    halo = per_second(WINDOW, tile, 2 * width)
    shape = lambda f, n, t: jax.ShapeDtypeStruct((f, patches, n), t)
    tokens = frames * patches
    return pl.pallas_call(
        temporal_back_kernel,
        grid=(patches // tile,),
        in_specs=[
            spec(width), spec(width), fixed(mod.shape), fixed(wto.shape), spec(3 * width), halo, halo,
            pl.BlockSpec((frames, SPAN, tile, 128), lambda i: (0, 0, i, 0)),
            fixed(ones.shape), fixed(ones.shape[::-1]),
        ],
        out_specs=[
            spec(width), spec(width), spec(2 * width), halo, halo,
            pl.BlockSpec((frames, width), lambda i: (0, 0)),
            pl.BlockSpec((1, width), lambda i: (0, 0)),
        ],
        out_shape=[
            shape(frames, width, BF16), shape(frames, width, BF16), shape(frames, 2 * width, F32),
            shape(WINDOW, 2 * width, BF16), shape(WINDOW, 2 * width, BF16),
            jax.ShapeDtypeStruct((frames, width), F32), jax.ShapeDtypeStruct((1, width), F32),
        ],
        scratch_shapes=[pltpu.VMEM((frames * SPAN, tile, width), BF16)] * 2
        + [pltpu.VMEM((frames, tile, width), BF16)]
        + [pltpu.VMEM((frames * SPAN, tile, width), BF16)] * 2,
        name="temporal_backward",
        **params(2 * tokens * width * (width + SPAN * 500), 36e6),
    )(g, branch, mod, wto, qkv, left, right, probs, ones, ones.T)


def spatial_back_kernel(
    dq2_ref, dkv2_ref, fl_ref, fr_ref, after_ref, g2_ref, branch_ref, x_ref, qkv_ref, mod_ref,
    wti, wso, wsi,
    dqkv2_ref, db_ref, dqkv1_ref, grad_ref, dmod_ref, sum2_ref, sumb_ref, sum1_ref, da_ref,
):
    tokens, width = after_ref.shape[1:]
    at = pl.program_id(0)

    @pl.when(at == 0)
    def _():
        sum2_ref[...] = jnp.zeros_like(sum2_ref)
        sumb_ref[...] = jnp.zeros_like(sumb_ref)
        sum1_ref[...] = jnp.zeros_like(sum1_ref)

    dqkv2_ref[0, :, :width] = dq2_ref[0]
    extra = jnp.where(at < WINDOW, fl_ref[0].astype(F32), fr_ref[0].astype(F32))
    dqkv2_ref[0, :, width:] = (dkv2_ref[0] + extra).astype(BF16)
    sum2_ref[...] += down(dqkv2_ref[0].astype(F32))
    dn = mm_nt(dqkv2_ref[0], wti[...])
    xhat, inv = unit(after_ref[0])
    dmod_ref[0, 3:4] = down(dn)
    dmod_ref[0, 4:5] = down(dn * xhat)
    g1 = g2_ref[0] + unit_back(dn, xhat, inv, mod_ref[0, 4:5])
    dmod_ref[0, 2:3] = down(g1 * branch_ref[0])
    db = (mod_ref[0, 2:3] * g1).astype(BF16)
    db_ref[0] = db
    sumb_ref[...] += down(db.astype(F32))
    grad_ref[0] = g1
    da_ref[...] = mm_nt(db, wso[...]).astype(BF16)
    half = low_half(tokens)
    for pair in range(width // (2 * HEAD_DIM)):
        cols = slice(pair * 2 * HEAD_DIM, (pair + 1) * 2 * HEAD_DIM)
        kcols = slice(width + cols.start, width + cols.stop)
        vcols = slice(2 * width + cols.start, 2 * width + cols.stop)
        q = qkv_ref[0, :, cols]
        k = qkv_ref[0, :, kcols]
        v = qkv_ref[0, :, vcols]
        da = da_ref[:, cols]
        zero = jnp.zeros_like(q)
        parts = []
        for side in range(2):
            pick = (lambda u: jnp.where(half, u, zero)) if side == 0 else (
                lambda u: jnp.where(half, zero, u))
            probs = soft(mm_nt(pick(q), k) * SCALE)
            dp = mm_nt(pick(da), v)
            both = probs * dp
            ds = (both - probs * jnp.sum(both, axis=-1, keepdims=True)).astype(BF16)
            parts.append((mm(ds, k), mm_tn(ds, q), mm_tn(probs.astype(BF16), da)))
        dq, dk, dv = (jnp.where(half, a, b) for a, b in zip(*parts))
        dqkv1_ref[0, :, cols] = (dq * SCALE).astype(BF16)
        dqkv1_ref[0, :, kcols] = (dk * SCALE).astype(BF16)
        dqkv1_ref[0, :, vcols] = dv.astype(BF16)
    sum1_ref[...] += down(dqkv1_ref[0].astype(F32))
    dn = mm_nt(dqkv1_ref[0], wsi[...])
    xhat, inv = unit(x_ref[0].astype(F32))
    dmod_ref[0, 0:1] = down(dn)
    dmod_ref[0, 1:2] = down(dn * xhat)
    grad_ref[0] += unit_back(dn, xhat, inv, mod_ref[0, 1:2])


def spatial_backward(dq2, dkv2, from_left, from_right, after, g2, branch, x, qkv1, mod, wti, wso, wsi):
    frames, patches, width = x.shape
    shape = lambda n, t: jax.ShapeDtypeStruct((frames, patches, n), t)
    block = lambda n: per_first((patches, n))
    vector = lambda n: pl.BlockSpec((1, n), lambda i: (0, 0))
    tokens = frames * patches
    return pl.pallas_call(
        spatial_back_kernel,
        grid=(frames,),
        in_specs=[
            block(width), block(2 * width),
            pl.BlockSpec((1, patches, 2 * width), lambda i: (jnp.minimum(i, WINDOW - 1), 0, 0)),
            pl.BlockSpec((1, patches, 2 * width), lambda i: (jnp.maximum(i - WINDOW, 0), 0, 0)),
            block(width), block(width), block(width), block(width), block(3 * width),
            per_first(mod.shape[1:]), fixed(wti.shape), fixed(wso.shape), fixed(wsi.shape),
        ],
        out_specs=[
            block(3 * width), block(width), block(3 * width), block(width), per_first((5, width)),
            vector(3 * width), vector(width), vector(3 * width),
        ],
        out_shape=[
            shape(3 * width, BF16), shape(width, BF16), shape(3 * width, BF16), shape(width, F32),
            jax.ShapeDtypeStruct((frames, 5, width), F32),
            jax.ShapeDtypeStruct((1, 3 * width), F32), jax.ShapeDtypeStruct((1, width), F32),
            jax.ShapeDtypeStruct((1, 3 * width), F32),
        ],
        scratch_shapes=[pltpu.VMEM((patches, width), BF16)],
        name="spatial_backward",
        **params(2 * tokens * width * (7 * width + 5 * patches), 45e6, tokens * patches * HEADS),
    )(dq2, dkv2, from_left, from_right, after, g2, branch, x, qkv1, mod, wti, wso, wsi)


def outer_kernel(left_ref, right_ref, out_ref, *, groups):
    total = mm_tn(left_ref[...], right_ref[...])
    parts = out_ref.shape[1]
    rows = out_ref.shape[2]
    for f in range(parts):
        for d in range(groups):
            at = (f * groups + d) * rows
            out_ref[d, f] = total[at : at + rows].astype(BF16)


def outer_pieces(left, right, width, groups, parts):
    left = left.reshape(-1, left.shape[-1])
    right = right.reshape(-1, right.shape[-1])
    tokens, depth = left.shape
    rows = depth // (groups * parts)
    stacks = right.shape[1] // width
    if rows % 8:
        total = mm_tn(left, right).astype(BF16).reshape(parts, groups, rows, stacks, width)
        return total.transpose(1, 0, 3, 2, 4).reshape(groups, parts, stacks * rows, width)
    step = 1
    while (step * depth // parts) % 128:
        step *= 2
    return pl.pallas_call(
        functools.partial(outer_kernel, groups=groups),
        grid=(parts // step, stacks),
        in_specs=[
            pl.BlockSpec((tokens, step * depth // parts), lambda i, j: (0, i)),
            pl.BlockSpec((tokens, width), lambda i, j: (0, j)),
        ],
        out_specs=pl.BlockSpec((groups, step, rows, width), lambda i, j: (0, i, j, 0)),
        out_shape=jax.ShapeDtypeStruct((groups, parts, stacks * rows, width), BF16),
        name="outer_pieces",
        **params(2 * tokens * depth * right.shape[1], 2 * (left.size + right.size * 2)),
    )(left, right)


def own_part(vector):
    size = vector.shape[0] // lax.axis_size("frame")
    return lax.dynamic_slice_in_dim(vector, lax.axis_index("frame") * size, size)


def stacked(block, width):
    count = block.shape[-1] // width
    return jnp.concatenate(
        [block[..., k * width : (k + 1) * width] for k in range(count)], axis=-2
    )


def unstacked(block, count):
    rows = block.shape[-2] // count
    return jnp.concatenate(
        [block[..., k * rows : (k + 1) * rows, :] for k in range(count)], axis=-1
    )


def gathered(shards):
    groups, parts = lax.axis_size("dp"), lax.axis_size("frame")
    width = min(shard.shape[1] for shard in shards)
    pieces = []
    for shard in shards:
        rows = shard.shape[0] // groups
        piece = lax.dynamic_slice_in_dim(shard, lax.axis_index("dp") * rows, rows)
        pieces.append(stacked(piece, width))
    mine = jnp.concatenate(pieces, axis=0)
    column = lax.all_gather(mine, "frame", axis=0)
    whole = lax.all_gather(column, "dp", axis=0)
    results, at = [], 0
    for shard, piece in zip(shards, pieces):
        part = unstacked(whole[:, :, at : at + piece.shape[0]], shard.shape[1] // width)
        results.append(jnp.swapaxes(part, 0, 1).reshape(parts * shard.shape[0], shard.shape[1]))
        at += piece.shape[0]
    return results


def gathered_small(biases, condition):
    parts = lax.axis_size("frame")
    flat = jnp.concatenate(biases + [condition.reshape(-1)])
    rows = lax.all_gather(flat, "frame", axis=0)
    results, at = [], 0
    for bias in biases:
        results.append(rows[:, at : at + bias.shape[0]].reshape(-1))
        at += bias.shape[0]
    results.append(rows[:, at:].reshape(parts * condition.shape[0], condition.shape[1]))
    return results


def modulated(act_group, matrix, frames):
    parts = lax.axis_size("frame")
    rows, width = matrix.shape
    columns = lax.dynamic_slice_in_dim(act_group, lax.axis_index("frame") * rows, rows, axis=1)
    partial = mm(columns, matrix).reshape(parts, frames, width)
    return jnp.sum(lax.all_to_all(partial, "frame", split_axis=0, concat_axis=0), axis=0)


def passed_along(x, axis, by):
    peers = lax.axis_size(axis)
    pairs = [(i, i + by) for i in range(peers) if 0 <= i + by < peers]
    return lax.ppermute(x, axis, pairs)


def reduced(blocks, width_of):
    groups, parts = lax.axis_size("dp"), lax.axis_size("frame")
    stack = jnp.concatenate(blocks, axis=2)
    size, width = stack.shape[2:]
    column = lax.psum_scatter(stack.reshape(-1, width), "dp", scatter_dimension=0, tiled=True)
    mine = lax.psum_scatter(column, "frame", scatter_dimension=0, tiled=True)
    whole = lax.all_gather(mine, "dp", axis=0, tiled=True).reshape(groups, size, width)
    results, at = [], 0
    for block, full in zip(blocks, width_of):
        part = unstacked(whole[:, at : at + block.shape[2]], full // width)
        results.append(part.reshape(-1, full).astype(F32))
        at += block.shape[2]
    return results


def per_device(
    frames_in,
    condition,
    segments,
    spatial_in,
    spatial_in_bias,
    spatial_out,
    spatial_out_bias,
    temporal_in,
    temporal_in_bias,
    temporal_out,
    temporal_out_bias,
    expand_weight,
    expand_bias,
    shrink_weight,
    shrink_bias,
    modulate_weight,
    modulate_bias,
    cotangent,
):
    groups, parts = lax.axis_size("dp"), lax.axis_size("frame")
    place = lax.axis_index("frame")
    frames, patches, width = frames_in.shape
    full_spatial_in = gathered([spatial_in])[0]
    full_spatial_out, full_temporal_in, full_temporal_out = gathered(
        [spatial_out, temporal_in, temporal_out]
    )
    full_expand, full_shrink = gathered([expand_weight, shrink_weight])
    biases = [
        spatial_in_bias,
        spatial_out_bias,
        temporal_in_bias,
        temporal_out_bias,
        expand_bias,
        shrink_bias,
        modulate_bias,
    ]
    *full_biases, cond_group = gathered_small(biases, condition)
    sinb, soutb, tinb, toutb, expb, shrb, modb = [b.astype(F32)[None, :] for b in full_biases]
    act_group = jax.nn.silu(cond_group.astype(F32)).astype(BF16)
    modvec = modulated(act_group, modulate_weight, frames) + modb
    mod = modvec.reshape(frames, 9, width)
    n1, qkv1, attn1, branch1, after1, n2, qkv2 = spatial_forward(
        frames_in, mod, full_spatial_in, sinb, full_spatial_out, soutb, full_temporal_in, tinb
    )
    left = passed_along(qkv2[frames - WINDOW :, :, width:], "frame", 1)
    right = passed_along(qkv2[:WINDOW, :, width:], "frame", -1)
    seg_row = segments[0]
    seg_pad = jnp.pad(seg_row, (WINDOW, WINDOW), constant_values=-1)
    nearby = lax.dynamic_slice_in_dim(seg_pad, place * frames, frames + 2 * WINDOW)
    own_seg = nearby[WINDOW : WINDOW + frames]
    allowed = jnp.stack([nearby[o : o + frames] == own_seg for o in range(SPAN)]).astype(jnp.int32)
    probs, attn2, branch2, after2 = temporal_forward(
        allowed, qkv2, left, right, after1, mod, full_temporal_out, toutb
    )
    frames_out, g2, n3, act, dpre, db3, dmod3, sum_exp, sum_shr = feed_forward(
        after2, cotangent, mod, full_expand, expb, full_shrink, shrb
    )
    sums = reduced(
        [
            outer_pieces(n3, dpre, width, groups, parts),
            outer_pieces(act, db3, width, groups, parts),
        ],
        [dpre.shape[-1], width],
    )
    grad_expand_sum, grad_shrink_sum = sums
    db2, dq2, dkv2, dleft, dright, dgate2, sum_tout = temporal_backward(
        g2, branch2, mod, full_temporal_out, qkv2, left, right, probs
    )
    from_right = passed_along(dleft, "frame", -1)
    from_left = passed_along(dright, "frame", 1)
    dqkv2, db1, dqkv1, grad_frames, dmod12, sum_tin, sum_sout, sum_sin = spatial_backward(
        dq2, dkv2, from_left, from_right, after1, g2, branch1, frames_in, qkv1, mod,
        full_temporal_in, full_spatial_out, full_spatial_in,
    )
    (
        grad_temporal_out_sum,
        grad_temporal_in_sum,
        grad_spatial_out_sum,
        grad_spatial_in_sum,
    ) = reduced(
        [
            outer_pieces(attn2, db2, width, groups, parts),
            outer_pieces(n2, dqkv2, width, groups, parts),
            outer_pieces(attn1, db1, width, groups, parts),
            outer_pieces(n1, dqkv1, width, groups, parts),
        ],
        [width, 3 * width, width, 3 * width],
    )
    dmod = jnp.concatenate([dmod12, dgate2[:, None], dmod3], axis=1)
    dmod = dmod.reshape(frames, 9 * width).astype(BF16)
    cond_float = condition.astype(F32)
    own_act = jax.nn.silu(cond_float).astype(BF16)
    every = lax.all_gather(jnp.concatenate([own_act, dmod], axis=1), "frame", axis=0, tiled=True)
    dmod_group = every[:, width:]
    every = lax.all_gather(every, "dp", axis=0, tiled=True)
    rows = modulate_weight.shape[0]
    own_columns = lax.dynamic_slice_in_dim(every[:, :width], place * rows, rows, axis=1)
    grad_modulate_weight = mm_tn(own_columns, every[:, width:])
    grad_modulate_bias = own_part(jnp.sum(every[:, width:].astype(F32), axis=0))
    dact_group = mm_nt(dmod_group, modulate_weight)
    pieces_act = lax.all_to_all(
        dact_group.reshape(parts, frames, rows), "frame", split_axis=0, concat_axis=0
    )
    dcond_act = jnp.swapaxes(pieces_act, 0, 1).reshape(frames, parts * rows)
    grad_condition = jax.vjp(jax.nn.silu, cond_float)[1](dcond_act)[0]
    bias_grads = [s[0] for s in (sum_sin, sum_sout, sum_tin, sum_tout, sum_exp, sum_shr)]
    together = lax.psum(jnp.concatenate(bias_grads), ("dp", "frame"))
    bias_sums, at = [], 0
    for grad in bias_grads:
        bias_sums.append(own_part(together[at : at + grad.shape[0]]))
        at += grad.shape[0]
    return (
        frames_out,
        grad_frames,
        grad_condition,
        grad_spatial_in_sum,
        bias_sums[0],
        grad_spatial_out_sum,
        bias_sums[1],
        grad_temporal_in_sum,
        bias_sums[2],
        grad_temporal_out_sum,
        bias_sums[3],
        grad_expand_sum,
        bias_sums[4],
        grad_shrink_sum,
        bias_sums[5],
        grad_modulate_weight,
        grad_modulate_bias,
    )


def solution(mesh):
    in_specs = (
        P(("dp", "frame"), None, None),
        P(("dp", "frame"), None),
        P("dp", None),
        P("frame", None),
        P("frame"),
        P("frame", None),
        P("frame"),
        P("frame", None),
        P("frame"),
        P("frame", None),
        P("frame"),
        P("frame", None),
        P("frame"),
        P("frame", None),
        P("frame"),
        P("frame", None),
        P("frame"),
        P(("dp", "frame"), None, None),
    )
    out_specs = (
        P(("dp", "frame"), None, None),
        P(("dp", "frame"), None, None),
        P(("dp", "frame"), None),
        P("frame", None),
        P("frame"),
        P("frame", None),
        P("frame"),
        P("frame", None),
        P("frame"),
        P("frame", None),
        P("frame"),
        P("frame", None),
        P("frame"),
        P("frame", None),
        P("frame"),
        P("frame", None),
        P("frame"),
    )
    return jax.shard_map(
        per_device, mesh=mesh, in_specs=in_specs, out_specs=out_specs, check_vma=False
    )
```

```python
import functools

import jax
import jax.numpy as jnp
from jax import lax
from jax.experimental import pallas as pl
from jax.experimental.pallas import tpu as pltpu
from jax.sharding import PartitionSpec as P


HEADS = 12
HEAD_DIM = 64
WINDOW = 2

F32 = jnp.float32
BF16 = jnp.bfloat16
SCALE = HEAD_DIM ** (-0.5)
SPAN = 2 * WINDOW + 1


def mm(a, b):
    return lax.dot_general(a, b, (((1,), (0,)), ((), ())), preferred_element_type=F32)


def mm_nt(a, b):
    return lax.dot_general(a, b, (((1,), (1,)), ((), ())), preferred_element_type=F32)


def mm_tn(a, b):
    return lax.dot_general(a, b, (((0,), (0,)), ((), ())), preferred_element_type=F32)


def unit(x):
    centred = x - jnp.mean(x, axis=-1, keepdims=True)
    inv = lax.rsqrt(jnp.mean(centred * centred, axis=-1, keepdims=True) + 1e-06)
    return centred * inv, inv


def unit_back(dn, xhat, inv, scale):
    e = dn * (1.0 + scale)
    first = jnp.mean(e, axis=-1, keepdims=True)
    second = jnp.mean(e * xhat, axis=-1, keepdims=True)
    return inv * (e - first - xhat * second)


def down(x):
    return jnp.sum(x, axis=0, keepdims=True)


def low_half(rows):
    return lax.broadcasted_iota(jnp.int32, (rows, 2 * HEAD_DIM), 1) < HEAD_DIM


def soft(scores):
    e = jnp.exp(scores - jnp.max(scores, axis=-1, keepdims=True))
    return e / jnp.sum(e, axis=-1, keepdims=True)


def params(flops, nbytes, trans=0):
    return dict(
        compiler_params=pltpu.CompilerParams(vmem_limit_bytes=60 * 2**20),
        cost_estimate=pl.CostEstimate(
            flops=int(flops), bytes_accessed=int(nbytes), transcendentals=int(trans)
        ),
    )


def fixed(shape):
    return pl.BlockSpec(shape, lambda *_: (0,) * len(shape), pipeline_mode=pl.Buffered(1))


def per_first(shape):
    return pl.BlockSpec((1,) + shape, lambda i: (i,) + (0,) * len(shape))


def per_second(lead, tile, width):
    return pl.BlockSpec((lead, tile, width), lambda i: (0, i, 0))


def spatial_kernel(x_ref, mod_ref, wsi, bsi, n1_ref, qkv1_ref, attn_ref):
    x = x_ref[0].astype(F32)
    width = x.shape[1]
    xhat, _ = unit(x)
    n1 = (xhat * (1.0 + mod_ref[0, 1:2]) + mod_ref[0, 0:1]).astype(BF16)
    n1_ref[0] = n1
    qkv1_ref[0] = (mm(n1, wsi[...]) + bsi[...]).astype(BF16)
    half = low_half(x.shape[0])
    for pair in range(width // (2 * HEAD_DIM)):
        at = pair * 2 * HEAD_DIM
        q = qkv1_ref[0, :, at : at + 2 * HEAD_DIM]
        k = qkv1_ref[0, :, width + at : width + at + 2 * HEAD_DIM]
        v = qkv1_ref[0, :, 2 * width + at : 2 * width + at + 2 * HEAD_DIM]
        zero = jnp.zeros_like(q)
        first = soft(mm_nt(jnp.where(half, q, zero), k) * SCALE).astype(BF16)
        second = soft(mm_nt(jnp.where(half, zero, q), k) * SCALE).astype(BF16)
        out = jnp.where(half, mm(first, v), mm(second, v))
        attn_ref[0, :, at : at + 2 * HEAD_DIM] = out.astype(BF16)


def spatial_forward(x, mod, wsi, bsi):
    frames, patches, width = x.shape
    block = lambda n: per_first((patches, n))
    outs = [width, 3 * width, width]
    tokens = frames * patches
    return pl.pallas_call(
        spatial_kernel,
        grid=(frames,),
        in_specs=[block(width), per_first(mod.shape[1:]), fixed(wsi.shape), fixed(bsi.shape)],
        out_specs=[block(n) for n in outs],
        out_shape=[jax.ShapeDtypeStruct((frames, patches, n), BF16) for n in outs],
        name="spatial_forward",
        **params(2 * tokens * width * (3 * width + 4 * patches), 12e6, tokens * patches * HEADS),
    )(x, mod, wsi, bsi)


def project_kernel(x_ref, attn_ref, mod_ref, wso, bso, branch_ref, after_ref, n2_ref):
    branch = mm(attn_ref[0], wso[...]) + bso[...]
    branch_ref[0] = branch
    after = x_ref[0].astype(F32) + mod_ref[0, 2:3] * branch
    after_ref[0] = after
    xhat, _ = unit(after)
    n2_ref[0] = (xhat * (1.0 + mod_ref[0, 4:5]) + mod_ref[0, 3:4]).astype(BF16)


def project_forward(x, attn, mod, wso, bso):
    frames, patches, width = x.shape
    block = per_first((patches, width))
    tokens = frames * patches
    return pl.pallas_call(
        project_kernel,
        grid=(frames,),
        in_specs=[block, block, per_first(mod.shape[1:]), fixed(wso.shape), fixed(bso.shape)],
        out_specs=[block] * 3,
        out_shape=[jax.ShapeDtypeStruct(x.shape, t) for t in (F32, F32, BF16)],
        name="project_forward",
        **params(2 * tokens * width * width, 13e6),
    )(x, attn, mod, wso, bso)


def split_store(hi_ref, lo_ref, row, prod):
    hi = prod.astype(BF16)
    hi_ref[row] = hi
    lo_ref[row] = (prod - hi.astype(F32)).astype(BF16)


def ext_rows(e, frames, left, own, right, base, width):
    if e < WINDOW:
        return left[e, :, base - width : base]
    if e < WINDOW + frames:
        return own[e - WINDOW, :, base : base + width]
    return right[e - WINDOW - frames, :, base - width : base]


def head_sums(hi_ref, lo_ref, first, count, ones):
    tile, width = hi_ref.shape[1:]
    hi = hi_ref[first : first + count].reshape(count * tile, width)
    lo = lo_ref[first : first + count].reshape(count * tile, width)
    return mm(hi, ones) + mm(lo, ones)


def temporal_kernel(
    allowed, qkv_ref, nl_ref, nr_ref, after_ref, mod_ref, wti, bti, wto, bto, ones, ones_t,
    probs_ref, attn_ref, branch_ref, out_ref, left_ref, right_ref, hi_ref, lo_ref,
):
    frames, tile, width = after_ref.shape
    for near, kv_ref in ((nl_ref, left_ref), (nr_ref, right_ref)):
        kv = mm(near[...].reshape(WINDOW * tile, width), wti[:, width:]) + bti[:, width:]
        kv_ref[...] = kv.astype(BF16).reshape(WINDOW, tile, 2 * width)
    for t in range(frames):
        q = qkv_ref[t, :, :width].astype(F32)
        for o in range(SPAN):
            k = ext_rows(t + o, frames, left_ref, qkv_ref, right_ref, width, width)
            split_store(hi_ref, lo_ref, t * SPAN + o, q * k.astype(F32))
    for t in range(frames):
        raw = head_sums(hi_ref, lo_ref, t * SPAN, SPAN, ones[...]) * SCALE
        raw = [
            jnp.where(allowed[o, t] > 0, raw[o * tile : (o + 1) * tile], -1e30)
            for o in range(SPAN)
        ]
        top = raw[0]
        for o in range(1, SPAN):
            top = jnp.maximum(top, raw[o])
        expo = [jnp.exp(r - top) for r in raw]
        total = expo[0]
        for o in range(1, SPAN):
            total = total + expo[o]
        inv = 1.0 / total
        probs = [e * inv for e in expo]
        for o in range(SPAN):
            probs_ref[t, o] = probs[o]
        wide = mm(jnp.concatenate(probs, axis=0).astype(BF16), ones_t[...])
        total = None
        for o in range(SPAN):
            v = ext_rows(t + o, frames, left_ref, qkv_ref, right_ref, 2 * width, width)
            term = wide[o * tile : (o + 1) * tile] * v.astype(F32)
            total = term if total is None else total + term
        attn_ref[t] = total.astype(BF16)
    branch = mm(attn_ref[...].reshape(frames * tile, width), wto[...]) + bto[...]
    for t in range(frames):
        part = branch[t * tile : (t + 1) * tile]
        branch_ref[t] = part
        out_ref[t] = after_ref[t] + mod_ref[t, 5:6] * part


def head_ones(width):
    head = jnp.arange(width, dtype=jnp.int32)[:, None] // HEAD_DIM
    return (head == jnp.arange(128, dtype=jnp.int32)[None, :]).astype(BF16)


def temporal_forward(allowed, qkv, near_left, near_right, after, mod, wti, bti, wto, bto):
    frames, patches, width = after.shape
    tile = 64
    ones = head_ones(width)
    spec = lambda n: per_second(frames, tile, n)
    halo = per_second(WINDOW, tile, 2 * width)
    near = per_second(WINDOW, tile, width)
    shape = lambda t: jax.ShapeDtypeStruct((frames, patches, width), t)
    tokens = frames * patches
    return pl.pallas_call(
        temporal_kernel,
        grid=(patches // tile,),
        in_specs=[
            pl.BlockSpec(memory_space=pltpu.SMEM),
            spec(3 * width), near, near, spec(width), fixed(mod.shape),
            fixed(wti.shape), fixed(bti.shape), fixed(wto.shape), fixed(bto.shape),
            fixed(ones.shape), fixed(ones.shape[::-1]),
        ],
        out_specs=[
            pl.BlockSpec((frames, SPAN, tile, 128), lambda i: (0, 0, i, 0)),
            spec(width), spec(width), spec(width), halo, halo,
        ],
        out_shape=[
            jax.ShapeDtypeStruct((frames, SPAN, patches, 128), F32),
            shape(BF16), shape(F32), shape(F32),
            jax.ShapeDtypeStruct((WINDOW, patches, 2 * width), BF16),
            jax.ShapeDtypeStruct((WINDOW, patches, 2 * width), BF16),
        ],
        scratch_shapes=[pltpu.VMEM((frames * SPAN, tile, width), BF16)] * 2,
        name="temporal_forward",
        **params(2 * tokens * width * (width + SPAN * 400), 22e6, tokens * SPAN * 128),
    )(allowed, qkv, near_left, near_right, after, mod, wti, bti, wto, bto, ones, ones.T)


def feed_kernel(
    after_ref, cot_ref, mod_ref, w1, b1, w2, b2,
    out_ref, g_ref, n_ref, act_ref, dpre_ref, db_ref, dmod_ref, sum1_ref, sum2_ref,
):
    after = after_ref[0]
    width = after.shape[1]
    hidden = w1.shape[1]
    xhat, inv = unit(after)
    scale = mod_ref[0, 7:8]
    gate = mod_ref[0, 8:9]
    n = (xhat * (1.0 + scale) + mod_ref[0, 6:7]).astype(BF16)
    n_ref[0] = n
    g3 = cot_ref[0].astype(F32)
    db = (gate * g3).astype(BF16)
    db_ref[0] = db

    @pl.when(pl.program_id(0) == 0)
    def _():
        sum1_ref[...] = jnp.zeros_like(sum1_ref)
        sum2_ref[...] = jnp.zeros_like(sum2_ref)

    sum2_ref[...] += down(db.astype(F32))
    branch = jnp.zeros_like(after)
    dn = jnp.zeros_like(after)
    chunk = width
    for c in range(hidden // chunk):
        cols = slice(c * chunk, (c + 1) * chunk)
        pre = mm(n, w1[:, cols]) + b1[:, cols]
        dact = mm_nt(db, w2[cols, :])
        phi = 0.5 * (1.0 + lax.erf(pre * 0.7071067811865476))
        act = (pre * phi).astype(BF16)
        slope = phi + pre * (jnp.exp(-0.5 * pre * pre) * 0.3989422804014327)
        dpre = (dact * slope).astype(BF16)
        act_ref[0, :, cols] = act
        dpre_ref[0, :, cols] = dpre
        sum1_ref[:, cols] += down(dpre.astype(F32))
        branch += mm(act, w2[cols, :])
        dn += mm_nt(dpre, w1[:, cols])
    branch = branch + b2[...]
    out_ref[0] = (after + gate * branch).astype(BF16)
    dmod_ref[0, 0:1] = down(dn)
    dmod_ref[0, 1:2] = down(dn * xhat)
    dmod_ref[0, 2:3] = down(g3 * branch)
    g_ref[0] = g3 + unit_back(dn, xhat, inv, scale)


def feed_forward(after, cot, mod, w1, b1, w2, b2):
    frames, patches, width = after.shape
    hidden = w1.shape[1]
    shape = lambda n, t: jax.ShapeDtypeStruct((frames, patches, n), t)
    block = lambda n: per_first((patches, n))
    outs = [(width, BF16), (width, F32), (width, BF16), (hidden, BF16), (hidden, BF16), (width, BF16)]
    tokens = frames * patches
    return pl.pallas_call(
        feed_kernel,
        grid=(frames,),
        in_specs=[block(width), block(width), per_first(mod.shape[1:])]
        + [fixed(w.shape) for w in (w1, b1, w2, b2)],
        out_specs=[block(n) for n, _ in outs]
        + [per_first((3, width)), pl.BlockSpec((1, hidden), lambda i: (0, 0)),
           pl.BlockSpec((1, width), lambda i: (0, 0))],
        out_shape=[shape(n, t) for n, t in outs]
        + [jax.ShapeDtypeStruct((frames, 3, width), F32),
           jax.ShapeDtypeStruct((1, hidden), F32), jax.ShapeDtypeStruct((1, width), F32)],
        name="feed_forward",
        **params(8 * tokens * width * hidden, 32e6, 2 * tokens * hidden),
    )(after, cot, mod, w1, b1, w2, b2)


def temporal_back_kernel(
    g_ref, branch_ref, mod_ref, wto, wti, qkv_ref, left_ref, right_ref, probs_ref, ones, ones_t,
    db_ref, dqkv_ref, dleft_ref, dright_ref, nleft_ref, nright_ref, dgate_ref, sum_ref, sumq_ref,
    hi_ref, lo_ref, da_ref, ds_ref, pw_ref,
):
    frames, tile, width = g_ref.shape

    @pl.when(pl.program_id(0) == 0)
    def _():
        dgate_ref[...] = jnp.zeros_like(dgate_ref)
        sum_ref[...] = jnp.zeros_like(sum_ref)
        sumq_ref[...] = jnp.zeros_like(sumq_ref)

    for t in range(frames):
        g = g_ref[t]
        dgate_ref[t : t + 1] += down(g * branch_ref[t])
        db = (mod_ref[t, 5:6] * g).astype(BF16)
        db_ref[t] = db
        sum_ref[...] += down(db.astype(F32))
    da_all = mm_nt(db_ref[...].reshape(frames * tile, width), wto[...]).astype(BF16)
    da_ref[...] = da_all.reshape(frames, tile, width)
    for t in range(frames):
        da = da_ref[t].astype(F32)
        for o in range(SPAN):
            v = ext_rows(t + o, frames, left_ref, qkv_ref, right_ref, 2 * width, width)
            split_store(hi_ref, lo_ref, t * SPAN + o, da * v.astype(F32))
    for t in range(frames):
        dp = head_sums(hi_ref, lo_ref, t * SPAN, SPAN, ones[...])
        probs = probs_ref[t].reshape(SPAN * tile, 128)
        both = probs * dp
        dot = both[:tile]
        for o in range(1, SPAN):
            dot = dot + both[o * tile : (o + 1) * tile]
        ds = both - probs * jnp.concatenate([dot] * SPAN, axis=0)
        wide = mm(ds.astype(BF16), ones_t[...]).astype(BF16)
        ds_ref[t * SPAN : (t + 1) * SPAN] = wide.reshape(SPAN, tile, width)
        wide = mm(probs.astype(BF16), ones_t[...]).astype(BF16)
        pw_ref[t * SPAN : (t + 1) * SPAN] = wide.reshape(SPAN, tile, width)
    for t in range(frames):
        total = None
        for o in range(SPAN):
            k = ext_rows(t + o, frames, left_ref, qkv_ref, right_ref, width, width)
            term = ds_ref[t * SPAN + o].astype(F32) * k.astype(F32)
            total = term if total is None else total + term
        dqkv_ref[t, :, :width] = (total * SCALE).astype(BF16)
    for e in range(frames + 2 * WINDOW):
        dk = dv = None
        for t in range(max(0, e - SPAN + 1), min(frames, e + 1)):
            row = t * SPAN + e - t
            q = qkv_ref[t, :, :width].astype(F32)
            term = ds_ref[row].astype(F32) * q
            dk = term if dk is None else dk + term
            term = pw_ref[row].astype(F32) * da_ref[t].astype(F32)
            dv = term if dv is None else dv + term
        dk = (dk * SCALE).astype(BF16)
        dv = dv.astype(BF16)
        if e < WINDOW:
            dleft_ref[e, :, :width] = dk
            dleft_ref[e, :, width:] = dv
        elif e < WINDOW + frames:
            dqkv_ref[e - WINDOW, :, width : 2 * width] = dk
            dqkv_ref[e - WINDOW, :, 2 * width :] = dv
        else:
            dright_ref[e - WINDOW - frames, :, :width] = dk
            dright_ref[e - WINDOW - frames, :, width:] = dv
    for dkv_ref, near_ref in ((dleft_ref, nleft_ref), (dright_ref, nright_ref)):
        flat = dkv_ref[...].reshape(WINDOW * tile, 2 * width)
        sumq_ref[:, width:] += down(flat.astype(F32))
        near_ref[...] = mm_nt(flat, wti[:, width:]).astype(BF16).reshape(WINDOW, tile, width)
    sumq_ref[...] += down(dqkv_ref[...].reshape(frames * tile, 3 * width).astype(F32))


def temporal_backward(g, branch, mod, wto, wti, qkv, left, right, probs):
    frames, patches, width = g.shape
    tile = 64
    ones = head_ones(width)
    spec = lambda n: per_second(frames, tile, n)
    halo = per_second(WINDOW, tile, 2 * width)
    near = per_second(WINDOW, tile, width)
    shape = lambda f, n, t: jax.ShapeDtypeStruct((f, patches, n), t)
    tokens = frames * patches
    return pl.pallas_call(
        temporal_back_kernel,
        grid=(patches // tile,),
        in_specs=[
            spec(width), spec(width), fixed(mod.shape), fixed(wto.shape), fixed(wti.shape),
            spec(3 * width), halo, halo,
            pl.BlockSpec((frames, SPAN, tile, 128), lambda i: (0, 0, i, 0)),
            fixed(ones.shape), fixed(ones.shape[::-1]),
        ],
        out_specs=[
            spec(width), spec(3 * width), halo, halo, near, near,
            pl.BlockSpec((frames, width), lambda i: (0, 0)),
            pl.BlockSpec((1, width), lambda i: (0, 0)),
            pl.BlockSpec((1, 3 * width), lambda i: (0, 0)),
        ],
        out_shape=[
            shape(frames, width, BF16), shape(frames, 3 * width, BF16),
            shape(WINDOW, 2 * width, BF16), shape(WINDOW, 2 * width, BF16),
            shape(WINDOW, width, BF16), shape(WINDOW, width, BF16),
            jax.ShapeDtypeStruct((frames, width), F32), jax.ShapeDtypeStruct((1, width), F32),
            jax.ShapeDtypeStruct((1, 3 * width), F32),
        ],
        scratch_shapes=[pltpu.VMEM((frames * SPAN, tile, width), BF16)] * 2
        + [pltpu.VMEM((frames, tile, width), BF16)]
        + [pltpu.VMEM((frames * SPAN, tile, width), BF16)] * 2,
        name="temporal_backward",
        **params(2 * tokens * width * (width + SPAN * 500), 36e6),
    )(g, branch, mod, wto, wti, qkv, left, right, probs, ones, ones.T)


def project_back_kernel(
    dn_ref, fl_ref, fr_ref, after_ref, g2_ref, branch_ref, mod_ref, wso,
    g_ref, db_ref, da_ref, dmod_ref, sum_ref,
):
    at = pl.program_id(0)

    @pl.when(at == 0)
    def _():
        sum_ref[...] = jnp.zeros_like(sum_ref)

    dn = dn_ref[0] + jnp.where(at < WINDOW, fl_ref[0].astype(F32), fr_ref[0].astype(F32))
    xhat, inv = unit(after_ref[0])
    dmod_ref[0, 1:2] = down(dn)
    dmod_ref[0, 2:3] = down(dn * xhat)
    g1 = g2_ref[0] + unit_back(dn, xhat, inv, mod_ref[0, 4:5])
    dmod_ref[0, 0:1] = down(g1 * branch_ref[0])
    g_ref[0] = g1
    db = (mod_ref[0, 2:3] * g1).astype(BF16)
    db_ref[0] = db
    sum_ref[...] += down(db.astype(F32))
    da_ref[0] = mm_nt(db, wso[...]).astype(BF16)


def project_backward(dn2, from_left, from_right, after, g2, branch, mod, wso):
    frames, patches, width = after.shape
    block = per_first((patches, width))
    tokens = frames * patches
    return pl.pallas_call(
        project_back_kernel,
        grid=(frames,),
        in_specs=[
            block,
            pl.BlockSpec((1, patches, width), lambda i: (jnp.minimum(i, WINDOW - 1), 0, 0)),
            pl.BlockSpec((1, patches, width), lambda i: (jnp.maximum(i - WINDOW, 0), 0, 0)),
            block, block, block, per_first(mod.shape[1:]), fixed(wso.shape),
        ],
        out_specs=[block, block, block, per_first((3, width)),
                   pl.BlockSpec((1, width), lambda i: (0, 0))],
        out_shape=[jax.ShapeDtypeStruct(after.shape, t) for t in (F32, BF16, BF16)]
        + [jax.ShapeDtypeStruct((frames, 3, width), F32), jax.ShapeDtypeStruct((1, width), F32)],
        name="project_backward",
        **params(2 * tokens * width * width, 22e6),
    )(dn2, from_left, from_right, after, g2, branch, mod, wso)


def heads_back(q_ref, k_ref, v_ref, da_ref, out_ref, sum_ref):
    tokens, width = q_ref.shape[1:]

    @pl.when(pl.program_id(0) == 0)
    def _():
        sum_ref[...] = jnp.zeros_like(sum_ref)

    half = low_half(tokens)
    for pair in range(width // (2 * HEAD_DIM)):
        cols = slice(pair * 2 * HEAD_DIM, (pair + 1) * 2 * HEAD_DIM)
        q, k, v, da = (ref[0, :, cols] for ref in (q_ref, k_ref, v_ref, da_ref))
        zero = jnp.zeros_like(q)
        parts = []
        for side in range(2):
            pick = (lambda u: jnp.where(half, u, zero)) if side == 0 else (
                lambda u: jnp.where(half, zero, u))
            probs = soft(mm_nt(pick(q), k) * SCALE)
            dp = mm_nt(pick(da), v)
            both = probs * dp
            ds = (both - probs * jnp.sum(both, axis=-1, keepdims=True)).astype(BF16)
            parts.append((mm(ds, k), mm_tn(ds, q), mm_tn(probs.astype(BF16), da)))
        grads = [jnp.where(half, a, b) for a, b in zip(*parts)]
        for at, grad in enumerate((grads[0] * SCALE, grads[1] * SCALE, grads[2])):
            out_ref[0, :, at * width + cols.start : at * width + cols.stop] = grad.astype(BF16)
    sum_ref[...] += down(out_ref[0].astype(F32))


def first_heads_kernel(q_ref, k_ref, v_ref, da_ref, out_ref, sum_ref):
    heads_back(q_ref, k_ref, v_ref, da_ref, out_ref, sum_ref)


def last_heads_kernel(
    q_ref, k_ref, v_ref, da_ref, first_ref, g_ref, x_ref, mod_ref, wsi,
    out_ref, sum_ref, grad_ref, dmod_ref,
):
    heads_back(q_ref, k_ref, v_ref, da_ref, out_ref, sum_ref)
    width = q_ref.shape[2]
    dn = None
    for at in range(3):
        for side, ref in enumerate((first_ref, out_ref)):
            cols = slice((2 * at + side) * width, (2 * at + side + 1) * width)
            term = mm_nt(ref[0, :, at * width : (at + 1) * width], wsi[:, cols])
            dn = term if dn is None else dn + term
    xhat, inv = unit(x_ref[0].astype(F32))
    dmod_ref[0, 0:1] = down(dn)
    dmod_ref[0, 1:2] = down(dn * xhat)
    grad_ref[0] = g_ref[0] + unit_back(dn, xhat, inv, mod_ref[0, 1:2])


def heads_backward(qkv1, da1, side, rest=None):
    frames, patches, width = da1.shape
    part = width // 2
    column = lambda at: pl.BlockSpec((1, patches, part), lambda i: (i, 0, at))
    block = lambda n: per_first((patches, n))
    tokens = frames * patches
    in_specs = [column(side), column(2 + side), column(4 + side), column(side)]
    operands = [qkv1, qkv1, qkv1, da1]
    out_specs = [block(3 * part), pl.BlockSpec((1, 3 * part), lambda i: (0, 0))]
    out_shape = [
        jax.ShapeDtypeStruct((frames, patches, 3 * part), BF16),
        jax.ShapeDtypeStruct((1, 3 * part), F32),
    ]
    if rest is not None:
        first, g1, x, mod, wsi = rest
        in_specs += [block(3 * part), block(width), block(width), per_first(mod.shape[1:]),
                     fixed(wsi.shape)]
        operands += [first, g1, x, mod, wsi]
        out_specs += [block(width), per_first((2, width))]
        out_shape += [
            jax.ShapeDtypeStruct((frames, patches, width), F32),
            jax.ShapeDtypeStruct((frames, 2, width), F32),
        ]
    return pl.pallas_call(
        first_heads_kernel if rest is None else last_heads_kernel,
        grid=(frames,),
        in_specs=in_specs,
        out_specs=out_specs,
        out_shape=out_shape,
        name="first_heads_backward" if rest is None else "last_heads_backward",
        **params(2 * tokens * width * (5 * patches + (0 if rest is None else 3 * width)),
                 16e6, tokens * patches * HEADS // 2),
    )(*operands)


def outer_kernel(*refs, jobs, order):
    out_ref = refs[-1]
    parts = out_ref.shape[1]
    groups = len(order)
    top = 0
    turned = {}
    for terms in jobs:
        total = None
        for left, right in terms:
            if left not in turned:
                turned[left] = refs[left][...].T
            term = mm(turned[left], refs[right][...])
            total = term if total is None else total + term
        rows = total.shape[0] // (groups * parts)
        width = out_ref.shape[3]
        for tile in range(total.shape[1] // width):
            for f in range(parts):
                for d in range(groups):
                    row = (f * groups + d) * rows
                    out_ref[order[d], f, top : top + rows] = total[
                        row : row + rows, tile * width : (tile + 1) * width
                    ].astype(BF16)
            top += rows


def outer_pieces(jobs, width, groups, parts, order, total_rows=None, into=None):
    shaped = {}

    def flat(a):
        return shaped.setdefault(id(a), a.reshape(-1, a.shape[-1]))

    jobs = [[(flat(left), flat(right), *tiles) for left, right, *tiles in job] for job in jobs]
    depth = jobs[0][0][0].shape[1]
    rows = depth // (groups * parts)
    height = sum(job[0][3] for job in jobs) * rows
    total_rows = total_rows or height
    if rows % 8:
        pieces = [] if into is None else [into[:, :, : total_rows - height]]
        for job in jobs:
            for tile in range(job[0][3]):
                cut = lambda r, t: r[:, (t + tile) * width : (t + tile + 1) * width]
                total = sum(mm_tn(l, cut(r, t)) for l, r, t, _ in job)
                total = total.astype(BF16).reshape(parts, groups, rows, width).swapaxes(0, 1)
                pieces.append(jnp.stack([total[order.index(d)] for d in range(groups)]))
        whole = jnp.concatenate(pieces, axis=2)
        return jnp.pad(whole, ((0, 0), (0, 0), (0, total_rows - whole.shape[2]), (0, 0)))
    step = 1
    while (step * depth // parts) % 128:
        step *= 2
    specs, operands, flops, known, terms = [], [], 0, {}, []

    def operand(array, spec, key):
        if key not in known:
            known[key] = len(operands)
            operands.append(array)
            specs.append(spec)
        return known[key]

    for job in jobs:
        pairs = []
        for left, right, tile, tiles in job:
            tokens = left.shape[0]
            spec = pl.BlockSpec((tokens, step * depth // parts), lambda i: (0, i))
            first = operand(left, spec, (id(left), None))
            spec = pl.BlockSpec(
                (tokens, tiles * width),
                lambda i, at=tile // tiles: (0, at),
                pipeline_mode=pl.Buffered(1),
            )
            pairs.append((first, operand(right, spec, (id(right), tile, tiles))))
            flops += 2 * tokens * depth * width * tiles
        terms.append(tuple(pairs))
    place = 0
    aliases = {}
    if into is not None:
        place = total_rows // height - 1
        aliases = {len(operands): 0}
        specs.append(pl.BlockSpec(memory_space=pl.ANY))
        operands.append(into)
    return pl.pallas_call(
        functools.partial(outer_kernel, jobs=tuple(terms), order=tuple(order)),
        grid=(parts // step,),
        in_specs=specs,
        out_specs=pl.BlockSpec((groups, step, height, width), lambda i: (0, i, place, 0)),
        out_shape=jax.ShapeDtypeStruct((groups, parts, total_rows, width), BF16),
        input_output_aliases=aliases,
        name="outer_pieces",
        **params(flops, 12e6),
    )(*operands)


def own_part(vector):
    size = vector.shape[0] // lax.axis_size("frame")
    return lax.dynamic_slice_in_dim(vector, lax.axis_index("frame") * size, size)


def stacked(block, width):
    count = block.shape[-1] // width
    return jnp.concatenate(
        [block[..., k * width : (k + 1) * width] for k in range(count)], axis=-2
    )


def unstacked(block, count):
    rows = block.shape[-2] // count
    return jnp.concatenate(
        [block[..., k * rows : (k + 1) * rows, :] for k in range(count)], axis=-1
    )


def line_gathered(mine):
    parts = lax.axis_size("frame")
    copies = jnp.broadcast_to(mine[None], (parts,) + mine.shape)
    return lax.all_to_all(copies, "frame", split_axis=0, concat_axis=0)


def line_swapped(pieces):
    parts = lax.axis_size("frame")
    place = lax.axis_index("frame")
    pick = lambda at: lax.dynamic_index_in_dim(pieces, (place + at) % parts, keepdims=False)
    seen = [pick(0)]
    for far in range(1, parts):
        pairs = [(i, (i + far) % parts) for i in range(parts)]
        seen.append(lax.ppermute(pick(far), "frame", pairs))
    seen = jnp.stack(seen)
    return jnp.stack(
        [
            lax.dynamic_index_in_dim(seen, (place - source) % parts, keepdims=False)
            for source in range(parts)
        ]
    )


def line_rotated(mine):
    parts = lax.axis_size("frame")
    place = lax.axis_index("frame")
    seen = [mine]
    for far in range(1, parts):
        seen.append(lax.ppermute(mine, "frame", [(i, (i + far) % parts) for i in range(parts)]))
    seen = jnp.stack(seen)
    return jnp.stack(
        [
            lax.dynamic_index_in_dim(seen, (place - source) % parts, keepdims=False)
            for source in range(parts)
        ]
    )


def packed(shards):
    groups = lax.axis_size("dp")
    width = min(shard.shape[1] for shard in shards)
    pieces = []
    for shard in shards:
        rows = shard.shape[0] // groups
        piece = lax.dynamic_slice_in_dim(shard, lax.axis_index("dp") * rows, rows)
        pieces.append(stacked(piece, width))
    return jnp.concatenate(pieces, axis=0)


def unpacked(whole, shards):
    groups, parts = lax.axis_size("dp"), lax.axis_size("frame")
    width = whole.shape[-1]
    results, at = [], 0
    for shard in shards:
        stacks = shard.shape[1] // width
        height = stacks * shard.shape[0] // groups
        part = unstacked(whole[:, :, at : at + height], stacks)
        results.append(jnp.swapaxes(part, 0, 1).reshape(parts * shard.shape[0], shard.shape[1]))
        at += height
    return results


def gathered_small(biases, condition):
    parts = lax.axis_size("frame")
    flat = jnp.concatenate(biases + [condition.reshape(-1)])
    rows = line_gathered(flat)
    results, at = [], 0
    for bias in biases:
        results.append(rows[:, at : at + bias.shape[0]].reshape(-1))
        at += bias.shape[0]
    results.append(rows[:, at:].reshape(parts * condition.shape[0], condition.shape[1]))
    return results


def modulated(act_group, matrix, frames):
    parts = lax.axis_size("frame")
    rows, width = matrix.shape
    columns = lax.dynamic_slice_in_dim(act_group, lax.axis_index("frame") * rows, rows, axis=1)
    return mm(columns, matrix).reshape(parts, frames, width)


def passed_along(x, axis, by):
    peers = lax.axis_size(axis)
    pairs = [(i, i + by) for i in range(peers) if 0 <= i + by < peers]
    return lax.ppermute(x, axis, pairs)


def own_bit(bit):
    return (lax.axis_index("dp") >> bit) & 1


def swapped(x, bit):
    return lax.ppermute(x, "dp", [(i, i ^ (1 << bit)) for i in range(lax.axis_size("dp"))])


def added(a, b):
    return (a.astype(F32) + b.astype(F32)).astype(BF16)


def halved(blocks, bit):
    half = blocks.shape[0] // 2
    mine = own_bit(bit)
    sent = lax.dynamic_slice_in_dim(blocks, (1 - mine) * half, half)
    kept = lax.dynamic_slice_in_dim(blocks, mine * half, half)
    return added(kept, swapped(sent, bit))


def summed(pieces):
    return jnp.sum(pieces.astype(F32), axis=0).astype(BF16)


def core_order():
    groups = lax.axis_size("dp")
    return [(d & 1) * (groups // 2) + (d >> 1) for d in range(groups)]


def plane_summed(blocks):
    groups = lax.axis_size("dp")
    same = [list(range(core, groups, 2)) for core in range(2)]
    return summed(
        lax.all_to_all(blocks, "dp", split_axis=0, concat_axis=0, axis_index_groups=same)
    )


def dp_summed_start(blocks):
    return lax.all_to_all(blocks, "dp", split_axis=0, concat_axis=0)


def line_summed(blocks):
    return summed(lax.all_to_all(blocks, "frame", split_axis=0, concat_axis=0))


def plane_gathered(piece):
    groups = lax.axis_size("dp")
    copies = jnp.broadcast_to(piece[None], (groups,) + piece.shape)
    return lax.all_to_all(copies, "dp", split_axis=0, concat_axis=0)


def per_device(
    frames_in,
    condition,
    segments,
    spatial_in,
    spatial_in_bias,
    spatial_out,
    spatial_out_bias,
    temporal_in,
    temporal_in_bias,
    temporal_out,
    temporal_out_bias,
    expand_weight,
    expand_bias,
    shrink_weight,
    shrink_bias,
    modulate_weight,
    modulate_bias,
    cotangent,
):
    groups, parts = lax.axis_size("dp"), lax.axis_size("frame")
    place = lax.axis_index("frame")
    frames, patches, width = frames_in.shape
    space, time = [spatial_in, spatial_out], [temporal_in, temporal_out]
    dense = [expand_weight, shrink_weight]
    biases = [
        spatial_in_bias,
        spatial_out_bias,
        temporal_in_bias,
        temporal_out_bias,
        expand_bias,
        shrink_bias,
        modulate_bias,
    ]
    space_column = line_gathered(packed(space))
    condition_held, space_column = lax.optimization_barrier((condition, space_column))
    *full_biases, cond_group = gathered_small(biases, condition_held)
    full_spatial_in, full_spatial_out = unpacked(lax.all_gather(space_column, "dp", axis=0), space)
    sinb, soutb, tinb, toutb, expb, shrb, modb = [b.astype(F32)[None, :] for b in full_biases]
    act_group = jax.nn.silu(cond_group.astype(F32)).astype(BF16)
    partial = modulated(act_group, modulate_weight, frames)
    partial = lax.all_to_all(partial, "frame", split_axis=0, concat_axis=0)
    time_piece, partial = lax.optimization_barrier((packed(time), partial))
    mod = (jnp.sum(partial, axis=0) + modb).reshape(frames, 9, width)
    time_column = line_gathered(time_piece)
    full_temporal_in, full_temporal_out = unpacked(lax.all_gather(time_column, "dp", axis=0), time)
    dense_piece, time_column, mod = lax.optimization_barrier((packed(dense), time_column, mod))
    dense_column = line_rotated(dense_piece)
    full_expand, full_shrink = unpacked(lax.all_gather(dense_column, "dp", axis=0), dense)
    n1, qkv1, attn1 = spatial_forward(frames_in, mod, full_spatial_in, sinb)
    branch1, after1, n2 = project_forward(frames_in, attn1, mod, full_spatial_out, soutb)
    near_left = passed_along(n2[frames - WINDOW :], "frame", 1)
    near_right = passed_along(n2[:WINDOW], "frame", -1)
    qkv2 = (mm(n2.reshape(-1, width), full_temporal_in) + tinb).astype(BF16)
    qkv2 = qkv2.reshape(frames, patches, 3 * width)
    seg_row = segments[0]
    seg_pad = jnp.pad(seg_row, (WINDOW, WINDOW), constant_values=-1)
    nearby = lax.dynamic_slice_in_dim(seg_pad, place * frames, frames + 2 * WINDOW)
    own_seg = nearby[WINDOW : WINDOW + frames]
    allowed = jnp.stack([nearby[o : o + frames] == own_seg for o in range(SPAN)]).astype(jnp.int32)
    probs, attn2, branch2, after2, left, right = temporal_forward(
        allowed, qkv2, near_left, near_right, after1, mod, full_temporal_in, tinb,
        full_temporal_out, toutb,
    )
    frames_out, g2, n3, act, dpre, db3, dmod3, sum_exp, sum_shr = feed_forward(
        after2, cotangent, mod, full_expand, expb, full_shrink, shrb
    )
    plain = list(range(groups))
    hidden = dpre.shape[-1]
    high = 2 * (hidden // width) * modulate_weight.shape[0] // groups
    feed = outer_pieces(
        [[(n3, dpre, 0, hidden // width)]], width, groups, parts, plain, total_rows=high
    )
    feed = outer_pieces(
        [[(act, db3, 0, 1)]], width, groups, parts, plain, total_rows=high, into=feed
    )
    feed = lax.psum_scatter(feed.reshape(-1, width), "dp", scatter_dimension=0, tiled=True)
    db2, dqkv2, dleft, dright, nleft, nright, dgate2, sum_tout, sum_tin = temporal_backward(
        g2, branch2, mod, full_temporal_out, full_temporal_in, qkv2, left, right, probs
    )
    from_right = passed_along(nleft, "frame", -1)
    from_left = passed_along(nright, "frame", 1)
    order = core_order()
    halo = lambda t: [(near_left, dleft, t, 1), (near_right, dright, t, 1)]
    temporal = outer_pieces(
        [
            [(n2, dqkv2, 0, 1)],
            [(n2, dqkv2, 1, 1)] + halo(0),
            [(n2, dqkv2, 2, 1)] + halo(1),
            [(attn2, db2, 0, 1)],
        ],
        width, groups, parts, order,
    )
    temporal = halved(temporal, 0)
    dn2 = mm_nt(dqkv2.reshape(-1, 3 * width), full_temporal_in).reshape(frames, patches, width)
    dn2, temporal = lax.optimization_barrier((dn2, temporal))
    temporal = plane_summed(temporal)
    g1, db1, da1, dmod1, sum_sout = project_backward(
        dn2, from_left, from_right, after1, g2, branch1, mod, full_spatial_out
    )
    cond_float = condition.astype(F32)
    own_act = jax.nn.silu(cond_float).astype(BF16)
    early_mod = jnp.concatenate([dmod1, dgate2[:, None], dmod3], axis=1)
    early_mod = early_mod.reshape(frames, 7 * width).astype(BF16)
    early_sums = [s[0] for s in (sum_sout, sum_tin, sum_tout, sum_exp, sum_shr)]
    early_rows = jnp.concatenate(early_sums).astype(BF16).reshape(frames, -1)
    early = line_rotated(jnp.concatenate([own_act, early_mod, early_rows], axis=1))
    dheads, sum_first = heads_backward(qkv1, da1, 0)
    early_rows = jnp.sum(early[:, :, 8 * width :].astype(F32), axis=0).astype(BF16)
    early = early[:, :, : 8 * width].reshape(parts * frames, 8 * width)
    early_group = early[:, width:]
    early = jnp.concatenate([early, early_rows.reshape(parts * frames, -1)], axis=1)
    dheads, temporal, feed, early = lax.optimization_barrier((dheads, temporal, feed, early))
    early = lax.all_gather(early, "dp", axis=0, tiled=True)
    feed = jnp.concatenate([feed.reshape(parts, high, width), temporal], axis=1)
    total_high = feed.shape[1]
    feed = lax.psum_scatter(
        feed.reshape(-1, width), "frame", scatter_dimension=0, tiled=True
    )
    part = width // 2
    first = outer_pieces(
        [[(n1, dheads, 0, 3)], [(attn1, db1, 0, 2)]], part, groups, parts, plain
    )
    dheads, first = lax.optimization_barrier((dheads, first))
    first = dp_summed_start(first)
    dtail, sum_last, grad_frames, dmod0 = heads_backward(
        qkv1, da1, 1, (dheads, g1, frames_in, mod, full_spatial_in)
    )
    dtail, dmod0, sum_first, sum_last, feed = lax.optimization_barrier(
        (dtail, dmod0, sum_first, sum_last, feed)
    )
    feed = lax.all_gather(feed, "dp", axis=0, tiled=True).reshape(groups, total_high, width)
    sums = [s[0].reshape(3, part) for s in (sum_first, sum_last)]
    sum_sin = jnp.stack(sums, axis=1).reshape(1, 3 * width)
    late_mod = dmod0.reshape(frames, 2 * width).astype(BF16)
    late_rows = sum_sin.astype(BF16).reshape(frames, -1)
    late = line_rotated(jnp.concatenate([late_mod, late_rows], axis=1))
    last = outer_pieces([[(n1, dtail, 0, 3)]], part, groups, parts, order)
    last = halved(last, 0)
    first = summed(first)
    last, first, late = lax.optimization_barrier((last, first, late))
    last = plane_summed(last)
    late_rows = jnp.sum(late[:, :, 2 * width :].astype(F32), axis=0).astype(BF16)
    late_group = late[:, :, : 2 * width].reshape(parts * frames, 2 * width)
    both = line_summed(jnp.concatenate([first, last], axis=1))
    sizes = [first.shape[1], last.shape[1], 4 * parts * frames, 3 * width // part]
    both = plane_gathered(
        jnp.concatenate(
            [both, late_group.reshape(-1, part), late_rows.reshape(-1, part)], axis=0
        )
    )
    cuts = [sum(sizes[: at + 1]) for at in range(3)]
    first, last, late, late_rows = jnp.split(both, cuts, axis=1)
    blocks = lambda whole, count: jnp.split(whole, count, axis=1)
    flat = lambda pieces: jnp.concatenate(
        [p.reshape(-1, p.shape[-1]) for p in pieces], axis=1
    ).astype(F32)
    feed, temporal = feed[:, :high], feed[:, high:]
    *wide, narrow = blocks(temporal, 4)
    grad_temporal_in_sum, grad_temporal_out_sum = flat(wide), flat([narrow])
    starts, ends = blocks(first, 5), blocks(last, 3)
    grad_spatial_in_sum = flat([p for pair in zip(starts[:3], ends) for p in pair])
    grad_spatial_out_sum = flat(starts[3:])
    wide = unstacked(feed[:, : high // 2], hidden // width)
    grad_expand_sum = wide.reshape(-1, hidden).astype(F32)
    grad_shrink_sum = feed[:, high // 2 :].reshape(-1, width).astype(F32)
    rows = modulate_weight.shape[0]
    own_columns = lax.dynamic_slice_in_dim(early[:, :width], place * rows, rows, axis=1)
    late_all = late.reshape(groups * parts * frames, 2 * width)
    dmod_all = jnp.concatenate([late_all, early[:, width : 8 * width]], axis=1)
    grad_modulate_weight = mm_tn(own_columns, dmod_all)
    grad_modulate_bias = own_part(jnp.sum(dmod_all.astype(F32), axis=0))
    dact_group = mm_nt(late_group, modulate_weight[:, : 2 * width])
    dact_group = dact_group + mm_nt(early_group, modulate_weight[:, 2 * width :])
    pieces_act = line_swapped(dact_group.reshape(parts, frames, rows))
    dcond_act = jnp.swapaxes(pieces_act, 0, 1).reshape(frames, parts * rows)
    grad_condition = jax.vjp(jax.nn.silu, cond_float)[1](dcond_act)[0]
    early_rows = early[:, 8 * width :].astype(F32).reshape(groups, parts * frames, -1)
    early_rows = jnp.sum(early_rows, axis=0).reshape(-1)
    late_rows = jnp.sum(late_rows.astype(F32), axis=0).reshape(-1)
    bias_sums, at = [own_part(late_rows)], 0
    for grad in early_sums:
        bias_sums.append(own_part(early_rows[at : at + grad.shape[0]]))
        at += grad.shape[0]
    return (
        frames_out,
        grad_frames,
        grad_condition,
        grad_spatial_in_sum,
        bias_sums[0],
        grad_spatial_out_sum,
        bias_sums[1],
        grad_temporal_in_sum,
        bias_sums[2],
        grad_temporal_out_sum,
        bias_sums[3],
        grad_expand_sum,
        bias_sums[4],
        grad_shrink_sum,
        bias_sums[5],
        grad_modulate_weight,
        grad_modulate_bias,
    )


def solution(mesh):
    in_specs = (
        P(("dp", "frame"), None, None),
        P(("dp", "frame"), None),
        P("dp", None),
        P("frame", None),
        P("frame"),
        P("frame", None),
        P("frame"),
        P("frame", None),
        P("frame"),
        P("frame", None),
        P("frame"),
        P("frame", None),
        P("frame"),
        P("frame", None),
        P("frame"),
        P("frame", None),
        P("frame"),
        P(("dp", "frame"), None, None),
    )
    out_specs = (
        P(("dp", "frame"), None, None),
        P(("dp", "frame"), None, None),
        P(("dp", "frame"), None),
        P("frame", None),
        P("frame"),
        P("frame", None),
        P("frame"),
        P("frame", None),
        P("frame"),
        P("frame", None),
        P("frame"),
        P("frame", None),
        P("frame"),
        P("frame", None),
        P("frame"),
        P("frame", None),
        P("frame"),
    )

    return jax.shard_map(
        per_device, mesh=mesh, in_specs=in_specs, out_specs=out_specs, check_vma=False
    )
```

```python
import functools

import jax
import jax.numpy as jnp
from jax import lax
from jax.experimental import pallas as pl
from jax.experimental.pallas import tpu as pltpu
from jax.sharding import PartitionSpec as P


HEADS = 12
HEAD_DIM = 64
WINDOW = 2
DP = "dp"
FRAME = "frame"

F32 = jnp.float32
BF16 = jnp.bfloat16
SCALE = HEAD_DIM ** (-0.5)
SPAN = 2 * WINDOW + 1


def mm(a, b):
    return lax.dot_general(a, b, (((1,), (0,)), ((), ())), preferred_element_type=F32)


def mm_nt(a, b):
    return lax.dot_general(a, b, (((1,), (1,)), ((), ())), preferred_element_type=F32)


def mm_tn(a, b):
    return lax.dot_general(a, b, (((0,), (0,)), ((), ())), preferred_element_type=F32)


def unit(x):
    centred = x - jnp.mean(x, axis=-1, keepdims=True)
    inv = lax.rsqrt(jnp.mean(centred * centred, axis=-1, keepdims=True) + 1e-06)
    return centred * inv, inv


def unit_back(dn, xhat, inv, scale):
    e = dn * (1.0 + scale)
    first = jnp.mean(e, axis=-1, keepdims=True)
    second = jnp.mean(e * xhat, axis=-1, keepdims=True)
    return inv * (e - first - xhat * second)


def down(x):
    return jnp.sum(x, axis=0, keepdims=True)


def low_half(rows):
    return lax.broadcasted_iota(jnp.int32, (rows, 2 * HEAD_DIM), 1) < HEAD_DIM


def soft(scores):
    e = jnp.exp(scores - jnp.max(scores, axis=-1, keepdims=True))
    return e / jnp.sum(e, axis=-1, keepdims=True)


def params(flops, nbytes, trans=0):
    return dict(
        compiler_params=pltpu.CompilerParams(vmem_limit_bytes=60 * 2**20),
        cost_estimate=pl.CostEstimate(
            flops=int(flops), bytes_accessed=int(nbytes), transcendentals=int(trans)
        ),
    )


def fixed(shape):
    return pl.BlockSpec(shape, lambda *_: (0,) * len(shape), pipeline_mode=pl.Buffered(1))


def per_first(shape):
    return pl.BlockSpec((1,) + shape, lambda i: (i,) + (0,) * len(shape))


def per_second(lead, tile, width):
    return pl.BlockSpec((lead, tile, width), lambda i: (0, i, 0))


def lay_out(raw, whole, first=0):
    @pl.when(pl.program_id(0) == 0)
    def _():
        groups, parts, _, width = raw.shape
        rows = whole.shape[0] // (groups * parts)
        for f in range(parts):
            for d in range(groups):
                at = (f * groups + d) * rows
                for tile in range(whole.shape[1] // width):
                    source = (first + tile) * rows
                    whole[at : at + rows, tile * width : (tile + 1) * width] = raw[
                        d, f, source : source + rows
                    ]


def rows_of(raw, stacks, total, at=0):
    groups, parts, height, width = raw.shape
    return pl.BlockSpec(
        (groups, parts, height * stacks // total, width),
        lambda *_: (0, 0, at, 0),
        pipeline_mode=pl.Buffered(1),
    )


def spatial_kernel(x_ref, mod_ref, raw, bsi, n1_ref, qkv1_ref, attn_ref, wsi):
    lay_out(raw, wsi)
    x = x_ref[0].astype(F32)
    width = x.shape[1]
    xhat, _ = unit(x)
    n1 = (xhat * (1.0 + mod_ref[0, 1:2]) + mod_ref[0, 0:1]).astype(BF16)
    n1_ref[0] = n1
    qkv1_ref[0] = (mm(n1, wsi[...]) + bsi[...]).astype(BF16)
    half = low_half(x.shape[0])
    for pair in range(width // (2 * HEAD_DIM)):
        at = pair * 2 * HEAD_DIM
        q = qkv1_ref[0, :, at : at + 2 * HEAD_DIM]
        k = qkv1_ref[0, :, width + at : width + at + 2 * HEAD_DIM]
        v = qkv1_ref[0, :, 2 * width + at : 2 * width + at + 2 * HEAD_DIM]
        zero = jnp.zeros_like(q)
        first = soft(mm_nt(jnp.where(half, q, zero), k) * SCALE).astype(BF16)
        second = soft(mm_nt(jnp.where(half, zero, q), k) * SCALE).astype(BF16)
        out = jnp.where(half, mm(first, v), mm(second, v))
        attn_ref[0, :, at : at + 2 * HEAD_DIM] = out.astype(BF16)


def spatial_forward(x, mod, space, bsi):
    frames, patches, width = x.shape
    block = lambda n: per_first((patches, n))
    outs = [width, 3 * width, width]
    tokens = frames * patches
    return pl.pallas_call(
        spatial_kernel,
        grid=(frames,),
        in_specs=[
            block(width), per_first(mod.shape[1:]),
            rows_of(space, 3, 4), fixed(bsi.shape),
        ],
        out_specs=[block(n) for n in outs],
        out_shape=[jax.ShapeDtypeStruct((frames, patches, n), BF16) for n in outs],
        scratch_shapes=[pltpu.VMEM((width, 3 * width), BF16)],
        name="spatial_forward",
        **params(2 * tokens * width * (3 * width + 4 * patches), 12e6, tokens * patches * HEADS),
    )(x, mod, space, bsi)


def project_kernel(x_ref, attn_ref, mod_ref, raw, bso, branch_ref, after_ref, n2_ref, wso):
    lay_out(raw, wso)
    branch = mm(attn_ref[0], wso[...]) + bso[...]
    branch_ref[0] = branch
    after = x_ref[0].astype(F32) + mod_ref[0, 2:3] * branch
    after_ref[0] = after
    xhat, _ = unit(after)
    n2_ref[0] = (xhat * (1.0 + mod_ref[0, 4:5]) + mod_ref[0, 3:4]).astype(BF16)


def project_forward(x, attn, mod, space, bso):
    frames, patches, width = x.shape
    block = per_first((patches, width))
    tokens = frames * patches
    return pl.pallas_call(
        project_kernel,
        grid=(frames,),
        in_specs=[
            block, block, per_first(mod.shape[1:]), rows_of(space, 1, 4, 3), fixed(bso.shape)
        ],
        scratch_shapes=[pltpu.VMEM((width, width), BF16)],
        out_specs=[block] * 3,
        out_shape=[jax.ShapeDtypeStruct(x.shape, t) for t in (F32, F32, BF16)],
        name="project_forward",
        **params(2 * tokens * width * width, 13e6),
    )(x, attn, mod, space, bso)


def qkv_kernel(n_ref, raw, bias, out_ref, whole):
    lay_out(raw, whole)
    out_ref[0] = (mm(n_ref[0], whole[...]) + bias[...]).astype(BF16)


def temporal_qkv(n, time, bias):
    frames, patches, width = n.shape
    tokens = frames * patches
    return pl.pallas_call(
        qkv_kernel,
        grid=(frames,),
        in_specs=[per_first((patches, width)), rows_of(time, 3, 4), fixed(bias.shape)],
        out_specs=per_first((patches, 3 * width)),
        out_shape=jax.ShapeDtypeStruct((frames, patches, 3 * width), BF16),
        scratch_shapes=[pltpu.VMEM((width, 3 * width), BF16)],
        name="temporal_qkv",
        **params(6 * tokens * width * width, 10e6),
    )(n, time, bias)


def split_store(hi_ref, lo_ref, row, prod):
    hi = prod.astype(BF16)
    hi_ref[row] = hi
    lo_ref[row] = (prod - hi.astype(F32)).astype(BF16)


def ext_rows(e, frames, left, own, right, base, width):
    if e < WINDOW:
        return left[e, :, base - width : base]
    if e < WINDOW + frames:
        return own[e - WINDOW, :, base : base + width]
    return right[e - WINDOW - frames, :, base - width : base]


def head_sums(hi_ref, lo_ref, first, count, ones):
    tile, width = hi_ref.shape[1:]
    hi = hi_ref[first : first + count].reshape(count * tile, width)
    lo = lo_ref[first : first + count].reshape(count * tile, width)
    return mm(hi, ones) + mm(lo, ones)


def temporal_kernel(
    allowed, qkv_ref, nl_ref, nr_ref, after_ref, mod_ref, raw_in, bti, raw_out, bto, ones, ones_t,
    probs_ref, attn_ref, branch_ref, out_ref, left_ref, right_ref, hi_ref, lo_ref, wkv, wto,
):
    frames, tile, width = after_ref.shape
    lay_out(raw_in, wkv, 1)
    lay_out(raw_out, wto)
    for near, kv_ref in ((nl_ref, left_ref), (nr_ref, right_ref)):
        kv = mm(near[...].reshape(WINDOW * tile, width), wkv[...]) + bti[:, width:]
        kv_ref[...] = kv.astype(BF16).reshape(WINDOW, tile, 2 * width)
    for t in range(frames):
        q = qkv_ref[t, :, :width].astype(F32)
        for o in range(SPAN):
            k = ext_rows(t + o, frames, left_ref, qkv_ref, right_ref, width, width)
            split_store(hi_ref, lo_ref, t * SPAN + o, q * k.astype(F32))
    for t in range(frames):
        raw = head_sums(hi_ref, lo_ref, t * SPAN, SPAN, ones[...]) * SCALE
        raw = [
            jnp.where(allowed[o, t] > 0, raw[o * tile : (o + 1) * tile], -1e30)
            for o in range(SPAN)
        ]
        top = raw[0]
        for o in range(1, SPAN):
            top = jnp.maximum(top, raw[o])
        expo = [jnp.exp(r - top) for r in raw]
        total = expo[0]
        for o in range(1, SPAN):
            total = total + expo[o]
        inv = 1.0 / total
        probs = [e * inv for e in expo]
        for o in range(SPAN):
            probs_ref[t, o] = probs[o]
        wide = mm(jnp.concatenate(probs, axis=0).astype(BF16), ones_t[...])
        total = None
        for o in range(SPAN):
            v = ext_rows(t + o, frames, left_ref, qkv_ref, right_ref, 2 * width, width)
            term = wide[o * tile : (o + 1) * tile] * v.astype(F32)
            total = term if total is None else total + term
        attn_ref[t] = total.astype(BF16)
    branch = mm(attn_ref[...].reshape(frames * tile, width), wto[...]) + bto[...]
    for t in range(frames):
        part = branch[t * tile : (t + 1) * tile]
        branch_ref[t] = part
        out_ref[t] = after_ref[t] + mod_ref[t, 5:6] * part


def head_ones(width):
    head = jnp.arange(width, dtype=jnp.int32)[:, None] // HEAD_DIM
    return (head == jnp.arange(128, dtype=jnp.int32)[None, :]).astype(BF16)


def temporal_forward(allowed, qkv, near_left, near_right, after, mod, time, bti, bto):
    frames, patches, width = after.shape
    tile = 64
    ones = head_ones(width)
    spec = lambda n: per_second(frames, tile, n)
    halo = per_second(WINDOW, tile, 2 * width)
    near = per_second(WINDOW, tile, width)
    shape = lambda t: jax.ShapeDtypeStruct((frames, patches, width), t)
    tokens = frames * patches
    return pl.pallas_call(
        temporal_kernel,
        grid=(patches // tile,),
        in_specs=[
            pl.BlockSpec(memory_space=pltpu.SMEM),
            spec(3 * width), near, near, spec(width), fixed(mod.shape),
            rows_of(time, 3, 4), fixed(bti.shape), rows_of(time, 1, 4, 3), fixed(bto.shape),
            fixed(ones.shape), fixed(ones.shape[::-1]),
        ],
        out_specs=[
            pl.BlockSpec((frames, SPAN, tile, 128), lambda i: (0, 0, i, 0)),
            spec(width), spec(width), spec(width), halo, halo,
        ],
        out_shape=[
            jax.ShapeDtypeStruct((frames, SPAN, patches, 128), F32),
            shape(BF16), shape(F32), shape(F32),
            jax.ShapeDtypeStruct((WINDOW, patches, 2 * width), BF16),
            jax.ShapeDtypeStruct((WINDOW, patches, 2 * width), BF16),
        ],
        scratch_shapes=[pltpu.VMEM((frames * SPAN, tile, width), BF16)] * 2
        + [pltpu.VMEM((width, 2 * width), BF16), pltpu.VMEM((width, width), BF16)],
        name="temporal_forward",
        **params(2 * tokens * width * (width + SPAN * 400), 22e6, tokens * SPAN * 128),
    )(allowed, qkv, near_left, near_right, after, mod, time, bti, time, bto, ones, ones.T)


def feed_kernel(
    after_ref, cot_ref, mod_ref, raw1, b1, raw2, b2,
    out_ref, g_ref, n_ref, act_ref, dpre_ref, db_ref, dmod_ref, sum1_ref, sum2_ref, w1, w2,
):
    lay_out(raw1, w1)
    lay_out(raw2, w2)
    after = after_ref[0]
    width = after.shape[1]
    hidden = w1.shape[1]
    xhat, inv = unit(after)
    scale = mod_ref[0, 7:8]
    gate = mod_ref[0, 8:9]
    n = (xhat * (1.0 + scale) + mod_ref[0, 6:7]).astype(BF16)
    n_ref[0] = n
    g3 = cot_ref[0].astype(F32)
    db = (gate * g3).astype(BF16)
    db_ref[0] = db

    @pl.when(pl.program_id(0) == 0)
    def _():
        sum1_ref[...] = jnp.zeros_like(sum1_ref)
        sum2_ref[...] = jnp.zeros_like(sum2_ref)

    sum2_ref[...] += down(db.astype(F32))
    branch = jnp.zeros_like(after)
    dn = jnp.zeros_like(after)
    chunk = width
    for c in range(hidden // chunk):
        cols = slice(c * chunk, (c + 1) * chunk)
        pre = mm(n, w1[:, cols]) + b1[:, cols]
        dact = mm_nt(db, w2[cols, :])
        phi = 0.5 * (1.0 + lax.erf(pre * 0.7071067811865476))
        act = (pre * phi).astype(BF16)
        slope = phi + pre * (jnp.exp(-0.5 * pre * pre) * 0.3989422804014327)
        dpre = (dact * slope).astype(BF16)
        act_ref[0, :, cols] = act
        dpre_ref[0, :, cols] = dpre
        sum1_ref[:, cols] += down(dpre.astype(F32))
        branch += mm(act, w2[cols, :])
        dn += mm_nt(dpre, w1[:, cols])
    branch = branch + b2[...]
    out_ref[0] = (after + gate * branch).astype(BF16)
    dmod_ref[0, 0:1] = down(dn)
    dmod_ref[0, 1:2] = down(dn * xhat)
    dmod_ref[0, 2:3] = down(g3 * branch)
    g_ref[0] = g3 + unit_back(dn, xhat, inv, scale)


def feed_forward(after, cot, mod, dense, b1, b2):
    frames, patches, width = after.shape
    hidden = b1.shape[1]
    shape = lambda n, t: jax.ShapeDtypeStruct((frames, patches, n), t)
    block = lambda n: per_first((patches, n))
    outs = [(width, BF16), (width, F32), (width, BF16), (hidden, BF16), (hidden, BF16), (width, BF16)]
    tokens = frames * patches
    return pl.pallas_call(
        feed_kernel,
        grid=(frames,),
        in_specs=[
            block(width), block(width), per_first(mod.shape[1:]),
            rows_of(dense, 1, 2), fixed(b1.shape), rows_of(dense, 1, 2, 1), fixed(b2.shape),
        ],
        scratch_shapes=[pltpu.VMEM((width, hidden), BF16), pltpu.VMEM((hidden, width), BF16)],
        out_specs=[block(n) for n, _ in outs]
        + [per_first((3, width)), pl.BlockSpec((1, hidden), lambda i: (0, 0)),
           pl.BlockSpec((1, width), lambda i: (0, 0))],
        out_shape=[shape(n, t) for n, t in outs]
        + [jax.ShapeDtypeStruct((frames, 3, width), F32),
           jax.ShapeDtypeStruct((1, hidden), F32), jax.ShapeDtypeStruct((1, width), F32)],
        name="feed_forward",
        **params(8 * tokens * width * hidden, 32e6, 2 * tokens * hidden),
    )(after, cot, mod, dense, b1, dense, b2)


def temporal_back_kernel(
    g_ref, branch_ref, mod_ref, raw_out, raw_in, qkv_ref, left_ref, right_ref, probs_ref, ones, ones_t,
    db_ref, dqkv_ref, dleft_ref, dright_ref, nleft_ref, nright_ref, dgate_ref, sum_ref, sumq_ref,
    hi_ref, lo_ref, da_ref, ds_ref, pw_ref, wkv, wto,
):
    frames, tile, width = g_ref.shape
    lay_out(raw_in, wkv, 1)
    lay_out(raw_out, wto)

    @pl.when(pl.program_id(0) == 0)
    def _():
        dgate_ref[...] = jnp.zeros_like(dgate_ref)
        sum_ref[...] = jnp.zeros_like(sum_ref)
        sumq_ref[...] = jnp.zeros_like(sumq_ref)

    for t in range(frames):
        g = g_ref[t]
        dgate_ref[t : t + 1] += down(g * branch_ref[t])
        db = (mod_ref[t, 5:6] * g).astype(BF16)
        db_ref[t] = db
        sum_ref[...] += down(db.astype(F32))
    da_all = mm_nt(db_ref[...].reshape(frames * tile, width), wto[...]).astype(BF16)
    da_ref[...] = da_all.reshape(frames, tile, width)
    for t in range(frames):
        da = da_ref[t].astype(F32)
        for o in range(SPAN):
            v = ext_rows(t + o, frames, left_ref, qkv_ref, right_ref, 2 * width, width)
            split_store(hi_ref, lo_ref, t * SPAN + o, da * v.astype(F32))
    for t in range(frames):
        dp = head_sums(hi_ref, lo_ref, t * SPAN, SPAN, ones[...])
        probs = probs_ref[t].reshape(SPAN * tile, 128)
        both = probs * dp
        dot = both[:tile]
        for o in range(1, SPAN):
            dot = dot + both[o * tile : (o + 1) * tile]
        ds = both - probs * jnp.concatenate([dot] * SPAN, axis=0)
        wide = mm(ds.astype(BF16), ones_t[...]).astype(BF16)
        ds_ref[t * SPAN : (t + 1) * SPAN] = wide.reshape(SPAN, tile, width)
        wide = mm(probs.astype(BF16), ones_t[...]).astype(BF16)
        pw_ref[t * SPAN : (t + 1) * SPAN] = wide.reshape(SPAN, tile, width)
    for t in range(frames):
        total = None
        for o in range(SPAN):
            k = ext_rows(t + o, frames, left_ref, qkv_ref, right_ref, width, width)
            term = ds_ref[t * SPAN + o].astype(F32) * k.astype(F32)
            total = term if total is None else total + term
        dqkv_ref[t, :, :width] = (total * SCALE).astype(BF16)
    for e in range(frames + 2 * WINDOW):
        dk = dv = None
        for t in range(max(0, e - SPAN + 1), min(frames, e + 1)):
            row = t * SPAN + e - t
            q = qkv_ref[t, :, :width].astype(F32)
            term = ds_ref[row].astype(F32) * q
            dk = term if dk is None else dk + term
            term = pw_ref[row].astype(F32) * da_ref[t].astype(F32)
            dv = term if dv is None else dv + term
        dk = (dk * SCALE).astype(BF16)
        dv = dv.astype(BF16)
        if e < WINDOW:
            dleft_ref[e, :, :width] = dk
            dleft_ref[e, :, width:] = dv
        elif e < WINDOW + frames:
            dqkv_ref[e - WINDOW, :, width : 2 * width] = dk
            dqkv_ref[e - WINDOW, :, 2 * width :] = dv
        else:
            dright_ref[e - WINDOW - frames, :, :width] = dk
            dright_ref[e - WINDOW - frames, :, width:] = dv
    for dkv_ref, near_ref in ((dleft_ref, nleft_ref), (dright_ref, nright_ref)):
        flat = dkv_ref[...].reshape(WINDOW * tile, 2 * width)
        sumq_ref[:, width:] += down(flat.astype(F32))
        near_ref[...] = mm_nt(flat, wkv[...]).astype(BF16).reshape(WINDOW, tile, width)
    sumq_ref[...] += down(dqkv_ref[...].reshape(frames * tile, 3 * width).astype(F32))


def temporal_backward(g, branch, mod, time, qkv, left, right, probs):
    frames, patches, width = g.shape
    tile = 64
    ones = head_ones(width)
    spec = lambda n: per_second(frames, tile, n)
    halo = per_second(WINDOW, tile, 2 * width)
    near = per_second(WINDOW, tile, width)
    shape = lambda f, n, t: jax.ShapeDtypeStruct((f, patches, n), t)
    tokens = frames * patches
    return pl.pallas_call(
        temporal_back_kernel,
        grid=(patches // tile,),
        in_specs=[
            spec(width), spec(width), fixed(mod.shape), rows_of(time, 1, 4, 3), rows_of(time, 3, 4),
            spec(3 * width), halo, halo,
            pl.BlockSpec((frames, SPAN, tile, 128), lambda i: (0, 0, i, 0)),
            fixed(ones.shape), fixed(ones.shape[::-1]),
        ],
        out_specs=[
            spec(width), spec(3 * width), halo, halo, near, near,
            pl.BlockSpec((frames, width), lambda i: (0, 0)),
            pl.BlockSpec((1, width), lambda i: (0, 0)),
            pl.BlockSpec((1, 3 * width), lambda i: (0, 0)),
        ],
        out_shape=[
            shape(frames, width, BF16), shape(frames, 3 * width, BF16),
            shape(WINDOW, 2 * width, BF16), shape(WINDOW, 2 * width, BF16),
            shape(WINDOW, width, BF16), shape(WINDOW, width, BF16),
            jax.ShapeDtypeStruct((frames, width), F32), jax.ShapeDtypeStruct((1, width), F32),
            jax.ShapeDtypeStruct((1, 3 * width), F32),
        ],
        scratch_shapes=[pltpu.VMEM((frames * SPAN, tile, width), BF16)] * 2
        + [pltpu.VMEM((frames, tile, width), BF16)]
        + [pltpu.VMEM((frames * SPAN, tile, width), BF16)] * 2
        + [pltpu.VMEM((width, 2 * width), BF16), pltpu.VMEM((width, width), BF16)],
        name="temporal_backward",
        **params(2 * tokens * width * (width + SPAN * 500), 36e6),
    )(g, branch, mod, time, time, qkv, left, right, probs, ones, ones.T)


def project_back_kernel(
    dqkv_ref, fl_ref, fr_ref, after_ref, g2_ref, branch_ref, mod_ref, raw_in, raw_out,
    g_ref, db_ref, da_ref, dmod_ref, sum_ref, wti, wso,
):
    lay_out(raw_in, wti)
    lay_out(raw_out, wso)
    at = pl.program_id(0)

    @pl.when(at == 0)
    def _():
        sum_ref[...] = jnp.zeros_like(sum_ref)

    dn = mm_nt(dqkv_ref[0], wti[...]) + jnp.where(at < WINDOW, fl_ref[0].astype(F32), fr_ref[0].astype(F32))
    xhat, inv = unit(after_ref[0])
    dmod_ref[0, 1:2] = down(dn)
    dmod_ref[0, 2:3] = down(dn * xhat)
    g1 = g2_ref[0] + unit_back(dn, xhat, inv, mod_ref[0, 4:5])
    dmod_ref[0, 0:1] = down(g1 * branch_ref[0])
    g_ref[0] = g1
    db = (mod_ref[0, 2:3] * g1).astype(BF16)
    db_ref[0] = db
    sum_ref[...] += down(db.astype(F32))
    da_ref[0] = mm_nt(db, wso[...]).astype(BF16)


def project_backward(dqkv2, from_left, from_right, after, g2, branch, mod, time, space):
    frames, patches, width = after.shape
    block = per_first((patches, width))
    tokens = frames * patches
    return pl.pallas_call(
        project_back_kernel,
        grid=(frames,),
        in_specs=[
            per_first((patches, 3 * width)),
            pl.BlockSpec((1, patches, width), lambda i: (jnp.minimum(i, WINDOW - 1), 0, 0)),
            pl.BlockSpec((1, patches, width), lambda i: (jnp.maximum(i - WINDOW, 0), 0, 0)),
            block, block, block, per_first(mod.shape[1:]), rows_of(time, 3, 4), rows_of(space, 1, 4, 3),
        ],
        scratch_shapes=[pltpu.VMEM((width, 3 * width), BF16), pltpu.VMEM((width, width), BF16)],
        out_specs=[block, block, block, per_first((3, width)),
                   pl.BlockSpec((1, width), lambda i: (0, 0))],
        out_shape=[jax.ShapeDtypeStruct(after.shape, t) for t in (F32, BF16, BF16)]
        + [jax.ShapeDtypeStruct((frames, 3, width), F32), jax.ShapeDtypeStruct((1, width), F32)],
        name="project_backward",
        **params(8 * tokens * width * width, 24e6),
    )(dqkv2, from_left, from_right, after, g2, branch, mod, time, space)


def heads_back(q_ref, k_ref, v_ref, da_ref, out_ref, sum_ref):
    tokens, width = q_ref.shape[1:]

    @pl.when(pl.program_id(0) == 0)
    def _():
        sum_ref[...] = jnp.zeros_like(sum_ref)

    half = low_half(tokens)
    for pair in range(width // (2 * HEAD_DIM)):
        cols = slice(pair * 2 * HEAD_DIM, (pair + 1) * 2 * HEAD_DIM)
        q, k, v, da = (ref[0, :, cols] for ref in (q_ref, k_ref, v_ref, da_ref))
        zero = jnp.zeros_like(q)
        parts = []
        for side in range(2):
            pick = (lambda u: jnp.where(half, u, zero)) if side == 0 else (
                lambda u: jnp.where(half, zero, u))
            probs = soft(mm_nt(pick(q), k) * SCALE)
            dp = mm_nt(pick(da), v)
            both = probs * dp
            ds = (both - probs * jnp.sum(both, axis=-1, keepdims=True)).astype(BF16)
            parts.append((mm(ds, k), mm_tn(ds, q), mm_tn(probs.astype(BF16), da)))
        grads = [jnp.where(half, a, b) for a, b in zip(*parts)]
        for at, grad in enumerate((grads[0] * SCALE, grads[1] * SCALE, grads[2])):
            out_ref[0, :, at * width + cols.start : at * width + cols.stop] = grad.astype(BF16)
    sum_ref[...] += down(out_ref[0].astype(F32))


def first_heads_kernel(q_ref, k_ref, v_ref, da_ref, out_ref, sum_ref):
    heads_back(q_ref, k_ref, v_ref, da_ref, out_ref, sum_ref)


def last_heads_kernel(
    q_ref, k_ref, v_ref, da_ref, first_ref, g_ref, x_ref, mod_ref, raw,
    out_ref, sum_ref, grad_ref, dmod_ref, wsi,
):
    lay_out(raw, wsi)
    heads_back(q_ref, k_ref, v_ref, da_ref, out_ref, sum_ref)
    width = q_ref.shape[2]
    dn = None
    for at in range(3):
        for side, ref in enumerate((first_ref, out_ref)):
            cols = slice((2 * at + side) * width, (2 * at + side + 1) * width)
            term = mm_nt(ref[0, :, at * width : (at + 1) * width], wsi[:, cols])
            dn = term if dn is None else dn + term
    xhat, inv = unit(x_ref[0].astype(F32))
    dmod_ref[0, 0:1] = down(dn)
    dmod_ref[0, 1:2] = down(dn * xhat)
    grad_ref[0] = g_ref[0] + unit_back(dn, xhat, inv, mod_ref[0, 1:2])


def heads_backward(qkv1, da1, side, rest=None):
    frames, patches, width = da1.shape
    part = width // 2
    column = lambda at: pl.BlockSpec((1, patches, part), lambda i: (i, 0, at))
    block = lambda n: per_first((patches, n))
    tokens = frames * patches
    in_specs = [column(side), column(2 + side), column(4 + side), column(side)]
    operands = [qkv1, qkv1, qkv1, da1]
    out_specs = [block(3 * part), pl.BlockSpec((1, 3 * part), lambda i: (0, 0))]
    out_shape = [
        jax.ShapeDtypeStruct((frames, patches, 3 * part), BF16),
        jax.ShapeDtypeStruct((1, 3 * part), F32),
    ]
    scratch = []
    if rest is not None:
        first, g1, x, mod, space = rest
        in_specs += [block(3 * part), block(width), block(width), per_first(mod.shape[1:]),
                     rows_of(space, 3, 4)]
        operands += [first, g1, x, mod, space]
        scratch = [pltpu.VMEM((width, 3 * width), BF16)]
        out_specs += [block(width), per_first((2, width))]
        out_shape += [
            jax.ShapeDtypeStruct((frames, patches, width), F32),
            jax.ShapeDtypeStruct((frames, 2, width), F32),
        ]
    return pl.pallas_call(
        first_heads_kernel if rest is None else last_heads_kernel,
        grid=(frames,),
        in_specs=in_specs,
        out_specs=out_specs,
        out_shape=out_shape,
        scratch_shapes=scratch,
        name="first_heads_backward" if rest is None else "last_heads_backward",
        **params(2 * tokens * width * (5 * patches + (0 if rest is None else 3 * width)),
                 16e6, tokens * patches * HEADS // 2),
    )(*operands)


def outer_kernel(*refs, jobs, order):
    out_ref = refs[-1]
    parts = out_ref.shape[1]
    groups = len(order)
    top = 0
    turned = {}
    for terms in jobs:
        total = None
        for left, right in terms:
            if left not in turned:
                turned[left] = refs[left][...].T
            term = mm(turned[left], refs[right][...])
            total = term if total is None else total + term
        rows = total.shape[0] // (groups * parts)
        width = out_ref.shape[3]
        for tile in range(total.shape[1] // width):
            for f in range(parts):
                for d in range(groups):
                    row = (f * groups + d) * rows
                    out_ref[order[d], f, top : top + rows] = total[
                        row : row + rows, tile * width : (tile + 1) * width
                    ].astype(BF16)
            top += rows


def outer_pieces(jobs, width, groups, parts, order, total_rows=None, into=None):
    shaped = {}

    def flat(a):
        return shaped.setdefault(id(a), a.reshape(-1, a.shape[-1]))

    jobs = [[(flat(left), flat(right), *tiles) for left, right, *tiles in job] for job in jobs]
    depth = jobs[0][0][0].shape[1]
    rows = depth // (groups * parts)
    height = sum(job[0][3] for job in jobs) * rows
    total_rows = total_rows or height
    if rows % 8:
        pieces = [] if into is None else [into[:, :, : total_rows - height]]
        for job in jobs:
            for tile in range(job[0][3]):
                cut = lambda r, t: r[:, (t + tile) * width : (t + tile + 1) * width]
                total = sum(mm_tn(l, cut(r, t)) for l, r, t, _ in job)
                total = total.astype(BF16).reshape(parts, groups, rows, width).swapaxes(0, 1)
                pieces.append(jnp.stack([total[order.index(d)] for d in range(groups)]))
        whole = jnp.concatenate(pieces, axis=2)
        return jnp.pad(whole, ((0, 0), (0, 0), (0, total_rows - whole.shape[2]), (0, 0)))
    step = 1
    while (step * depth // parts) % 128:
        step *= 2
    specs, operands, flops, known, terms = [], [], 0, {}, []

    def operand(array, spec, key):
        if key not in known:
            known[key] = len(operands)
            operands.append(array)
            specs.append(spec)
        return known[key]

    for job in jobs:
        pairs = []
        for left, right, tile, tiles in job:
            tokens = left.shape[0]
            spec = pl.BlockSpec((tokens, step * depth // parts), lambda i: (0, i))
            first = operand(left, spec, (id(left), None))
            spec = pl.BlockSpec(
                (tokens, tiles * width),
                lambda i, at=tile // tiles: (0, at),
                pipeline_mode=pl.Buffered(1),
            )
            pairs.append((first, operand(right, spec, (id(right), tile, tiles))))
            flops += 2 * tokens * depth * width * tiles
        terms.append(tuple(pairs))
    place = 0
    aliases = {}
    if into is not None:
        place = total_rows // height - 1
        aliases = {len(operands): 0}
        specs.append(pl.BlockSpec(memory_space=pl.ANY))
        operands.append(into)
    return pl.pallas_call(
        functools.partial(outer_kernel, jobs=tuple(terms), order=tuple(order)),
        grid=(parts // step,),
        in_specs=specs,
        out_specs=pl.BlockSpec((groups, step, height, width), lambda i: (0, i, place, 0)),
        out_shape=jax.ShapeDtypeStruct((groups, parts, total_rows, width), BF16),
        input_output_aliases=aliases,
        name="outer_pieces",
        **params(flops, 12e6),
    )(*operands)


def last_kernel(own_ref, *refs, sizes):
    groups = len(refs) - 9
    pieces, (columns, early) = refs[:groups], refs[groups : groups + 2]
    in_ref, out_ref, mod_ref, sum_ref, bias_ref, late_ref, turned = refs[groups + 2 :]
    part = pieces[0].shape[1]
    rows = in_ref.shape[0] // groups
    tall = sizes[2] // 4
    begin = sizes[0] + sizes[1]
    bias = None
    for far, piece in enumerate(pieces):
        d = own_ref[0] ^ far
        there = pl.ds(pl.multiple_of(d * rows, 8), rows)
        for at in range(3):
            for side, top in enumerate((0, sizes[0])):
                column = (2 * at + side) * part
                in_ref[there, column : column + part] = piece[
                    top + at * rows : top + (at + 1) * rows
                ].astype(F32)
        for at in range(2):
            source = (3 + at) * rows
            out_ref[there, at * part : (at + 1) * part] = piece[source : source + rows].astype(F32)
        there = pl.ds(pl.multiple_of(d * tall, 16), tall)
        for at in range(4):
            source = begin + at * tall
            late_ref[there, at * part : (at + 1) * part] = piece[source : source + tall]
        term = piece[begin + sizes[2] : begin + sizes[2] + sizes[3]].astype(F32)
        bias = term if bias is None else bias + term
    bias_ref[...] = bias
    turned[...] = columns[...].T
    wide = 4 * part
    mod_ref[:, :wide] = mm(turned[...], late_ref[...])
    sum_ref[:, :wide] = down(late_ref[...].astype(F32))
    for at in range(early.shape[1] // wide + 1):
        cols = slice(at * wide, min((at + 1) * wide, early.shape[1]))
        mod_ref[:, wide + cols.start : wide + cols.stop] = mm(turned[...], early[:, cols])
        sum_ref[:, wide + cols.start : wide + cols.stop] = down(early[:, cols].astype(F32))


def last_outputs(pieces, columns, early, sizes, rows):
    part = pieces[0].shape[1]
    tokens, more = early.shape
    total = more + 4 * part
    shapes = [(rows, 6 * part), (rows, 2 * part), (rows, total), (1, total), (sizes[3], part)]
    own = lax.axis_index(DP).reshape(1)
    whole = pl.BlockSpec(memory_space=pltpu.VMEM)
    return pl.pallas_call(
        functools.partial(last_kernel, sizes=tuple(sizes)),
        in_specs=[pl.BlockSpec(memory_space=pltpu.SMEM)] + [whole] * (len(pieces) + 2),
        out_specs=[whole] * 5,
        out_shape=[jax.ShapeDtypeStruct(s, F32) for s in shapes],
        scratch_shapes=[
            pltpu.VMEM((tokens, 4 * part), BF16), pltpu.VMEM((rows, tokens), BF16),
        ],
        name="last_outputs",
        **params(2 * rows * tokens * total, 12e6),
    )(own, *pieces, columns, early)


def own_part(vector):
    size = vector.shape[0] // lax.axis_size(FRAME)
    return lax.dynamic_slice_in_dim(vector, lax.axis_index(FRAME) * size, size)


def stacked(block, width):
    count = block.shape[-1] // width
    return jnp.concatenate(
        [block[..., k * width : (k + 1) * width] for k in range(count)], axis=-2
    )


def unstacked(block, count):
    rows = block.shape[-2] // count
    return jnp.concatenate(
        [block[..., k * rows : (k + 1) * rows, :] for k in range(count)], axis=-1
    )


def line_gathered(mine):
    parts = lax.axis_size(FRAME)
    copies = jnp.broadcast_to(mine[None], (parts,) + mine.shape)
    return lax.all_to_all(copies, FRAME, split_axis=0, concat_axis=0)


def line_swapped(pieces):
    parts = lax.axis_size(FRAME)
    place = lax.axis_index(FRAME)
    pick = lambda at: lax.dynamic_index_in_dim(pieces, (place + at) % parts, keepdims=False)
    seen = [pick(0)]
    for far in range(1, parts):
        pairs = [(i, (i + far) % parts) for i in range(parts)]
        seen.append(lax.ppermute(pick(far), FRAME, pairs))
    seen = jnp.stack(seen)
    return jnp.stack(
        [
            lax.dynamic_index_in_dim(seen, (place - source) % parts, keepdims=False)
            for source in range(parts)
        ]
    )


def line_rotated(mine):
    parts = lax.axis_size(FRAME)
    place = lax.axis_index(FRAME)
    seen = [mine]
    for far in range(1, parts):
        seen.append(lax.ppermute(mine, FRAME, [(i, (i + far) % parts) for i in range(parts)]))
    seen = jnp.stack(seen)
    return jnp.stack(
        [
            lax.dynamic_index_in_dim(seen, (place - source) % parts, keepdims=False)
            for source in range(parts)
        ]
    )


def packed(shards):
    groups = lax.axis_size(DP)
    width = min(shard.shape[1] for shard in shards)
    pieces = []
    for shard in shards:
        rows = shard.shape[0] // groups
        piece = lax.dynamic_slice_in_dim(shard, lax.axis_index(DP) * rows, rows)
        pieces.append(stacked(piece, width))
    return jnp.concatenate(pieces, axis=0)


def plane_pieces(column, shards):
    groups, parts = lax.axis_size(DP), lax.axis_size(FRAME)
    whole = lax.all_gather(column, DP, axis=0)
    if shards[0].shape[0] // groups % 8 == 0:
        return whole
    width = whole.shape[-1]
    results, at = [], 0
    for shard in shards:
        stacks = shard.shape[1] // width
        height = stacks * shard.shape[0] // groups
        part = unstacked(whole[:, :, at : at + height], stacks)
        part = jnp.swapaxes(part, 0, 1).reshape(parts * shard.shape[0], shard.shape[1])
        results.append(stacked(part, width))
        at += height
    return jnp.concatenate(results, axis=0)[None, None]


def gathered_small(biases, condition):
    parts = lax.axis_size(FRAME)
    flat = jnp.concatenate(biases + [condition.reshape(-1)])
    rows = line_gathered(flat)
    results, at = [], 0
    for bias in biases:
        results.append(rows[:, at : at + bias.shape[0]].reshape(-1))
        at += bias.shape[0]
    results.append(rows[:, at:].reshape(parts * condition.shape[0], condition.shape[1]))
    return results


def modulated(act_group, matrix, frames):
    parts = lax.axis_size(FRAME)
    rows, width = matrix.shape
    columns = lax.dynamic_slice_in_dim(act_group, lax.axis_index(FRAME) * rows, rows, axis=1)
    return mm(columns, matrix).reshape(parts, frames, width)


def passed_along(x, axis, by):
    peers = lax.axis_size(axis)
    pairs = [(i, i + by) for i in range(peers) if 0 <= i + by < peers]
    return lax.ppermute(x, axis, pairs)


def own_bit(bit):
    return (lax.axis_index(DP) >> bit) & 1


def swapped(x, bit):
    return lax.ppermute(x, DP, [(i, i ^ (1 << bit)) for i in range(lax.axis_size(DP))])


def halved(blocks, bit):
    half = blocks.shape[0] // 2
    mine = own_bit(bit)
    sent = lax.dynamic_slice_in_dim(blocks, (1 - mine) * half, half)
    kept = lax.dynamic_slice_in_dim(blocks, mine * half, half)
    return kept.astype(F32) + swapped(sent, bit).astype(F32)


def summed(pieces):
    return jnp.sum(pieces.astype(F32), axis=0)


def core_order():
    groups = lax.axis_size(DP)
    return [(d & 1) * (groups // 2) + (d >> 1) for d in range(groups)]


def plane_summed(blocks):
    count = blocks.shape[0]
    own = lax.axis_index(DP) >> 1
    pick = lambda at: lax.dynamic_index_in_dim(blocks, at, keepdims=False)
    total = pick(own)
    for far in range(1, count):
        pairs = [(i, i ^ (2 * far)) for i in range(2 * count)]
        total = total + lax.ppermute(pick(own ^ far).astype(BF16), DP, pairs).astype(F32)
    return total


def dp_summed_start(blocks):
    return lax.all_to_all(blocks, DP, split_axis=0, concat_axis=0)


def line_summed(blocks, sent=BF16):
    parts = blocks.shape[0]
    place = lax.axis_index(FRAME)
    pick = lambda at: lax.dynamic_index_in_dim(blocks, (place + at) % parts, keepdims=False)
    total = pick(0)
    for far in range(1, parts):
        pairs = [(i, (i + far) % parts) for i in range(parts)]
        total = total + lax.ppermute(pick(far).astype(sent), FRAME, pairs).astype(F32)
    return total


def plane_gathered(piece):
    groups = lax.axis_size(DP)
    if groups > 8:
        copies = jnp.broadcast_to(piece[None], (groups,) + piece.shape)
        return lax.all_to_all(copies, DP, split_axis=0, concat_axis=0)
    pairs = lambda far: [(i, i ^ far) for i in range(groups)]
    return [piece] + [lax.ppermute(piece, DP, pairs(far)) for far in range(1, groups)]


def in_order(seen):
    if not isinstance(seen, list):
        return seen
    own = lax.axis_index(DP)
    seen = jnp.stack(seen)
    return jnp.stack(
        [lax.dynamic_index_in_dim(seen, own ^ d, keepdims=False) for d in range(len(seen))]
    )


def per_device(
    frames_in,
    condition,
    segments,
    spatial_in,
    spatial_in_bias,
    spatial_out,
    spatial_out_bias,
    temporal_in,
    temporal_in_bias,
    temporal_out,
    temporal_out_bias,
    expand_weight,
    expand_bias,
    shrink_weight,
    shrink_bias,
    modulate_weight,
    modulate_bias,
    cotangent,
):
    groups, parts = lax.axis_size(DP), lax.axis_size(FRAME)
    place = lax.axis_index(FRAME)
    frames, _, width = frames_in.shape
    space, time = [spatial_in, spatial_out], [temporal_in, temporal_out]
    dense = [expand_weight, shrink_weight]
    biases = [
        spatial_in_bias,
        spatial_out_bias,
        temporal_in_bias,
        temporal_out_bias,
        expand_bias,
        shrink_bias,
        modulate_bias,
    ]
    space_column = line_rotated(packed(space))
    time_piece, space_column = lax.optimization_barrier((packed(time), space_column))
    time_column = line_rotated(time_piece)
    *full_biases, cond_group = gathered_small(biases, condition)
    space_raw = plane_pieces(space_column, space)
    sinb, soutb, tinb, toutb, expb, shrb, modb = [b.astype(F32)[None, :] for b in full_biases]
    act_group = jax.nn.silu(cond_group.astype(F32)).astype(BF16)
    partial = modulated(act_group, modulate_weight, frames)
    partial = line_summed(partial, F32)
    mod = (partial + modb).reshape(frames, 9, width)
    time_raw = plane_pieces(time_column, time)
    dense_piece, time_column = lax.optimization_barrier((packed(dense), time_column))
    dense_column = line_rotated(dense_piece)
    dense_raw = plane_pieces(dense_column, dense)
    n1, qkv1, attn1 = spatial_forward(frames_in, mod, space_raw, sinb)
    branch1, after1, n2 = project_forward(frames_in, attn1, mod, space_raw, soutb)
    near_left = passed_along(n2[frames - WINDOW :], FRAME, 1)
    near_right = passed_along(n2[:WINDOW], FRAME, -1)
    qkv2 = temporal_qkv(n2, time_raw, tinb)
    seg_row = segments[0]
    seg_pad = jnp.pad(seg_row, (WINDOW, WINDOW), constant_values=-1)
    nearby = lax.dynamic_slice_in_dim(seg_pad, place * frames, frames + 2 * WINDOW)
    own_seg = nearby[WINDOW : WINDOW + frames]
    allowed = jnp.stack([nearby[o : o + frames] == own_seg for o in range(SPAN)]).astype(jnp.int32)
    probs, attn2, branch2, after2, left, right = temporal_forward(
        allowed, qkv2, near_left, near_right, after1, mod, time_raw, tinb, toutb
    )
    frames_out, g2, n3, act, dpre, db3, dmod3, sum_exp, sum_shr = feed_forward(
        after2, cotangent, mod, dense_raw, expb, shrb
    )
    plain = list(range(groups))
    hidden = dpre.shape[-1]
    high = 2 * (hidden // width) * modulate_weight.shape[0] // groups
    feed = outer_pieces(
        [[(n3, dpre, 0, hidden // width)]], width, groups, parts, plain, total_rows=high
    )
    feed = outer_pieces(
        [[(act, db3, 0, 1)]], width, groups, parts, plain, total_rows=high, into=feed
    )
    feed = lax.psum_scatter(feed.reshape(-1, width), DP, scatter_dimension=0, tiled=True)
    db2, dqkv2, dleft, dright, nleft, nright, dgate2, sum_tout, sum_tin = temporal_backward(
        g2, branch2, mod, time_raw, qkv2, left, right, probs
    )
    from_right = passed_along(nleft, FRAME, -1)
    from_left = passed_along(nright, FRAME, 1)
    order = core_order()
    halo = lambda t: [(near_left, dleft, t, 1), (near_right, dright, t, 1)]
    temporal = outer_pieces(
        [
            [(n2, dqkv2, 0, 1)],
            [(n2, dqkv2, 1, 1)] + halo(0),
            [(n2, dqkv2, 2, 1)] + halo(1),
            [(attn2, db2, 0, 1)],
        ],
        width, groups, parts, order,
    )
    temporal = halved(temporal, 0)
    dqkv2, temporal = lax.optimization_barrier((dqkv2, temporal))
    temporal = plane_summed(temporal)
    g1, db1, da1, dmod1, sum_sout = project_backward(
        dqkv2, from_left, from_right, after1, g2, branch1, mod, time_raw, space_raw
    )
    cond_float = condition.astype(F32)
    own_act = jax.nn.silu(cond_float).astype(BF16)
    early_mod = jnp.concatenate([dmod1, dgate2[:, None], dmod3], axis=1)
    early_mod = early_mod.reshape(frames, 7 * width).astype(BF16)
    early_sums = [s[0] for s in (sum_sout, sum_tin, sum_tout, sum_exp, sum_shr)]
    early_rows = jnp.concatenate(early_sums).astype(BF16).reshape(frames, -1)
    early = jnp.concatenate([own_act, early_mod, early_rows], axis=1)
    dheads, sum_first = heads_backward(qkv1, da1, 0)
    dheads, temporal, feed, early = lax.optimization_barrier((dheads, temporal, feed, early))
    early = line_rotated(early)
    feed = jnp.concatenate([feed.reshape(parts, high, width), temporal.astype(BF16)], axis=1)
    total_high = feed.shape[1]
    feed = lax.psum_scatter(
        feed.reshape(-1, width), FRAME, scatter_dimension=0, tiled=True
    )
    part = width // 2
    first = outer_pieces([[(n1, dheads, 0, 3)], [(attn1, db1, 0, 2)]], part, groups, parts, plain)
    dheads, first, early = lax.optimization_barrier((dheads, first, early))
    early_rows = jnp.sum(early[:, :, 8 * width :].astype(F32), axis=0).astype(BF16)
    early = early[:, :, : 8 * width].reshape(parts * frames, 8 * width)
    early_group = early[:, width:]
    early = jnp.concatenate([early, early_rows.reshape(parts * frames, -1)], axis=1)
    early = lax.all_gather(early, DP, axis=0, tiled=True)
    first = dp_summed_start(first)
    dtail, sum_last, grad_frames, dmod0 = heads_backward(
        qkv1, da1, 1, (dheads, g1, frames_in, mod, space_raw)
    )
    dtail, dmod0, sum_first, sum_last, feed = lax.optimization_barrier(
        (dtail, dmod0, sum_first, sum_last, feed)
    )
    feed = lax.all_gather(feed, DP, axis=0, tiled=True).reshape(groups, total_high, width)
    sums = [s[0].reshape(3, part) for s in (sum_first, sum_last)]
    sum_sin = jnp.stack(sums, axis=1).reshape(1, 3 * width)
    late_mod = dmod0.reshape(frames, 2 * width).astype(BF16)
    late_rows = sum_sin.astype(BF16).reshape(frames, -1)
    late = line_rotated(jnp.concatenate([late_mod, late_rows], axis=1))
    last = outer_pieces([[(n1, dtail, 0, 3)]], part, groups, parts, order)
    last = halved(last, 0)
    first = summed(first)
    last, first, late = lax.optimization_barrier((last, first, late))
    last = plane_summed(last)
    late_rows = jnp.sum(late[:, :, 2 * width :].astype(F32), axis=0).astype(BF16)
    late_group = late[:, :, : 2 * width].reshape(parts * frames, 2 * width)
    both = line_summed(jnp.concatenate([first, last], axis=1))
    sizes = [first.shape[1], last.shape[1], 4 * parts * frames, 3 * width // part]
    sizes = [first.shape[1], last.shape[1], 4 * parts * frames, 3 * width // part]
    piece = [both.astype(BF16), stacked(late_group, part), late_rows.reshape(-1, part)]
    both = plane_gathered(jnp.concatenate(piece, axis=0))
    blocks = lambda whole, count: jnp.split(whole, count, axis=1)
    flat = lambda pieces: jnp.concatenate(
        [p.reshape(-1, p.shape[-1]) for p in pieces], axis=1
    ).astype(F32)
    feed, temporal = feed[:, :high], feed[:, high:]
    *wide, narrow = blocks(temporal, 4)
    grad_temporal_in_sum, grad_temporal_out_sum = flat(wide), flat([narrow])
    wide = unstacked(feed[:, : high // 2], hidden // width)
    grad_expand_sum = wide.reshape(-1, hidden).astype(F32)
    grad_shrink_sum = feed[:, high // 2 :].reshape(-1, width).astype(F32)
    (
        both,
        early,
        grad_temporal_in_sum,
        grad_temporal_out_sum,
        grad_expand_sum,
        grad_shrink_sum,
    ) = lax.optimization_barrier(
        (both, early, grad_temporal_in_sum, grad_temporal_out_sum, grad_expand_sum, grad_shrink_sum)
    )
    rows = modulate_weight.shape[0]
    own_columns = lax.dynamic_slice_in_dim(early[:, :width], place * rows, rows, axis=1)
    early_mod = early[:, width : 8 * width]
    if rows // groups % 8 == 0 and groups <= 8:
        outs = last_outputs(both, own_columns, early_mod, sizes, rows)
        grad_spatial_in_sum, grad_spatial_out_sum, grad_modulate_weight, mod_sum, sin_sum = outs
        mod_sum, sin_sum = mod_sum[0], sin_sum.reshape(-1)
    else:
        cuts = [sum(sizes[: at + 1]) for at in range(3)]
        first, last, late, late_rows = jnp.split(in_order(both), cuts, axis=1)
        starts, ends = blocks(first, 5), blocks(last, 3)
        grad_spatial_in_sum = flat([p for pair in zip(starts[:3], ends) for p in pair])
        grad_spatial_out_sum = flat(starts[3:])
        late_all = unstacked(late, 4).reshape(groups * parts * frames, 2 * width)
        dmod_all = jnp.concatenate([late_all, early_mod], axis=1)
        grad_modulate_weight = mm_tn(own_columns, dmod_all)
        mod_sum = jnp.sum(dmod_all.astype(F32), axis=0)
        sin_sum = jnp.sum(late_rows.astype(F32), axis=0).reshape(-1)
    grad_modulate_bias = own_part(mod_sum)
    dact_group = mm_nt(late_group, modulate_weight[:, : 2 * width])
    dact_group = dact_group + mm_nt(early_group, modulate_weight[:, 2 * width :])
    pieces_act = line_swapped(dact_group.reshape(parts, frames, rows))
    dcond_act = jnp.swapaxes(pieces_act, 0, 1).reshape(frames, parts * rows)
    grad_condition = jax.vjp(jax.nn.silu, cond_float)[1](dcond_act)[0]
    early_rows = early[:, 8 * width :].astype(F32).reshape(groups, parts * frames, -1)
    early_rows = jnp.sum(early_rows, axis=0).reshape(-1)
    bias_sums, at = [own_part(sin_sum)], 0
    for grad in early_sums:
        bias_sums.append(own_part(early_rows[at : at + grad.shape[0]]))
        at += grad.shape[0]
    return (
        frames_out,
        grad_frames,
        grad_condition,
        grad_spatial_in_sum,
        bias_sums[0],
        grad_spatial_out_sum,
        bias_sums[1],
        grad_temporal_in_sum,
        bias_sums[2],
        grad_temporal_out_sum,
        bias_sums[3],
        grad_expand_sum,
        bias_sums[4],
        grad_shrink_sum,
        bias_sums[5],
        grad_modulate_weight,
        grad_modulate_bias,
    )


def solution(mesh):
    in_specs = (
        P((DP, FRAME), None, None),
        P((DP, FRAME), None),
        P(DP, None),
        P(FRAME, None),
        P(FRAME),
        P(FRAME, None),
        P(FRAME),
        P(FRAME, None),
        P(FRAME),
        P(FRAME, None),
        P(FRAME),
        P(FRAME, None),
        P(FRAME),
        P(FRAME, None),
        P(FRAME),
        P(FRAME, None),
        P(FRAME),
        P((DP, FRAME), None, None),
    )
    out_specs = (
        P((DP, FRAME), None, None),
        P((DP, FRAME), None, None),
        P((DP, FRAME), None),
        P(FRAME, None),
        P(FRAME),
        P(FRAME, None),
        P(FRAME),
        P(FRAME, None),
        P(FRAME),
        P(FRAME, None),
        P(FRAME),
        P(FRAME, None),
        P(FRAME),
        P(FRAME, None),
        P(FRAME),
        P(FRAME, None),
        P(FRAME),
    )

    return jax.shard_map(
        per_device, mesh=mesh, in_specs=in_specs, out_specs=out_specs, check_vma=False
    )
```

```python
import functools

import jax
import jax.numpy as jnp
from jax import lax
from jax.experimental import pallas as pl
from jax.experimental.pallas import tpu as pltpu
from jax.sharding import PartitionSpec as P


HEADS = 12
HEAD_DIM = 64
WINDOW = 2
DP = "dp"
FRAME = "frame"

F32 = jnp.float32
BF16 = jnp.bfloat16
SCALE = HEAD_DIM ** (-0.5)
SPAN = 2 * WINDOW + 1


def mm(a, b):
    return lax.dot_general(a, b, (((1,), (0,)), ((), ())), preferred_element_type=F32)


def mm_nt(a, b):
    return lax.dot_general(a, b, (((1,), (1,)), ((), ())), preferred_element_type=F32)


def mm_tn(a, b):
    return lax.dot_general(a, b, (((0,), (0,)), ((), ())), preferred_element_type=F32)


def unit(x):
    centred = x - jnp.mean(x, axis=-1, keepdims=True)
    inv = lax.rsqrt(jnp.mean(centred * centred, axis=-1, keepdims=True) + 1e-06)
    return centred * inv, inv


def unit_back(dn, xhat, inv, scale):
    e = dn * (1.0 + scale)
    first = jnp.mean(e, axis=-1, keepdims=True)
    second = jnp.mean(e * xhat, axis=-1, keepdims=True)
    return inv * (e - first - xhat * second)


def down(x):
    return jnp.sum(x, axis=0, keepdims=True)


def low_half(rows):
    return lax.broadcasted_iota(jnp.int32, (rows, 2 * HEAD_DIM), 1) < HEAD_DIM


def soft(scores):
    e = jnp.exp(scores - jnp.max(scores, axis=-1, keepdims=True))
    return e / jnp.sum(e, axis=-1, keepdims=True)


def params(flops, nbytes, trans=0):
    return dict(
        compiler_params=pltpu.CompilerParams(vmem_limit_bytes=60 * 2**20),
        cost_estimate=pl.CostEstimate(
            flops=int(flops), bytes_accessed=int(nbytes), transcendentals=int(trans)
        ),
    )


def fixed(shape):
    return pl.BlockSpec(shape, lambda *_: (0,) * len(shape), pipeline_mode=pl.Buffered(1))


def per_first(shape):
    return pl.BlockSpec((1,) + shape, lambda i: (i,) + (0,) * len(shape))


def per_second(lead, tile, width):
    return pl.BlockSpec((lead, tile, width), lambda i: (0, i, 0))


def lay_out(raw, whole, first=0):
    @pl.when(pl.program_id(0) == 0)
    def _():
        groups, parts, _, width = raw.shape
        rows = whole.shape[0] // (groups * parts)
        for f in range(parts):
            for d in range(groups):
                at = (f * groups + d) * rows
                for tile in range(whole.shape[1] // width):
                    source = (first + tile) * rows
                    whole[at : at + rows, tile * width : (tile + 1) * width] = raw[
                        d, f, source : source + rows
                    ]


def rows_of(raw, stacks, total, at=0):
    groups, parts, height, width = raw.shape
    return pl.BlockSpec(
        (groups, parts, height * stacks // total, width),
        lambda *_: (0, 0, at, 0),
        pipeline_mode=pl.Buffered(1),
    )


def spatial_kernel(x_ref, mod_ref, raw, bsi, n1_ref, qkv1_ref, attn_ref, wsi):
    lay_out(raw, wsi)
    x = x_ref[0].astype(F32)
    width = x.shape[1]
    xhat, _ = unit(x)
    n1 = (xhat * (1.0 + mod_ref[0, 1:2]) + mod_ref[0, 0:1]).astype(BF16)
    n1_ref[0] = n1
    qkv1_ref[0] = (mm(n1, wsi[...]) + bsi[...]).astype(BF16)
    half = low_half(x.shape[0])
    for pair in range(width // (2 * HEAD_DIM)):
        at = pair * 2 * HEAD_DIM
        q = qkv1_ref[0, :, at : at + 2 * HEAD_DIM]
        k = qkv1_ref[0, :, width + at : width + at + 2 * HEAD_DIM]
        v = qkv1_ref[0, :, 2 * width + at : 2 * width + at + 2 * HEAD_DIM]
        zero = jnp.zeros_like(q)
        first = soft(mm_nt(jnp.where(half, q, zero), k) * SCALE).astype(BF16)
        second = soft(mm_nt(jnp.where(half, zero, q), k) * SCALE).astype(BF16)
        out = jnp.where(half, mm(first, v), mm(second, v))
        attn_ref[0, :, at : at + 2 * HEAD_DIM] = out.astype(BF16)


def spatial_forward(x, mod, space, bsi):
    frames, patches, width = x.shape
    block = lambda n: per_first((patches, n))
    outs = [width, 3 * width, width]
    tokens = frames * patches
    return pl.pallas_call(
        spatial_kernel,
        grid=(frames,),
        in_specs=[
            block(width), per_first(mod.shape[1:]),
            rows_of(space, 1, 1), fixed(bsi.shape),
        ],
        out_specs=[block(n) for n in outs],
        out_shape=[jax.ShapeDtypeStruct((frames, patches, n), BF16) for n in outs],
        scratch_shapes=[pltpu.VMEM((width, 3 * width), BF16)],
        name="spatial_forward",
        **params(2 * tokens * width * (3 * width + 4 * patches), 12e6, tokens * patches * HEADS),
    )(x, mod, space, bsi)


def project_kernel(x_ref, attn_ref, mod_ref, raw, bso, branch_ref, after_ref, n2_ref, wso):
    lay_out(raw, wso)
    branch = mm(attn_ref[0], wso[...]) + bso[...]
    branch_ref[0] = branch
    after = x_ref[0].astype(F32) + mod_ref[0, 2:3] * branch
    after_ref[0] = after
    xhat, _ = unit(after)
    n2_ref[0] = (xhat * (1.0 + mod_ref[0, 4:5]) + mod_ref[0, 3:4]).astype(BF16)


def project_forward(x, attn, mod, time, bso):
    frames, patches, width = x.shape
    block = per_first((patches, width))
    tokens = frames * patches
    return pl.pallas_call(
        project_kernel,
        grid=(frames,),
        in_specs=[
            block, block, per_first(mod.shape[1:]), rows_of(time, 1, 5, 4), fixed(bso.shape)
        ],
        scratch_shapes=[pltpu.VMEM((width, width), BF16)],
        out_specs=[block] * 3,
        out_shape=[jax.ShapeDtypeStruct(x.shape, t) for t in (F32, F32, BF16)],
        name="project_forward",
        **params(2 * tokens * width * width, 13e6),
    )(x, attn, mod, time, bso)


def qkv_kernel(n_ref, raw, bias, out_ref, whole):
    lay_out(raw, whole)
    out_ref[0] = (mm(n_ref[0], whole[...]) + bias[...]).astype(BF16)


def temporal_qkv(n, time, bias):
    frames, patches, width = n.shape
    tokens = frames * patches
    return pl.pallas_call(
        qkv_kernel,
        grid=(frames,),
        in_specs=[per_first((patches, width)), rows_of(time, 3, 5), fixed(bias.shape)],
        out_specs=per_first((patches, 3 * width)),
        out_shape=jax.ShapeDtypeStruct((frames, patches, 3 * width), BF16),
        scratch_shapes=[pltpu.VMEM((width, 3 * width), BF16)],
        name="temporal_qkv",
        **params(6 * tokens * width * width, 10e6),
    )(n, time, bias)


def ext_rows(e, frames, left, own, right, base, width):
    if e < WINDOW:
        return left[e, :, base - width : base]
    if e < WINDOW + frames:
        return own[e - WINDOW, :, base : base + width]
    return right[e - WINDOW - frames, :, base - width : base]


def head_sums(prod_ref, first, count, ones):
    tile, width = prod_ref.shape[1:]
    return mm(prod_ref[first : first + count].reshape(count * tile, width), ones)


def temporal_kernel(
    allowed, qkv_ref, nl_ref, nr_ref, after_ref, mod_ref, raw_in, bti, raw_out, bto, ones, ones_t,
    probs_ref, attn_ref, branch_ref, out_ref, left_ref, right_ref, prod_ref, wkv, wto,
):
    frames, tile, width = after_ref.shape
    lay_out(raw_in, wkv, 1)
    lay_out(raw_out, wto)
    for near, kv_ref in ((nl_ref, left_ref), (nr_ref, right_ref)):
        kv = mm(near[...].reshape(WINDOW * tile, width), wkv[...]) + bti[:, width:]
        kv_ref[...] = kv.astype(BF16).reshape(WINDOW, tile, 2 * width)
    for t in range(frames):
        q = qkv_ref[t, :, :width].astype(F32)
        for o in range(SPAN):
            k = ext_rows(t + o, frames, left_ref, qkv_ref, right_ref, width, width)
            prod_ref[t * SPAN + o] = (q * k.astype(F32)).astype(BF16)
    for t in range(frames):
        raw = head_sums(prod_ref, t * SPAN, SPAN, ones[...]) * SCALE
        raw = [
            jnp.where(allowed[o, t] > 0, raw[o * tile : (o + 1) * tile], -1e30)
            for o in range(SPAN)
        ]
        top = raw[0]
        for o in range(1, SPAN):
            top = jnp.maximum(top, raw[o])
        expo = [jnp.exp(r - top) for r in raw]
        total = expo[0]
        for o in range(1, SPAN):
            total = total + expo[o]
        inv = 1.0 / total
        probs = [e * inv for e in expo]
        for o in range(SPAN):
            probs_ref[t, o] = probs[o]
        wide = mm(jnp.concatenate(probs, axis=0).astype(BF16), ones_t[...])
        total = None
        for o in range(SPAN):
            v = ext_rows(t + o, frames, left_ref, qkv_ref, right_ref, 2 * width, width)
            term = wide[o * tile : (o + 1) * tile] * v.astype(F32)
            total = term if total is None else total + term
        attn_ref[t] = total.astype(BF16)
    branch = mm(attn_ref[...].reshape(frames * tile, width), wto[...]) + bto[...]
    for t in range(frames):
        part = branch[t * tile : (t + 1) * tile]
        branch_ref[t] = part
        out_ref[t] = after_ref[t] + mod_ref[t, 5:6] * part


def head_ones(width):
    head = jnp.arange(width, dtype=jnp.int32)[:, None] // HEAD_DIM
    return (head == jnp.arange(128, dtype=jnp.int32)[None, :]).astype(BF16)


def temporal_forward(allowed, qkv, near_left, near_right, after, mod, time, bti, bto):
    frames, patches, width = after.shape
    tile = 64
    ones = head_ones(width)
    spec = lambda n: per_second(frames, tile, n)
    halo = per_second(WINDOW, tile, 2 * width)
    near = per_second(WINDOW, tile, width)
    shape = lambda t: jax.ShapeDtypeStruct((frames, patches, width), t)
    tokens = frames * patches
    return pl.pallas_call(
        temporal_kernel,
        grid=(patches // tile,),
        in_specs=[
            pl.BlockSpec(memory_space=pltpu.SMEM),
            spec(3 * width), near, near, spec(width), fixed(mod.shape),
            rows_of(time, 3, 5), fixed(bti.shape), rows_of(time, 1, 5, 3), fixed(bto.shape),
            fixed(ones.shape), fixed(ones.shape[::-1]),
        ],
        out_specs=[
            pl.BlockSpec((frames, SPAN, tile, 128), lambda i: (0, 0, i, 0)),
            spec(width), spec(width), spec(width), halo, halo,
        ],
        out_shape=[
            jax.ShapeDtypeStruct((frames, SPAN, patches, 128), F32),
            shape(BF16), shape(F32), shape(F32),
            jax.ShapeDtypeStruct((WINDOW, patches, 2 * width), BF16),
            jax.ShapeDtypeStruct((WINDOW, patches, 2 * width), BF16),
        ],
        scratch_shapes=[pltpu.VMEM((frames * SPAN, tile, width), BF16)]
        + [pltpu.VMEM((width, 2 * width), BF16), pltpu.VMEM((width, width), BF16)],
        name="temporal_forward",
        **params(2 * tokens * width * (width + SPAN * 400), 22e6, tokens * SPAN * 128),
    )(allowed, qkv, near_left, near_right, after, mod, time, bti, time, bto, ones, ones.T)


def feed_kernel(
    after_ref, cot_ref, mod_ref, raw1, b1, raw2, b2,
    out_ref, g_ref, n_ref, act_ref, dpre_ref, db_ref, dmod_ref, sum1_ref, sum2_ref, w1, w2,
):
    lay_out(raw1, w1)
    lay_out(raw2, w2)
    after = after_ref[0]
    width = after.shape[1]
    hidden = w1.shape[1]
    xhat, inv = unit(after)
    scale = mod_ref[0, 7:8]
    gate = mod_ref[0, 8:9]
    n = (xhat * (1.0 + scale) + mod_ref[0, 6:7]).astype(BF16)
    n_ref[0] = n
    g3 = cot_ref[0].astype(F32)
    db = (gate * g3).astype(BF16)
    db_ref[0] = db

    @pl.when(pl.program_id(0) == 0)
    def _():
        sum1_ref[...] = jnp.zeros_like(sum1_ref)
        sum2_ref[...] = jnp.zeros_like(sum2_ref)

    sum2_ref[...] += down(db.astype(F32))
    branch = jnp.zeros_like(after)
    dn = jnp.zeros_like(after)
    chunk = width
    for c in range(hidden // chunk):
        cols = slice(c * chunk, (c + 1) * chunk)
        pre = mm(n, w1[:, cols]) + b1[:, cols]
        dact = mm_nt(db, w2[cols, :])
        phi = 0.5 * (1.0 + lax.erf(pre * 0.7071067811865476))
        act = (pre * phi).astype(BF16)
        slope = phi + pre * (jnp.exp(-0.5 * pre * pre) * 0.3989422804014327)
        dpre = (dact * slope).astype(BF16)
        act_ref[0, :, cols] = act
        dpre_ref[0, :, cols] = dpre
        sum1_ref[:, cols] += down(dpre.astype(F32))
        branch += mm(act, w2[cols, :])
        dn += mm_nt(dpre, w1[:, cols])
    branch = branch + b2[...]
    out_ref[0] = (after + gate * branch).astype(BF16)
    dmod_ref[0, 0:1] = down(dn)
    dmod_ref[0, 1:2] = down(dn * xhat)
    dmod_ref[0, 2:3] = down(g3 * branch)
    g_ref[0] = g3 + unit_back(dn, xhat, inv, scale)


def feed_forward(after, cot, mod, dense, b1, b2):
    frames, patches, width = after.shape
    hidden = b1.shape[1]
    shape = lambda n, t: jax.ShapeDtypeStruct((frames, patches, n), t)
    block = lambda n: per_first((patches, n))
    outs = [(width, BF16), (width, F32), (width, BF16), (hidden, BF16), (hidden, BF16), (width, BF16)]
    tokens = frames * patches
    return pl.pallas_call(
        feed_kernel,
        grid=(frames,),
        in_specs=[
            block(width), block(width), per_first(mod.shape[1:]),
            rows_of(dense, 1, 2), fixed(b1.shape), rows_of(dense, 1, 2, 1), fixed(b2.shape),
        ],
        scratch_shapes=[pltpu.VMEM((width, hidden), BF16), pltpu.VMEM((hidden, width), BF16)],
        out_specs=[block(n) for n, _ in outs]
        + [per_first((3, width)), pl.BlockSpec((1, hidden), lambda i: (0, 0)),
           pl.BlockSpec((1, width), lambda i: (0, 0))],
        out_shape=[shape(n, t) for n, t in outs]
        + [jax.ShapeDtypeStruct((frames, 3, width), F32),
           jax.ShapeDtypeStruct((1, hidden), F32), jax.ShapeDtypeStruct((1, width), F32)],
        name="feed_forward",
        **params(8 * tokens * width * hidden, 32e6, 2 * tokens * hidden),
    )(after, cot, mod, dense, b1, dense, b2)


def temporal_back_kernel(
    g_ref, branch_ref, mod_ref, raw_out, raw_in, qkv_ref, left_ref, right_ref, probs_ref, ones, ones_t,
    db_ref, dqkv_ref, dleft_ref, dright_ref, nleft_ref, nright_ref, dgate_ref, sum_ref, sumq_ref,
    prod_ref, da_ref, ds_ref, pw_ref, wkv, wto,
):
    frames, tile, width = g_ref.shape
    lay_out(raw_in, wkv, 1)
    lay_out(raw_out, wto)

    @pl.when(pl.program_id(0) == 0)
    def _():
        dgate_ref[...] = jnp.zeros_like(dgate_ref)
        sum_ref[...] = jnp.zeros_like(sum_ref)
        sumq_ref[...] = jnp.zeros_like(sumq_ref)

    for t in range(frames):
        g = g_ref[t]
        dgate_ref[t : t + 1] += down(g * branch_ref[t])
        db = (mod_ref[t, 5:6] * g).astype(BF16)
        db_ref[t] = db
        sum_ref[...] += down(db.astype(F32))
    da_all = mm_nt(db_ref[...].reshape(frames * tile, width), wto[...]).astype(BF16)
    da_ref[...] = da_all.reshape(frames, tile, width)
    for t in range(frames):
        da = da_ref[t].astype(F32)
        for o in range(SPAN):
            v = ext_rows(t + o, frames, left_ref, qkv_ref, right_ref, 2 * width, width)
            prod_ref[t * SPAN + o] = (da * v.astype(F32)).astype(BF16)
    for t in range(frames):
        dp = head_sums(prod_ref, t * SPAN, SPAN, ones[...])
        probs = probs_ref[t].reshape(SPAN * tile, 128)
        both = probs * dp
        dot = both[:tile]
        for o in range(1, SPAN):
            dot = dot + both[o * tile : (o + 1) * tile]
        ds = both - probs * jnp.concatenate([dot] * SPAN, axis=0)
        wide = mm(ds.astype(BF16), ones_t[...]).astype(BF16)
        ds_ref[t * SPAN : (t + 1) * SPAN] = wide.reshape(SPAN, tile, width)
        wide = mm(probs.astype(BF16), ones_t[...]).astype(BF16)
        pw_ref[t * SPAN : (t + 1) * SPAN] = wide.reshape(SPAN, tile, width)
    for t in range(frames):
        total = None
        for o in range(SPAN):
            k = ext_rows(t + o, frames, left_ref, qkv_ref, right_ref, width, width)
            term = ds_ref[t * SPAN + o].astype(F32) * k.astype(F32)
            total = term if total is None else total + term
        dqkv_ref[t, :, :width] = (total * SCALE).astype(BF16)
    for e in range(frames + 2 * WINDOW):
        dk = dv = None
        for t in range(max(0, e - SPAN + 1), min(frames, e + 1)):
            row = t * SPAN + e - t
            q = qkv_ref[t, :, :width].astype(F32)
            term = ds_ref[row].astype(F32) * q
            dk = term if dk is None else dk + term
            term = pw_ref[row].astype(F32) * da_ref[t].astype(F32)
            dv = term if dv is None else dv + term
        dk = (dk * SCALE).astype(BF16)
        dv = dv.astype(BF16)
        if e < WINDOW:
            dleft_ref[e, :, :width] = dk
            dleft_ref[e, :, width:] = dv
        elif e < WINDOW + frames:
            dqkv_ref[e - WINDOW, :, width : 2 * width] = dk
            dqkv_ref[e - WINDOW, :, 2 * width :] = dv
        else:
            dright_ref[e - WINDOW - frames, :, :width] = dk
            dright_ref[e - WINDOW - frames, :, width:] = dv
    for dkv_ref, near_ref in ((dleft_ref, nleft_ref), (dright_ref, nright_ref)):
        flat = dkv_ref[...].reshape(WINDOW * tile, 2 * width)
        sumq_ref[:, width:] += down(flat.astype(F32))
        near_ref[...] = mm_nt(flat, wkv[...]).astype(BF16).reshape(WINDOW, tile, width)
    sumq_ref[...] += down(dqkv_ref[...].reshape(frames * tile, 3 * width).astype(F32))


def temporal_backward(g, branch, mod, time, qkv, left, right, probs):
    frames, patches, width = g.shape
    tile = 64
    ones = head_ones(width)
    spec = lambda n: per_second(frames, tile, n)
    halo = per_second(WINDOW, tile, 2 * width)
    near = per_second(WINDOW, tile, width)
    shape = lambda f, n, t: jax.ShapeDtypeStruct((f, patches, n), t)
    tokens = frames * patches
    return pl.pallas_call(
        temporal_back_kernel,
        grid=(patches // tile,),
        in_specs=[
            spec(width), spec(width), fixed(mod.shape), rows_of(time, 1, 5, 3), rows_of(time, 3, 5),
            spec(3 * width), halo, halo,
            pl.BlockSpec((frames, SPAN, tile, 128), lambda i: (0, 0, i, 0)),
            fixed(ones.shape), fixed(ones.shape[::-1]),
        ],
        out_specs=[
            spec(width), spec(3 * width), halo, halo, near, near,
            pl.BlockSpec((frames, width), lambda i: (0, 0)),
            pl.BlockSpec((1, width), lambda i: (0, 0)),
            pl.BlockSpec((1, 3 * width), lambda i: (0, 0)),
        ],
        out_shape=[
            shape(frames, width, BF16), shape(frames, 3 * width, BF16),
            shape(WINDOW, 2 * width, BF16), shape(WINDOW, 2 * width, BF16),
            shape(WINDOW, width, BF16), shape(WINDOW, width, BF16),
            jax.ShapeDtypeStruct((frames, width), F32), jax.ShapeDtypeStruct((1, width), F32),
            jax.ShapeDtypeStruct((1, 3 * width), F32),
        ],
        scratch_shapes=[pltpu.VMEM((frames * SPAN, tile, width), BF16)]
        + [pltpu.VMEM((frames, tile, width), BF16)]
        + [pltpu.VMEM((frames * SPAN, tile, width), BF16)] * 2
        + [pltpu.VMEM((width, 2 * width), BF16), pltpu.VMEM((width, width), BF16)],
        name="temporal_backward",
        **params(2 * tokens * width * (width + SPAN * 500), 36e6),
    )(g, branch, mod, time, time, qkv, left, right, probs, ones, ones.T)


def project_back_kernel(
    dqkv_ref, fl_ref, fr_ref, after_ref, g2_ref, branch_ref, mod_ref, raw_in, raw_out,
    g_ref, db_ref, da_ref, dmod_ref, sum_ref, wti, wso,
):
    lay_out(raw_in, wti)
    lay_out(raw_out, wso)
    at = pl.program_id(0)

    @pl.when(at == 0)
    def _():
        sum_ref[...] = jnp.zeros_like(sum_ref)

    dn = mm_nt(dqkv_ref[0], wti[...]) + jnp.where(at < WINDOW, fl_ref[0].astype(F32), fr_ref[0].astype(F32))
    xhat, inv = unit(after_ref[0])
    dmod_ref[0, 1:2] = down(dn)
    dmod_ref[0, 2:3] = down(dn * xhat)
    g1 = g2_ref[0] + unit_back(dn, xhat, inv, mod_ref[0, 4:5])
    dmod_ref[0, 0:1] = down(g1 * branch_ref[0])
    g_ref[0] = g1
    db = (mod_ref[0, 2:3] * g1).astype(BF16)
    db_ref[0] = db
    sum_ref[...] += down(db.astype(F32))
    da_ref[0] = mm_nt(db, wso[...]).astype(BF16)


def project_backward(dqkv2, from_left, from_right, after, g2, branch, mod, time):
    frames, patches, width = after.shape
    block = per_first((patches, width))
    tokens = frames * patches
    return pl.pallas_call(
        project_back_kernel,
        grid=(frames,),
        in_specs=[
            per_first((patches, 3 * width)),
            pl.BlockSpec((1, patches, width), lambda i: (jnp.minimum(i, WINDOW - 1), 0, 0)),
            pl.BlockSpec((1, patches, width), lambda i: (jnp.maximum(i - WINDOW, 0), 0, 0)),
            block, block, block, per_first(mod.shape[1:]), rows_of(time, 3, 5), rows_of(time, 1, 5, 4),
        ],
        scratch_shapes=[pltpu.VMEM((width, 3 * width), BF16), pltpu.VMEM((width, width), BF16)],
        out_specs=[block, block, block, per_first((3, width)),
                   pl.BlockSpec((1, width), lambda i: (0, 0))],
        out_shape=[jax.ShapeDtypeStruct(after.shape, t) for t in (F32, BF16, BF16)]
        + [jax.ShapeDtypeStruct((frames, 3, width), F32), jax.ShapeDtypeStruct((1, width), F32)],
        name="project_backward",
        **params(8 * tokens * width * width, 24e6),
    )(dqkv2, from_left, from_right, after, g2, branch, mod, time, time)


def heads_back(q_ref, k_ref, v_ref, da_ref, out_ref, sum_ref):
    tokens, width = q_ref.shape[1:]

    @pl.when(pl.program_id(0) == 0)
    def _():
        sum_ref[...] = jnp.zeros_like(sum_ref)

    half = low_half(tokens)
    for pair in range(width // (2 * HEAD_DIM)):
        cols = slice(pair * 2 * HEAD_DIM, (pair + 1) * 2 * HEAD_DIM)
        q, k, v, da = (ref[0, :, cols] for ref in (q_ref, k_ref, v_ref, da_ref))
        zero = jnp.zeros_like(q)
        parts = []
        for side in range(2):
            pick = (lambda u: jnp.where(half, u, zero)) if side == 0 else (
                lambda u: jnp.where(half, zero, u))
            probs = soft(mm_nt(pick(q), k) * SCALE)
            dp = mm_nt(pick(da), v)
            both = probs * dp
            ds = (both - probs * jnp.sum(both, axis=-1, keepdims=True)).astype(BF16)
            parts.append((mm(ds, k), mm_tn(ds, q), mm_tn(probs.astype(BF16), da)))
        grads = [jnp.where(half, a, b) for a, b in zip(*parts)]
        for at, grad in enumerate((grads[0] * SCALE, grads[1] * SCALE, grads[2])):
            out_ref[0, :, at * width + cols.start : at * width + cols.stop] = grad.astype(BF16)
    sum_ref[...] += down(out_ref[0].astype(F32))


def first_heads_kernel(q_ref, k_ref, v_ref, da_ref, out_ref, sum_ref):
    heads_back(q_ref, k_ref, v_ref, da_ref, out_ref, sum_ref)


def last_heads_kernel(
    q_ref, k_ref, v_ref, da_ref, first_ref, g_ref, x_ref, mod_ref, raw,
    out_ref, sum_ref, grad_ref, dmod_ref, wsi,
):
    lay_out(raw, wsi)
    heads_back(q_ref, k_ref, v_ref, da_ref, out_ref, sum_ref)
    width = q_ref.shape[2]
    dn = None
    for at in range(3):
        for side, ref in enumerate((first_ref, out_ref)):
            cols = slice((2 * at + side) * width, (2 * at + side + 1) * width)
            term = mm_nt(ref[0, :, at * width : (at + 1) * width], wsi[:, cols])
            dn = term if dn is None else dn + term
    xhat, inv = unit(x_ref[0].astype(F32))
    dmod_ref[0, 0:1] = down(dn)
    dmod_ref[0, 1:2] = down(dn * xhat)
    grad_ref[0] = g_ref[0] + unit_back(dn, xhat, inv, mod_ref[0, 1:2])


def heads_backward(qkv1, da1, side, rest=None):
    frames, patches, width = da1.shape
    part = width // 2
    column = lambda at: pl.BlockSpec((1, patches, part), lambda i: (i, 0, at))
    block = lambda n: per_first((patches, n))
    tokens = frames * patches
    in_specs = [column(side), column(2 + side), column(4 + side), column(side)]
    operands = [qkv1, qkv1, qkv1, da1]
    out_specs = [block(3 * part), pl.BlockSpec((1, 3 * part), lambda i: (0, 0))]
    out_shape = [
        jax.ShapeDtypeStruct((frames, patches, 3 * part), BF16),
        jax.ShapeDtypeStruct((1, 3 * part), F32),
    ]
    scratch = []
    if rest is not None:
        first, g1, x, mod, space = rest
        in_specs += [block(3 * part), block(width), block(width), per_first(mod.shape[1:]),
                     rows_of(space, 1, 1)]
        operands += [first, g1, x, mod, space]
        scratch = [pltpu.VMEM((width, 3 * width), BF16)]
        out_specs += [block(width), per_first((2, width))]
        out_shape += [
            jax.ShapeDtypeStruct((frames, patches, width), F32),
            jax.ShapeDtypeStruct((frames, 2, width), F32),
        ]
    return pl.pallas_call(
        first_heads_kernel if rest is None else last_heads_kernel,
        grid=(frames,),
        in_specs=in_specs,
        out_specs=out_specs,
        out_shape=out_shape,
        scratch_shapes=scratch,
        name="first_heads_backward" if rest is None else "last_heads_backward",
        **params(2 * tokens * width * (5 * patches + (0 if rest is None else 3 * width)),
                 16e6, tokens * patches * HEADS // 2),
    )(*operands)


def outer_kernel(*refs, jobs, order, split):
    refs, out_refs = (refs[:-2], refs[-2:]) if split else (refs[:-1], refs[-1:])
    parts, width = out_refs[0].shape[1], out_refs[0].shape[3]
    groups = len(order)
    top = 0
    turned = {}
    for terms in jobs:
        total = None
        for left, right in terms:
            if left not in turned:
                turned[left] = refs[left][...].T
            term = mm(turned[left], refs[right][...])
            total = term if total is None else total + term
        rows = total.shape[0] // (groups * parts)

        def write(first, total=total, top=top):
            for tile in range(total.shape[1] // width):
                for f in range(parts):
                    for d in range(groups):
                        row = (f * groups + d) * rows
                        at = order[d]
                        ref = out_refs[0]
                        if split:
                            ref = out_refs[at // (groups // 2) ^ first]
                            at = at % (groups // 2)
                        ref[at, f, top + tile * rows : top + (tile + 1) * rows] = total[
                            row : row + rows, tile * width : (tile + 1) * width
                        ].astype(BF16)

        if split:
            core = refs[-1][0]
            pl.when(core == 0)(functools.partial(write, 0))
            pl.when(core == 1)(functools.partial(write, 1))
        else:
            write(0)
        top += rows * (total.shape[1] // width)


def outer_pieces(jobs, width, groups, parts, order, total_rows=None, into=None, core=None):
    shaped = {}

    def flat(a):
        return shaped.setdefault(id(a), a.reshape(-1, a.shape[-1]))

    jobs = [[(flat(left), flat(right), *tiles) for left, right, *tiles in job] for job in jobs]
    depth = jobs[0][0][0].shape[1]
    rows = depth // (groups * parts)
    height = sum(job[0][3] for job in jobs) * rows
    total_rows = total_rows or height
    if rows % 8:
        pieces = [] if into is None else [into[:, :, : total_rows - height]]
        for job in jobs:
            for tile in range(job[0][3]):
                cut = lambda r, t: r[:, (t + tile) * width : (t + tile + 1) * width]
                total = sum(mm_tn(l, cut(r, t)) for l, r, t, _ in job)
                total = total.astype(BF16).reshape(parts, groups, rows, width).swapaxes(0, 1)
                pieces.append(jnp.stack([total[order.index(d)] for d in range(groups)]))
        whole = jnp.concatenate(pieces, axis=2)
        whole = jnp.pad(whole, ((0, 0), (0, 0), (0, total_rows - whole.shape[2]), (0, 0)))
        if core is None:
            return whole
        half = groups // 2
        part = lambda number: lax.dynamic_slice_in_dim(whole, number * half, half)
        return part(core), part(1 - core)
    step = 1
    while (step * depth // parts) % 128:
        step *= 2
    specs, operands, flops, known, terms = [], [], 0, {}, []

    def operand(array, spec, key):
        if key not in known:
            known[key] = len(operands)
            operands.append(array)
            specs.append(spec)
        return known[key]

    for job in jobs:
        pairs = []
        for left, right, tile, tiles in job:
            tokens = left.shape[0]
            spec = pl.BlockSpec((tokens, step * depth // parts), lambda i: (0, i))
            first = operand(left, spec, (id(left), None))
            spec = pl.BlockSpec(
                (tokens, tiles * width),
                lambda i, at=tile // tiles: (0, at),
                pipeline_mode=pl.Buffered(1),
            )
            pairs.append((first, operand(right, spec, (id(right), tile, tiles))))
            flops += 2 * tokens * depth * width * tiles
        terms.append(tuple(pairs))
    place = 0
    aliases = {}
    if into is not None:
        place = total_rows // height - 1
        aliases = {len(operands): 0}
        specs.append(pl.BlockSpec(memory_space=pl.ANY))
        operands.append(into)
    split = core is not None
    if split:
        specs.append(pl.BlockSpec(memory_space=pltpu.SMEM))
        operands.append(core.reshape(1))
    lead = groups // 2 if split else groups
    spec = pl.BlockSpec((lead, step, height, width), lambda i: (0, i, place, 0))
    shape = jax.ShapeDtypeStruct((lead, parts, total_rows, width), BF16)
    return pl.pallas_call(
        functools.partial(outer_kernel, jobs=tuple(terms), order=tuple(order), split=split),
        grid=(parts // step,),
        in_specs=specs,
        out_specs=[spec] * 2 if split else spec,
        out_shape=[shape] * 2 if split else shape,
        input_output_aliases=aliases,
        name="outer_pieces",
        **params(flops, 12e6),
    )(*operands)


def last_kernel(own_ref, *refs, sizes):
    groups = len(refs) - 9
    pieces, (columns, early) = refs[:groups], refs[groups : groups + 2]
    in_ref, out_ref, mod_ref, sum_ref, bias_ref, late_ref, turned = refs[groups + 2 :]
    part = pieces[0].shape[1]
    rows = in_ref.shape[0] // groups
    tall = sizes[2] // 4
    begin = sizes[0] + sizes[1]
    bias = None
    for far, piece in enumerate(pieces):
        d = own_ref[0] ^ far
        there = pl.ds(pl.multiple_of(d * rows, 8), rows)
        for at in range(3):
            for side, top in enumerate((0, sizes[0])):
                column = (2 * at + side) * part
                in_ref[there, column : column + part] = piece[
                    top + at * rows : top + (at + 1) * rows
                ].astype(F32)
        for at in range(2):
            source = (3 + at) * rows
            out_ref[there, at * part : (at + 1) * part] = piece[source : source + rows].astype(F32)
        there = pl.ds(pl.multiple_of(d * tall, 16), tall)
        for at in range(4):
            source = begin + at * tall
            late_ref[there, at * part : (at + 1) * part] = piece[source : source + tall]
        term = piece[begin + sizes[2] : begin + sizes[2] + sizes[3]].astype(F32)
        bias = term if bias is None else bias + term
    bias_ref[...] = bias
    turned[...] = columns[...].T
    wide = 4 * part
    mod_ref[:, :wide] = mm(turned[...], late_ref[...])
    sum_ref[:, :wide] = down(late_ref[...].astype(F32))
    for at in range(early.shape[1] // wide + 1):
        cols = slice(at * wide, min((at + 1) * wide, early.shape[1]))
        mod_ref[:, wide + cols.start : wide + cols.stop] = mm(turned[...], early[:, cols])
        sum_ref[:, wide + cols.start : wide + cols.stop] = down(early[:, cols].astype(F32))


def last_outputs(pieces, columns, early, sizes, rows):
    part = pieces[0].shape[1]
    tokens, more = early.shape
    total = more + 4 * part
    shapes = [(rows, 6 * part), (rows, 2 * part), (rows, total), (1, total), (sizes[3], part)]
    own = lax.axis_index(DP).reshape(1)
    whole = pl.BlockSpec(memory_space=pltpu.VMEM)
    return pl.pallas_call(
        functools.partial(last_kernel, sizes=tuple(sizes)),
        in_specs=[pl.BlockSpec(memory_space=pltpu.SMEM)] + [whole] * (len(pieces) + 2),
        out_specs=[whole] * 5,
        out_shape=[jax.ShapeDtypeStruct(s, F32) for s in shapes],
        scratch_shapes=[
            pltpu.VMEM((tokens, 4 * part), BF16), pltpu.VMEM((rows, tokens), BF16),
        ],
        name="last_outputs",
        **params(2 * rows * tokens * total, 12e6),
    )(own, *pieces, columns, early)


def feed_outputs_kernel(
    piece, expand_ref, shrink_ref, in_ref, out_ref, act_ref, mod_ref, sum_ref
):
    width = piece.shape[2]
    at = 0
    for ref in (expand_ref, shrink_ref, in_ref, out_ref, act_ref, mod_ref):
        height = ref.shape[0]
        for tile in range(ref.shape[1] // width):
            block = piece[0, at : at + height]
            ref[:, tile * width : (tile + 1) * width] = block.astype(ref.dtype)
            at += height

    @pl.when(pl.program_id(0) == 0)
    def _():
        sum_ref[...] = jnp.zeros_like(sum_ref)

    sum_ref[...] += piece[0, at:].astype(F32)


def feed_outputs(feed, hidden, rows, tall):
    groups, height, width = feed.shape
    more = hidden // width
    shapes = [
        (rows, hidden, F32), (more * rows, width, F32), (rows, 3 * width, F32), (rows, width, F32),
        (tall, width, BF16), (tall, 7 * width, BF16),
    ]
    left = height - 2 * more * rows - 4 * rows - 8 * tall
    return pl.pallas_call(
        feed_outputs_kernel,
        grid=(groups,),
        in_specs=[pl.BlockSpec((1, height, width), lambda d: (d, 0, 0))],
        out_specs=[pl.BlockSpec((h, w), lambda d: (d, 0)) for h, w, _ in shapes]
        + [pl.BlockSpec((left, width), lambda d: (0, 0))],
        out_shape=[jax.ShapeDtypeStruct((groups * h, w), t) for h, w, t in shapes]
        + [jax.ShapeDtypeStruct((left, width), F32)],
        name="feed_outputs",
        **params(0, 15e6),
    )(feed)


def own_part(vector):
    size = vector.shape[0] // lax.axis_size(FRAME)
    return lax.dynamic_slice_in_dim(vector, lax.axis_index(FRAME) * size, size)


def stacked(block, width):
    count = block.shape[-1] // width
    return jnp.concatenate(
        [block[..., k * width : (k + 1) * width] for k in range(count)], axis=-2
    )


def unstacked(block, count):
    rows = block.shape[-2] // count
    return jnp.concatenate(
        [block[..., k * rows : (k + 1) * rows, :] for k in range(count)], axis=-1
    )


def line_gathered(mine):
    parts = lax.axis_size(FRAME)
    copies = jnp.broadcast_to(mine[None], (parts,) + mine.shape)
    return lax.all_to_all(copies, FRAME, split_axis=0, concat_axis=0)


def line_swapped(pieces):
    parts = lax.axis_size(FRAME)
    place = lax.axis_index(FRAME)
    pick = lambda at: lax.dynamic_index_in_dim(pieces, (place + at) % parts, keepdims=False)
    seen = [pick(0)]
    for far in range(1, parts):
        pairs = [(i, (i + far) % parts) for i in range(parts)]
        seen.append(lax.ppermute(pick(far), FRAME, pairs))
    seen = jnp.stack(seen)
    return jnp.stack(
        [
            lax.dynamic_index_in_dim(seen, (place - source) % parts, keepdims=False)
            for source in range(parts)
        ]
    )


def line_rotated(mine):
    parts = lax.axis_size(FRAME)
    place = lax.axis_index(FRAME)
    seen = [mine]
    for far in range(1, parts):
        seen.append(lax.ppermute(mine, FRAME, [(i, (i + far) % parts) for i in range(parts)]))
    seen = jnp.stack(seen)
    return jnp.stack(
        [
            lax.dynamic_index_in_dim(seen, (place - source) % parts, keepdims=False)
            for source in range(parts)
        ]
    )


def packed(shards, width):
    groups = lax.axis_size(DP)
    pieces = []
    for shard in shards:
        rows = shard.shape[0] // groups
        piece = lax.dynamic_slice_in_dim(shard, lax.axis_index(DP) * rows, rows)
        pieces.append(stacked(piece, width))
    return jnp.concatenate(pieces, axis=0)


def plane_pieces(column, shards):
    groups, parts = lax.axis_size(DP), lax.axis_size(FRAME)
    whole = lax.all_gather(column, DP, axis=0)
    if shards[0].shape[0] // groups % 8 == 0:
        return whole
    width = whole.shape[-1]
    results, at = [], 0
    for shard in shards:
        stacks = shard.shape[1] // width
        height = stacks * shard.shape[0] // groups
        part = unstacked(whole[:, :, at : at + height], stacks)
        part = jnp.swapaxes(part, 0, 1).reshape(parts * shard.shape[0], shard.shape[1])
        results.append(stacked(part, width))
        at += height
    return jnp.concatenate(results, axis=0)[None, None]


def gathered_small(biases, condition):
    parts = lax.axis_size(FRAME)
    flat = jnp.concatenate(biases + [condition.reshape(-1)])
    rows = line_gathered(flat)
    results, at = [], 0
    for bias in biases:
        results.append(rows[:, at : at + bias.shape[0]].reshape(-1))
        at += bias.shape[0]
    results.append(rows[:, at:].reshape(parts * condition.shape[0], condition.shape[1]))
    return results


def modulated(act_group, matrix, frames):
    parts = lax.axis_size(FRAME)
    rows, width = matrix.shape
    columns = lax.dynamic_slice_in_dim(act_group, lax.axis_index(FRAME) * rows, rows, axis=1)
    return mm(columns, matrix).reshape(parts, frames, width)


def passed_along(x, axis, by):
    peers = lax.axis_size(axis)
    pairs = [(i, i + by) for i in range(peers) if 0 <= i + by < peers]
    return lax.ppermute(x, axis, pairs)


def own_bit(bit):
    return (lax.axis_index(DP) >> bit) & 1


def swapped(x, bit):
    return lax.ppermute(x, DP, [(i, i ^ (1 << bit)) for i in range(lax.axis_size(DP))])


def paired(kept, sent):
    return kept.astype(F32) + swapped(sent, 0).astype(F32)


def summed(pieces):
    return jnp.sum(pieces.astype(F32), axis=0)


def core_order():
    groups = lax.axis_size(DP)
    return [(d & 1) * (groups // 2) + (d >> 1) for d in range(groups)]


def plane_summed(blocks):
    count = blocks.shape[0]
    own = lax.axis_index(DP) >> 1
    pick = lambda at: lax.dynamic_index_in_dim(blocks, at, keepdims=False)
    total = pick(own)
    for far in range(1, count):
        pairs = [(i, i ^ (2 * far)) for i in range(2 * count)]
        total = total + lax.ppermute(pick(own ^ far).astype(BF16), DP, pairs).astype(F32)
    return total


def dp_summed_start(blocks):
    return lax.all_to_all(blocks, DP, split_axis=0, concat_axis=0)


def line_summed(blocks, sent=BF16):
    parts = blocks.shape[0]
    place = lax.axis_index(FRAME)
    pick = lambda at: lax.dynamic_index_in_dim(blocks, (place + at) % parts, keepdims=False)
    total = pick(0)
    for far in range(1, parts):
        pairs = [(i, (i + far) % parts) for i in range(parts)]
        total = total + lax.ppermute(pick(far).astype(sent), FRAME, pairs).astype(F32)
    return total


def plane_gathered(piece):
    groups = lax.axis_size(DP)
    if groups > 8:
        copies = jnp.broadcast_to(piece[None], (groups,) + piece.shape)
        return lax.all_to_all(copies, DP, split_axis=0, concat_axis=0)
    pairs = lambda far: [(i, i ^ far) for i in range(groups)]
    return [piece] + [lax.ppermute(piece, DP, pairs(far)) for far in range(1, groups)]


def in_order(seen):
    if not isinstance(seen, list):
        return seen
    own = lax.axis_index(DP)
    seen = jnp.stack(seen)
    return jnp.stack(
        [lax.dynamic_index_in_dim(seen, own ^ d, keepdims=False) for d in range(len(seen))]
    )


def per_device(
    frames_in,
    condition,
    segments,
    spatial_in,
    spatial_in_bias,
    spatial_out,
    spatial_out_bias,
    temporal_in,
    temporal_in_bias,
    temporal_out,
    temporal_out_bias,
    expand_weight,
    expand_bias,
    shrink_weight,
    shrink_bias,
    modulate_weight,
    modulate_bias,
    cotangent,
):
    groups, parts = lax.axis_size(DP), lax.axis_size(FRAME)
    place = lax.axis_index(FRAME)
    frames, _, width = frames_in.shape
    space, time = [spatial_in], [temporal_in, temporal_out, spatial_out]
    dense = [expand_weight, shrink_weight]
    biases = [
        spatial_in_bias,
        spatial_out_bias,
        temporal_in_bias,
        temporal_out_bias,
        expand_bias,
        shrink_bias,
        modulate_bias,
    ]
    space_column = line_rotated(packed(space, width))
    time_piece, space_column = lax.optimization_barrier((packed(time, width), space_column))
    time_column = line_rotated(time_piece)
    *full_biases, cond_group = gathered_small(biases, condition)
    space_raw = plane_pieces(space_column, space)
    sinb, soutb, tinb, toutb, expb, shrb, modb = [b.astype(F32)[None, :] for b in full_biases]
    act_group = jax.nn.silu(cond_group.astype(F32)).astype(BF16)
    partial = modulated(act_group, modulate_weight, frames)
    partial = line_summed(partial, F32)
    mod = (partial + modb).reshape(frames, 9, width)
    time_raw = plane_pieces(time_column, time)
    dense_piece, time_column = lax.optimization_barrier((packed(dense, width), time_column))
    dense_column = line_rotated(dense_piece)
    dense_raw = plane_pieces(dense_column, dense)
    n1, qkv1, attn1 = spatial_forward(frames_in, mod, space_raw, sinb)
    branch1, after1, n2 = project_forward(frames_in, attn1, mod, time_raw, soutb)
    near_left = passed_along(n2[frames - WINDOW :], FRAME, 1)
    near_right = passed_along(n2[:WINDOW], FRAME, -1)
    qkv2 = temporal_qkv(n2, time_raw, tinb)
    seg_row = segments[0]
    seg_pad = jnp.pad(seg_row, (WINDOW, WINDOW), constant_values=-1)
    nearby = lax.dynamic_slice_in_dim(seg_pad, place * frames, frames + 2 * WINDOW)
    own_seg = nearby[WINDOW : WINDOW + frames]
    allowed = jnp.stack([nearby[o : o + frames] == own_seg for o in range(SPAN)]).astype(jnp.int32)
    probs, attn2, branch2, after2, left, right = temporal_forward(
        allowed, qkv2, near_left, near_right, after1, mod, time_raw, tinb, toutb
    )
    frames_out, g2, n3, act, dpre, db3, dmod3, sum_exp, sum_shr = feed_forward(
        after2, cotangent, mod, dense_raw, expb, shrb
    )
    plain = list(range(groups))
    hidden = dpre.shape[-1]
    high = 2 * (hidden // width) * modulate_weight.shape[0] // groups
    feed = outer_pieces(
        [[(n3, dpre, 0, hidden // width)]], width, groups, parts, plain, total_rows=high
    )
    feed = outer_pieces(
        [[(act, db3, 0, 1)]], width, groups, parts, plain, total_rows=high, into=feed
    )
    feed = lax.psum_scatter(feed.reshape(-1, width), DP, scatter_dimension=0, tiled=True)
    db2, dqkv2, dleft, dright, nleft, nright, dgate2, sum_tout, sum_tin = temporal_backward(
        g2, branch2, mod, time_raw, qkv2, left, right, probs
    )
    from_right = passed_along(nleft, FRAME, -1)
    from_left = passed_along(nright, FRAME, 1)
    order = core_order()
    halo = lambda t: [(near_left, dleft, t, 1), (near_right, dright, t, 1)]
    temporal = outer_pieces(
        [
            [(n2, dqkv2, 0, 1)],
            [(n2, dqkv2, 1, 1)] + halo(0),
            [(n2, dqkv2, 2, 1)] + halo(1),
            [(attn2, db2, 0, 1)],
        ],
        width, groups, parts, order, core=own_bit(0),
    )
    temporal = paired(*temporal)
    dqkv2, temporal = lax.optimization_barrier((dqkv2, temporal))
    temporal = plane_summed(temporal)
    g1, db1, da1, dmod1, sum_sout = project_backward(
        dqkv2, from_left, from_right, after1, g2, branch1, mod, time_raw
    )
    cond_float = condition.astype(F32)
    own_act = jax.nn.silu(cond_float).astype(BF16)
    early_mod = jnp.concatenate([dmod1, dgate2[:, None], dmod3], axis=1)
    early_mod = early_mod.reshape(frames, 7 * width).astype(BF16)
    early_sums = [s[0] for s in (sum_sout, sum_tin, sum_tout, sum_exp, sum_shr)]
    early_rows = jnp.concatenate(early_sums).astype(BF16).reshape(frames, -1)
    early = jnp.concatenate([own_act, early_mod, early_rows], axis=1)
    dheads, sum_first = heads_backward(qkv1, da1, 0)
    dheads, temporal, feed, early = lax.optimization_barrier((dheads, temporal, feed, early))
    early = line_rotated(early)
    feed = jnp.concatenate([feed.reshape(parts, high, width), temporal.astype(BF16)], axis=1)
    total_high = feed.shape[1]
    feed = lax.psum_scatter(
        feed.reshape(-1, width), FRAME, scatter_dimension=0, tiled=True
    )
    part = width // 2
    first = outer_pieces([[(n1, dheads, 0, 3)], [(attn1, db1, 0, 2)]], part, groups, parts, plain)
    dheads, first, early = lax.optimization_barrier((dheads, first, early))
    early_rows = jnp.sum(early[:, :, 8 * width :].astype(F32), axis=0).astype(BF16)
    early = early[:, :, : 8 * width].reshape(parts * frames, 8 * width)
    early_group = early[:, width:]
    early = jnp.concatenate([stacked(early, width), early_rows.reshape(-1, width)], axis=0)
    first = dp_summed_start(first)
    dtail, sum_last, grad_frames, dmod0 = heads_backward(
        qkv1, da1, 1, (dheads, g1, frames_in, mod, space_raw)
    )
    dtail, dmod0, sum_first, sum_last, feed, early = lax.optimization_barrier(
        (dtail, dmod0, sum_first, sum_last, feed, early)
    )
    whole_high = total_high + early.shape[0]
    feed = jnp.concatenate([feed, early], axis=0)
    feed = lax.all_gather(feed, DP, axis=0, tiled=True).reshape(groups, whole_high, width)
    sums = [s[0].reshape(3, part) for s in (sum_first, sum_last)]
    sum_sin = jnp.stack(sums, axis=1).reshape(1, 3 * width)
    late_mod = dmod0.reshape(frames, 2 * width).astype(BF16)
    late_rows = sum_sin.astype(BF16).reshape(frames, -1)
    late = line_rotated(jnp.concatenate([late_mod, late_rows], axis=1))
    last = outer_pieces([[(n1, dtail, 0, 3)]], part, groups, parts, order, core=own_bit(0))
    last = paired(*last)
    first = summed(first)
    last, first, late = lax.optimization_barrier((last, first, late))
    last = plane_summed(last)
    late_rows = jnp.sum(late[:, :, 2 * width :].astype(F32), axis=0).astype(BF16)
    late_group = late[:, :, : 2 * width].reshape(parts * frames, 2 * width)
    both = line_summed(jnp.concatenate([first, last], axis=1))
    late_held, both = lax.optimization_barrier((late_group, both))
    sizes = [first.shape[1], last.shape[1], 4 * parts * frames, 3 * width // part]
    sizes = [first.shape[1], last.shape[1], 4 * parts * frames, 3 * width // part]
    piece = [both.astype(BF16), stacked(late_group, part), late_rows.reshape(-1, part)]
    both = plane_gathered(jnp.concatenate(piece, axis=0))
    blocks = lambda whole, count: jnp.split(whole, count, axis=1)
    flat = lambda pieces: jnp.concatenate(
        [p.reshape(-1, p.shape[-1]) for p in pieces], axis=1
    ).astype(F32)
    tall = parts * frames
    share = modulate_weight.shape[0] // groups
    if share % 8 == 0:
        (
            grad_expand_sum,
            grad_shrink_sum,
            grad_temporal_in_sum,
            grad_temporal_out_sum,
            acts,
            early_mod,
            early_rows,
        ) = feed_outputs(feed, hidden, share, tall)
        early_rows = early_rows.reshape(-1)
    else:
        early = feed[:, total_high:]
        acts = early[:, :tall].reshape(-1, width)
        pick = lambda k: early[:, k * tall : (k + 1) * tall].reshape(-1, width)
        early_mod = jnp.concatenate([pick(k) for k in range(1, 8)], axis=1)
        early_rows = jnp.sum(early[:, 8 * tall :].astype(F32), axis=0).reshape(-1)
        feed, temporal = feed[:, :high], feed[:, high:total_high]
        *wide, narrow = blocks(temporal, 4)
        grad_temporal_in_sum, grad_temporal_out_sum = flat(wide), flat([narrow])
        wide = unstacked(feed[:, : high // 2], hidden // width)
        grad_expand_sum = wide.reshape(-1, hidden).astype(F32)
        grad_shrink_sum = feed[:, high // 2 :].reshape(-1, width).astype(F32)
    early_biases, at = [], 0
    for grad in early_sums:
        early_biases.append(own_part(early_rows[at : at + grad.shape[0]]))
        at += grad.shape[0]
    (
        both,
        acts,
        early_mod,
        early_biases,
        grad_temporal_in_sum,
        grad_temporal_out_sum,
        grad_expand_sum,
        grad_shrink_sum,
    ) = lax.optimization_barrier(
        (both, acts, early_mod, early_biases, grad_temporal_in_sum, grad_temporal_out_sum, grad_expand_sum, grad_shrink_sum)
    )
    rows = modulate_weight.shape[0]
    own_columns = lax.dynamic_slice_in_dim(acts, place * rows, rows, axis=1)
    if rows // groups % 8 == 0 and groups <= 8:
        outs = last_outputs(both, own_columns, early_mod, sizes, rows)
        grad_spatial_in_sum, grad_spatial_out_sum, grad_modulate_weight, mod_sum, sin_sum = outs
        mod_sum, sin_sum = mod_sum[0], sin_sum.reshape(-1)
    else:
        cuts = [sum(sizes[: at + 1]) for at in range(3)]
        first, last, late, late_rows = jnp.split(in_order(both), cuts, axis=1)
        starts, ends = blocks(first, 5), blocks(last, 3)
        grad_spatial_in_sum = flat([p for pair in zip(starts[:3], ends) for p in pair])
        grad_spatial_out_sum = flat(starts[3:])
        late_all = unstacked(late, 4).reshape(groups * parts * frames, 2 * width)
        dmod_all = jnp.concatenate([late_all, early_mod], axis=1)
        grad_modulate_weight = mm_tn(own_columns, dmod_all)
        mod_sum = jnp.sum(dmod_all.astype(F32), axis=0)
        sin_sum = jnp.sum(late_rows.astype(F32), axis=0).reshape(-1)
    grad_modulate_bias = own_part(mod_sum)
    dact_group = mm_nt(late_held, modulate_weight[:, : 2 * width])
    dact_group = dact_group + mm_nt(early_group, modulate_weight[:, 2 * width :])
    pieces_act = line_swapped(dact_group.reshape(parts, frames, rows))
    dcond_act = jnp.swapaxes(pieces_act, 0, 1).reshape(frames, parts * rows)
    grad_condition = jax.vjp(jax.nn.silu, cond_float)[1](dcond_act)[0]
    bias_sums = [own_part(sin_sum)] + early_biases
    return (
        frames_out,
        grad_frames,
        grad_condition,
        grad_spatial_in_sum,
        bias_sums[0],
        grad_spatial_out_sum,
        bias_sums[1],
        grad_temporal_in_sum,
        bias_sums[2],
        grad_temporal_out_sum,
        bias_sums[3],
        grad_expand_sum,
        bias_sums[4],
        grad_shrink_sum,
        bias_sums[5],
        grad_modulate_weight,
        grad_modulate_bias,
    )


def solution(mesh):
    in_specs = (
        P((DP, FRAME), None, None),
        P((DP, FRAME), None),
        P(DP, None),
        P(FRAME, None),
        P(FRAME),
        P(FRAME, None),
        P(FRAME),
        P(FRAME, None),
        P(FRAME),
        P(FRAME, None),
        P(FRAME),
        P(FRAME, None),
        P(FRAME),
        P(FRAME, None),
        P(FRAME),
        P(FRAME, None),
        P(FRAME),
        P((DP, FRAME), None, None),
    )
    out_specs = (
        P((DP, FRAME), None, None),
        P((DP, FRAME), None, None),
        P((DP, FRAME), None),
        P(FRAME, None),
        P(FRAME),
        P(FRAME, None),
        P(FRAME),
        P(FRAME, None),
        P(FRAME),
        P(FRAME, None),
        P(FRAME),
        P(FRAME, None),
        P(FRAME),
        P(FRAME, None),
        P(FRAME),
        P(FRAME, None),
        P(FRAME),
    )

    return jax.shard_map(
        per_device, mesh=mesh, in_specs=in_specs, out_specs=out_specs, check_vma=False
    )
```
